32 devices in a mesh: dp: 4 (over z), seq: 8 (over y, x, core).
Axes of the slice: x: 2, y: 2, z: 4, core: 2. Of those that a mesh axis runs over, the one named last changes fastest.
Arguments:
- inputs: bfloat16 [4, 2048, 768], P('dp', 'seq'), may hold values from -6 to 6
- cotangent: float32 [4, 2048, 768], P('dp', 'seq'), may hold values from -6 to 6
- doc_lengths: int32 [4, 8], P('dp'), may hold values from 1 to 1920, 2048 in all within a row
- doc_labels: int32 [4, 8], P('dp'), may hold values from 0 to 2
- query_weight: bfloat16 [768, 768], P('seq'), may hold values from -0.3125 to 0.3125
- query_bias: bfloat16 [768], P('seq'), may hold values from -4 to 4
- key_weight: bfloat16 [768, 768], P('seq'), may hold values from -0.3125 to 0.3125
- value_weight: bfloat16 [768, 768], P('seq'), may hold values from -0.21875 to 0.21875
- value_bias: bfloat16 [768], P('seq'), may hold values from -0.75 to 0.75
- proj_weight: bfloat16 [768, 768], P('seq'), may hold values from -0.625 to 0.625
- proj_bias: bfloat16 [768], P('seq'), may hold values from -4 to 4
- norm_gain: bfloat16 [768], P('seq'), may hold values from 0.099609375 to 1.8984375
- norm_shift: bfloat16 [768], P('seq'), may hold values from -4 to 4
- up_weight: bfloat16 [768, 3072], P('seq'), may hold values from -0.21875 to 0.21875
- up_bias: bfloat16 [3072], P('seq'), may hold values from -4 to 4
- down_weight: bfloat16 [3072, 768], P('seq'), may hold values from -0.109375 to 0.109375
- down_bias: bfloat16 [768], P('seq'), may hold values from -4 to 4
- final_gain: bfloat16 [768], P('seq'), may hold values from 0.099609375 to 1.8984375
- final_shift: bfloat16 [768], P('seq'), may hold values from -4 to 4
- pool_weight: bfloat16 [768, 768], P('seq'), may hold values from -0.21875 to 0.21875
- pool_bias: bfloat16 [768], P('seq'), may hold values from -4 to 4
- class_weight: bfloat16 [768, 3], P('seq'), may hold values from -0.4375 to 0.4375
- class_bias: bfloat16 [3], replicated, may hold values from -6 to 6
Outputs:
- output: bfloat16 [4, 2048, 768], P('dp', 'seq')
- logits: float32 [4, 8, 3], P('dp')
- input_grad: float32 [4, 2048, 768], P('dp', 'seq')
- query_wgrad: float32 [768, 768], P('seq')
- query_bgrad: float32 [768], P('seq')
- key_wgrad: float32 [768, 768], P('seq')
- value_wgrad: float32 [768, 768], P('seq')
- value_bgrad: float32 [768], P('seq')
- proj_wgrad: float32 [768, 768], P('seq')
- proj_bgrad: float32 [768], P('seq')
- norm_ggrad: float32 [768], P('seq')
- norm_sgrad: float32 [768], P('seq')
- up_wgrad: float32 [768, 3072], P('seq')
- up_bgrad: float32 [3072], P('seq')
- down_wgrad: float32 [3072, 768], P('seq')
- down_bgrad: float32 [768], P('seq')
- final_ggrad: float32 [768], P('seq')
- final_sgrad: float32 [768], P('seq')
- pool_wgrad: float32 [768, 768], P('seq')
- pool_bgrad: float32 [768], P('seq')
- class_wgrad: float32 [768, 3], P('seq')
- class_bgrad: float32 [3], replicated
The draws below stay inside these ranges and needn't reach their ends.
Inputs may be any that keep to these rules, and one draw needn't show every extreme that they name: `doc_lengths`: in each sequence the 8 lengths sum to 2048, and one document has exactly 1920 tokens.
All inputs are finite; a program needn't handle non-finite values.
Results may differ from the reference program's by a relative error of at most 0.025.
Values may be sent and summed in bfloat16 or wider, within the bound.
No kernel may reach another device: no remote copies, remote signals or barrier semaphores. Data moves between devices by JAX's collectives and lax.ppermute only.
A program may use at most 192 MiB of HBM per device.

```python
import math
import jax
import jax.numpy as jnp
import numpy as np
from jax import lax

D = 768
HEADS = 12
HEAD_DIM = 64
FF = 3072
CLASSES = 3
DOCS = 8
TOK_DEV = 256
LENGTH = 2048
SEQS = 4
N_SEQ = 8


def with_ends(entries, key, least, top_value):
    extent = entries.shape
    index_at = [jax.random.randint(jax.random.fold_in(key, axis), (), 0, extent[axis]) for axis in range(len(extent))]
    entries = entries.at[tuple(index_at)].set(least)
    longest = extent.index(max(extent))
    index_at[longest] = (index_at[longest] + 1) % extent[longest]
    return entries.at[tuple(index_at)].set(top_value)


def steps_of(stream_key, shape, pieces, least, top_value):
    level = 1.0
    for dim, shards_of in pieces:
        steps = jax.random.uniform(jax.random.fold_in(jax.random.fold_in(stream_key, 6), dim), (shards_of,), jnp.float32, least / len(pieces), top_value / len(pieces))
        level = level * jnp.repeat(jnp.exp(steps), shape[dim] // shards_of).reshape((-1,) + (1,) * (len(shape) - 1 - dim))
    return level


def profile(count, total, limit, lean):
    loads = [(1 << 20) // math.isqrt(grade ** lean) + 1 for grade in range(2, count + 1)]
    spare, holding = total - limit - (count - 1), [1] * (count - 1)
    while spare > 0:
        free = [i for i in range(count - 1) if holding[i] < limit]
        whole, budget = sum([loads[i] for i in free]), spare
        for i in free:
            addition = min(limit - holding[i], max(1, budget * loads[i] // whole), spare)
            holding[i] = holding[i] + addition
            spare = spare - addition
    return np.array([limit] + holding)


def uneven_parts(key, amount, total, limit, skew):
    if amount == 2:
        one = jax.random.randint(key, (), max(1, total - limit), min(limit, total - 1) + 1)
        return jnp.stack([one, total - one])
    tallies = jnp.asarray(profile(amount, total, limit, skew), jnp.int32)
    couples = (amount - 1) // 2
    donor, taker = tallies[1:1 + 2 * couples:2], tallies[2:2 + 2 * couples:2]
    margin = jnp.minimum(donor - 1, limit - taker)
    passed = jax.random.randint(jax.random.fold_in(key, 1), (couples,), 0, 1 << 20) % (margin + 1)
    tallies = tallies.at[1:1 + 2 * couples:2].set(donor - passed).at[2:2 + 2 * couples:2].set(taker + passed)
    return tallies[jax.random.permutation(jax.random.fold_in(key, 2), amount)]


def noise(stream_key, dims, scale, most, pieces=(), kind=jnp.bfloat16):
    entries = scale * jax.random.normal(stream_key, dims, jnp.float32)
    if pieces:
        entries = entries * steps_of(stream_key, dims, pieces, -0.22, 0.18)
    return jnp.clip(entries, -most, most).astype(kind)


def setup_inputs(seed: int = 0) -> dict:
    key_list = jax.random.split(jax.random.key(seed), 24)
    inputs = noise(key_list[0], (SEQS, LENGTH, D), 1.0, 6.0, ((0, 4), (1, 8)))
    cotangent = noise(key_list[1], (SEQS, LENGTH, D), 1.0, 6.0, ((0, 4), (1, 8)), jnp.float32)
    doc_lengths = jax.vmap(lambda own: uneven_parts(own, DOCS, LENGTH, LENGTH - TOK_DEV // 2, 2))(jax.random.split(key_list[2], SEQS)).reshape((SEQS, DOCS)).astype(jnp.int32)
    doc_labels = with_ends(jax.random.randint(key_list[3], (SEQS, DOCS), 0, CLASSES), jax.random.fold_in(key_list[3], 1), 0, CLASSES - 1).astype(jnp.int32)
    query_weight = noise(key_list[4], (D, D), (D // 2) ** -0.5, 0.3125, ((0, 8),))
    query_bias = noise(key_list[5], (D,), 0.3, 4.0, ((0, 8),))
    key_weight = noise(key_list[6], (D, D), (D // 2) ** -0.5, 0.3125, ((0, 8),))
    value_weight = noise(key_list[7], (D, D), D ** -0.5, 0.21875, ((0, 8),))
    value_bias = noise(key_list[8], (D,), 0.05, 0.75, ((0, 8),))
    proj_weight = noise(key_list[9], (D, D), (D // N_SEQ) ** -0.5, 0.625, ((0, 8),))
    proj_bias = noise(key_list[10], (D,), 0.3, 4.0, ((0, 8),))
    norm_gain = jnp.clip(1.0 + 0.18 * jax.random.normal(key_list[11], (D,), jnp.float32), 0.099609375, 1.8984375).astype(jnp.bfloat16)
    norm_shift = noise(key_list[12], (D,), 0.3, 4.0, ((0, 8),))
    up_weight = noise(key_list[13], (D, FF), D ** -0.5, 0.21875, ((0, 8),))
    up_bias = noise(key_list[14], (FF,), 0.3, 4.0, ((0, 8),))
    down_weight = noise(key_list[15], (FF, D), FF ** -0.5, 0.109375, ((0, 8),))
    down_bias = noise(key_list[16], (D,), 0.3, 4.0, ((0, 8),))
    final_gain = jnp.clip(1.0 + 0.18 * jax.random.normal(key_list[17], (D,), jnp.float32), 0.099609375, 1.8984375).astype(jnp.bfloat16)
    final_shift = noise(key_list[18], (D,), 0.3, 4.0, ((0, 8),))
    pool_weight = noise(key_list[19], (D, D), D ** -0.5, 0.21875, ((0, 8),))
    pool_bias = noise(key_list[20], (D,), 0.3, 4.0, ((0, 8),))
    class_weight = noise(key_list[21], (D, CLASSES), (D // 4) ** -0.5, 0.4375, ((0, 8),))
    class_bias = noise(key_list[22], (CLASSES,), 0.5, 6.0)
    return dict(inputs=inputs, cotangent=cotangent, doc_lengths=doc_lengths, doc_labels=doc_labels, query_weight=query_weight, query_bias=query_bias, key_weight=key_weight, value_weight=value_weight, value_bias=value_bias, proj_weight=proj_weight, proj_bias=proj_bias, norm_gain=norm_gain, norm_shift=norm_shift, up_weight=up_weight, up_bias=up_bias, down_weight=down_weight, down_bias=down_bias, final_gain=final_gain, final_shift=final_shift, pool_weight=pool_weight, pool_bias=pool_bias, class_weight=class_weight, class_bias=class_bias)


epsilon = 1e-06
masked_score = -1e+30

@jax.custom_vjp
def low(v):
    return lax.optimization_barrier(v.astype(jnp.bfloat16)).astype(jnp.float32)

@jax.custom_vjp
def low_back(v):
    return v

def low_keep(v):
    return (low(v), None)

def low_pass(kept, grad):
    return (grad,)

def back_keep(v):
    return (v, None)

def back_low(kept, grad):
    return (low(grad),)
low.defvjp(low_keep, low_pass)
low_back.defvjp(back_keep, back_low)

def product(left, right):
    return jnp.dot(left, right, precision=lax.Precision.HIGHEST)

def layer_norm(value, gain, shift):
    centre = lax.optimization_barrier(jnp.mean(value, axis=-1, keepdims=True))
    centred = value - centre
    spread = lax.optimization_barrier(jnp.mean(centred * centred, axis=-1, keepdims=True))
    return centred * lax.rsqrt(spread + epsilon) * gain + shift

def segment_of(positions, starts):
    return lax.optimization_barrier(jnp.sum((positions[:, None] >= starts[None, :]).astype(jnp.int32), axis=1)) - 1

def attention(queries, keys_full, values_full, segment):
    block_rows = 512 if LENGTH % 512 == 0 else LENGTH
    blocks = LENGTH // block_rows
    scaling = HEAD_DIM ** (-0.5)
    key_heads = keys_full.reshape(LENGTH, HEADS, HEAD_DIM)
    value_heads = values_full.reshape(LENGTH, HEADS, HEAD_DIM)

    def one_block(block_in):
        query_part, query_seg = block_in
        scores = jnp.einsum('thd,shd->hts', query_part, key_heads, precision=lax.Precision.HIGHEST) * scaling
        scores = low_back(scores)
        allowed = (query_seg[:, None] == segment[None, :])[None]
        scores = jnp.where(allowed, scores, masked_score)
        top_score = lax.optimization_barrier(jnp.max(scores, axis=-1, keepdims=True))
        weights = jnp.where(allowed, jnp.exp(scores - top_score), 0.0)
        soft_low = low(weights / lax.optimization_barrier(jnp.sum(weights, axis=-1, keepdims=True)))
        return jnp.einsum('hts,shd->thd', soft_low, value_heads, precision=lax.Precision.HIGHEST)
    parts = lax.map(jax.checkpoint(one_block), (queries.reshape(blocks, block_rows, HEADS, HEAD_DIM), segment.reshape(blocks, block_rows)))
    return parts.reshape(LENGTH, D)

def forward(tokens, weights, lengths, labels, grad_seq):
    query_weight, query_bias, key_weight, value_weight, value_bias, proj_weight, proj_bias, norm_gain, norm_shift, up_weight, up_bias, down_weight, down_bias, final_gain, final_shift, pool_weight, pool_bias, class_weight, class_bias = weights
    starts = (jnp.cumsum(lengths) - lengths).astype(jnp.int32)
    segment = segment_of(jnp.arange(LENGTH, dtype=jnp.int32), starts)
    queries = low(low_back(product(tokens, query_weight) + query_bias))
    keys_full = low(low_back(product(tokens, key_weight)))
    values_full = low(low_back(product(tokens, value_weight) + value_bias))
    attended = low(low_back(attention(queries, keys_full, values_full, segment)))
    first_residual = tokens + low_back(product(attended, proj_weight)) + proj_bias
    normed = layer_norm(first_residual, norm_gain, norm_shift)
    normed_low = low(low_back(normed))
    upward = low_back(product(normed_low, up_weight)) + up_bias
    activation = low(low_back(jax.nn.gelu(upward, approximate=False)))
    second_residual = normed + low_back(product(activation, down_weight)) + down_bias
    outcome = layer_norm(second_residual, final_gain, final_shift)
    first_low = low(outcome[starts])
    pooled = jnp.tanh(product(first_low, pool_weight) + pool_bias)
    pooled_low = low(pooled)
    logits = product(pooled_low, class_weight) + class_bias
    onehot = (labels[:, None] == jnp.arange(CLASSES, dtype=jnp.int32)[None, :]).astype(logits.dtype)
    entropy = jax.nn.logsumexp(logits, axis=1) - lax.optimization_barrier(jnp.sum(logits * onehot, axis=1))
    loss = jnp.sum(outcome * grad_seq) + jnp.sum(entropy)
    return (loss, (outcome, logits))

def reference(inputs, cotangent, doc_lengths, doc_labels, query_weight, query_bias, key_weight, value_weight, value_bias, proj_weight, proj_bias, norm_gain, norm_shift, up_weight, up_bias, down_weight, down_bias, final_gain, final_shift, pool_weight, pool_bias, class_weight, class_bias):
    params = tuple((item.astype(jnp.float32) for item in (query_weight, query_bias, key_weight, value_weight, value_bias, proj_weight, proj_bias, norm_gain, norm_shift, up_weight, up_bias, down_weight, down_bias, final_gain, final_shift, pool_weight, pool_bias, class_weight, class_bias)))
    start_totals = tuple((jnp.zeros_like(item) for item in params))

    def one_sequence(totals, seq_inputs):
        tokens, grad_seq, lengths, labels = seq_inputs

        def objective(tokens32, *weights):
            return forward(tokens32, weights, lengths, labels, grad_seq.astype(jnp.float32))
        loss, pullback, extras = jax.vjp(objective, tokens.astype(jnp.float32), *params, has_aux=True)
        grads = pullback(jnp.ones_like(loss))
        totals = tuple((total + grad for total, grad in zip(totals, grads[1:])))
        return (totals, (extras[0].astype(jnp.bfloat16), extras[1], grads[0]))
    totals, stacked = lax.scan(one_sequence, start_totals, (inputs, cotangent, doc_lengths, doc_labels))
    return (stacked[0], stacked[1], stacked[2], totals[0], totals[1], totals[2], totals[3], totals[4], totals[5], totals[6], totals[7], totals[8], totals[9], totals[10], totals[11], totals[12], totals[13], totals[14], totals[15], totals[16], totals[17], totals[18])
```

```python
import functools

import jax
import jax.numpy as jnp
from jax import lax
from jax.experimental import pallas as pl
from jax.experimental.pallas import tpu as pltpu
from jax.sharding import PartitionSpec as P

D = 768
HEADS = 12
HEAD_DIM = 64
FF = 3072
CLASSES = 3
PAIR = 2 * HEAD_DIM
ROWS = 256
EPSILON = 1e-06
FAR = -1e30
LIMIT = 56 * 1024 * 1024
F32, BF16 = jnp.float32, jnp.bfloat16

QUERY_B, VALUE_B, PROJ_B, NORM_G, NORM_S, DOWN_B, FINAL_G, FINAL_S, POOL_B, CLASS_W, UP_B = (
    0, 1, 2, 3, 4, 5, 6, 7, 8, 9, 12,
)
TABLE = 16


def swap(value, partner):
    dp, seq = lax.axis_size("dp"), lax.axis_size("seq")
    pairs = []
    for z in range(dp):
        for i in range(seq):
            to_z, to_i = partner(z, i)
            pairs.append((z * seq + i, to_z * seq + to_i))
    return lax.ppermute(value, ("dp", "seq"), pairs)


def along(bit):
    return lambda z, i: (z, i ^ bit)


def is_small():
    return lax.axis_size("seq") == 8 and lax.axis_size("dp") == 4


def gather_shared(shard, role):
    me, z = lax.axis_index("seq"), lax.axis_index("dp")
    if not is_small():
        whole = lax.all_gather(shard, "seq", axis=shard.ndim - 2, tiled=True)
        return [whole], [jnp.int32(0)]
    one = swap(shard, lambda z, i: (z, i ^ (2 if (z + role) % 2 == 0 else 4)))
    both = swap(one, lambda z, i: (z, i ^ (4 if (z + role) % 2 == 0 else 2)))
    other = swap(one, lambda z, i: (z ^ 1, i))
    near = jnp.where((z + role) % 2 == 0, 2, 4)
    blocks = [shard, one, both, other]
    owners = [me, me ^ near, me ^ 6, me ^ (6 - near)]
    blocks += [swap(block, along(1)) for block in blocks]
    owners += [owner ^ 1 for owner in owners]
    return blocks, owners


def gather_own(shard, order):
    if not is_small():
        return [lax.all_gather(shard, "seq", axis=0)]
    near = {2: swap(shard, along(order[0]))}
    near = {order[0]: near[2], order[1]: swap(shard, along(order[1]))}
    both = swap(near[order[0]], along(order[1]))
    blocks = [shard, near[4], near[2], both]
    return blocks + [swap(block, along(1)) for block in blocks]


def slot_owners():
    if not is_small():
        return jnp.arange(lax.axis_size("seq"), dtype=jnp.int32)
    return lax.axis_index("seq") ^ jnp.array([0, 4, 2, 6, 1, 5, 3, 7], jnp.int32)


def scatter_sum(parts, order):
    if not is_small():
        (part,) = parts
        return lax.psum_scatter(part, "seq", scatter_dimension=0, tiled=True)[0].astype(F32)
    keep, away = parts
    come = swap(away, along(1))
    if order == (2, 4):
        last, far = 1, slice(2, 4)
    else:
        last, far = 2, slice(1, 4, 2)
    send = (keep[far].astype(F32) + come[far].astype(F32)).astype(BF16)
    second = swap(send, along(order[0]))
    send = (
        keep[last].astype(F32) + come[last].astype(F32) + second[1].astype(F32)
    ).astype(BF16)
    third = swap(send, along(order[1]))
    return (
        keep[0].astype(F32) + come[0].astype(F32) + second[0].astype(F32) + third.astype(F32)
    )


def sum_dp(shard):
    if not is_small():
        return lax.psum(shard.astype(BF16), "dp").astype(F32)
    z = lax.axis_index("dp")
    half = shard.shape[0] // 2
    low = jnp.logical_or(z == 0, z == 3)
    first, second = shard[:half], shard[half:]
    keep, away = jnp.where(low, first, second), jnp.where(low, second, first)
    come = swap(away.astype(BF16), lambda z, i: (z ^ 1, i))
    pair = (keep + come.astype(F32)).astype(BF16)
    cross = swap(pair, lambda z, i: (z ^ 3, i))
    total = (pair.astype(F32) + cross.astype(F32)).astype(BF16)
    back = swap(total, lambda z, i: (z ^ 1, i))
    return jnp.concatenate(
        [jnp.where(low, total, back), jnp.where(low, back, total)], axis=0
    ).astype(F32)


def sum_seq(value):
    if not is_small():
        return lax.psum(value, "seq")
    for bit in (1, 2, 4):
        value = value + swap(value, along(bit))
    return value


def sum_all(value):
    value = sum_seq(value)
    if not is_small():
        return lax.psum(value, "dp")
    for bit in (1, 2):
        value = value + swap(value, lambda z, i: (z ^ bit, i))
    return value


def stack_dp(value):
    if not is_small():
        return lax.all_gather(value, "dp", axis=0, tiled=True)
    for bit in (1, 2):
        value = jnp.concatenate([value, swap(value, lambda z, i: (z ^ bit, i))], axis=0)
    return value


def dot(left, right, contract=((1,), (0,))):
    return lax.dot_general(left, right, (contract, ((), ())), preferred_element_type=F32)


def call(body, name, **kwargs):
    return pl.pallas_call(
        body,
        name=name,
        compiler_params=pltpu.CompilerParams(vmem_limit_bytes=LIMIT),
        **kwargs,
    )


VMEM = pl.BlockSpec(memory_space=pltpu.VMEM)
ANY = pl.BlockSpec(memory_space=pl.ANY)
SMEM = pl.BlockSpec(memory_space=pltpu.SMEM)


def block_copies(owners, refs, target, sems, part=None):
    copies = []
    for slot, ref in enumerate(refs):
        source = ref if part is None else ref.at[part]
        rows = source.shape[-2]
        start = pl.multiple_of(owners[0, slot] * rows, rows)
        if source.ndim == 3:
            place = target.at[:, pl.ds(start, rows), :]
        else:
            place = target.at[pl.ds(start, rows), :]
        copies.append(pltpu.make_async_copy(source, place, sems.at[slot]))
    for copy in copies:
        copy.start()
    return copies


def wait(copies):
    for copy in copies:
        copy.wait()


def qkv_kernel(count, owners, *refs):
    blocks, (tokens, table, query, key, value, weights, sems) = refs[:count], refs[count:]
    wait(block_copies(owners, blocks, weights, sems))
    rows = tokens[...]
    key[...] = dot(rows, weights[1]).astype(BF16)
    value[...] = (dot(rows, weights[2]) + table[VALUE_B : VALUE_B + 1]).astype(BF16)
    query[...] = (dot(rows, weights[0]) + table[QUERY_B : QUERY_B + 1]).astype(BF16)


def qkv_project(owners, blocks, tokens, table):
    out = jax.ShapeDtypeStruct(tokens.shape, BF16)
    count = len(blocks)
    return call(
        functools.partial(qkv_kernel, count),
        "qkv",
        out_shape=(out,) * 3,
        in_specs=[SMEM] + [ANY] * count + [VMEM] * 2,
        out_specs=(VMEM,) * 3,
        scratch_shapes=[pltpu.VMEM((3, D, D), BF16), pltpu.SemaphoreType.DMA((count,))],
    )(owners, *blocks, tokens, table)


def left_half(shape):
    return lax.broadcasted_iota(jnp.int32, shape, len(shape) - 1) < HEAD_DIM


def split3(value):
    high = value.astype(BF16).astype(F32)
    middle = (value - high).astype(BF16).astype(F32)
    low = (value - high - middle).astype(BF16).astype(F32)
    return high, middle, low


def spread3(value, docs, shape):
    lane = lax.broadcasted_iota(jnp.int32, shape, 1) % HEAD_DIM
    high, middle, low = split3(value)
    return jnp.where(
        lane == docs, high, jnp.where(lane == docs + 1, middle, jnp.where(lane == docs + 2, low, 0.0))
    )


def attend_kernel(count, docs, *refs):
    query, feature_q, feature_k = refs[:3]
    keys, values = refs[3 : 3 + count], refs[3 + count : 3 + 2 * count]
    out, total, scores = refs[3 + 2 * count :]
    chunks = feature_k.shape[0]
    left = left_half((ROWS, PAIR))
    rows = query[...] * 0.125
    spare = feature_q[...]
    results, totals = [], []
    for head in range(2):
        mine = left if head == 0 else jnp.logical_not(left)
        aug = jnp.where(mine, rows, spare)

        def score_step(chunk, key):
            full = jnp.where(mine, key, feature_k[chunk])
            scores[chunk] = dot(aug, full, ((1,), (1,)))

        def value_step(chunk, value, top):
            full = jnp.where(mine, value, feature_k[chunk])
            return dot(jnp.exp(scores[chunk] - top).astype(BF16), full)

        if count > 1:
            for chunk in range(count):
                score_step(chunk, keys[chunk][...])
            most = scores[0]
            for chunk in range(1, count):
                most = jnp.maximum(most, scores[chunk])
            top = jnp.max(most, axis=1, keepdims=True)
            acc = value_step(0, values[0][...], top)
            for chunk in range(1, count):
                acc = acc + value_step(chunk, values[chunk][...], top)
        else:

            @pl.loop(0, chunks)
            def _(chunk):
                score_step(chunk, keys[0][chunk])

            most = lax.fori_loop(
                1, chunks, lambda chunk, had: jnp.maximum(had, scores[chunk]), scores[0]
            )
            top = jnp.max(most, axis=1, keepdims=True)
            acc = lax.fori_loop(
                0,
                chunks,
                lambda chunk, had: had + value_step(chunk, values[0][chunk], top),
                jnp.zeros((ROWS, PAIR), F32),
            )
        lane = docs + (HEAD_DIM if head == 0 else 0)
        weight = acc[:, lane : lane + 1]
        results.append(acc / weight)
        totals.append(top + jnp.log(weight))
    out[...] = jnp.where(left, results[0], results[1])
    total[...] = jnp.where(left, totals[0], totals[1])


def pair_spec(array):
    lead = array.shape[:-1]
    return pl.BlockSpec(lead + (PAIR,), lambda pair: (0,) * len(lead) + (pair,))


def fixed_spec(array):
    return pl.BlockSpec(array.shape, lambda pair: (0,) * array.ndim)


def attend(query, keys, values, feature_q, feature_k, docs):
    count = len(keys)
    out = jax.ShapeDtypeStruct((ROWS, D), F32)
    return call(
        functools.partial(attend_kernel, count, docs),
        "attend",
        grid=(HEADS // 2,),
        out_shape=(out, out),
        in_specs=[pair_spec(query), fixed_spec(feature_q), fixed_spec(feature_k)]
        + [pair_spec(block) for block in (*keys, *values)],
        out_specs=(pair_spec(out), pair_spec(out)),
        scratch_shapes=[pltpu.VMEM((feature_k.shape[0], ROWS, ROWS), F32)],
    )(query, feature_q, feature_k, *keys, *values)


def attend_back_kernel(count, docs, groups, *refs):
    query, grad, attended, total, feature_q, feature_k = refs[:6]
    keys, values = refs[6 : 6 + count], refs[6 + count : 6 + 2 * count]
    rest = refs[6 + 2 * count :]
    grad_q, grad_k, grad_v = rest[0], rest[1 : 1 + groups], rest[1 + groups : 1 + 2 * groups]
    acc = rest[-1]
    chunks = feature_k.shape[0]
    left = left_half((ROWS, PAIR))
    rows = query[...] * 0.125
    grads = grad[...]
    product = grads.astype(F32) * attended[...]
    spare = feature_q[...]
    zero = jnp.zeros_like(rows)
    sides = []
    for head in range(2):
        mine = left if head == 0 else jnp.logical_not(left)
        at = head * HEAD_DIM
        delta = jnp.sum(jnp.where(mine, product, 0.0), axis=1, keepdims=True)
        sums = total[:, at : at + 1]
        query_aug = jnp.where(
            mine, rows.astype(F32), spare.astype(F32) + spread3(-sums, docs, (ROWS, PAIR))
        )
        grad_aug = jnp.where(mine, grads.astype(F32), spread3(-delta, docs, (ROWS, PAIR)))
        sides.append(
            (
                mine,
                query_aug.T.astype(BF16),
                grad_aug.T.astype(BF16),
                jnp.where(mine, rows, zero),
                jnp.where(mine, grads, zero),
            )
        )
    acc[...] = jnp.zeros_like(acc)

    def step(chunk, key, value):
        feature = feature_k[chunk]
        key_t = key.astype(F32).T.astype(BF16)
        out_k, out_v = 0.0, 0.0
        for head in range(2):
            mine, query_t, grad_t, query_own, grad_own = sides[head]
            soft = jnp.exp(dot(jnp.where(mine, key, feature), query_t))
            change = dot(jnp.where(mine, value, feature), grad_t)
            slope = (soft * change).astype(BF16)
            out_v = out_v + dot(soft.astype(BF16), grad_own)
            out_k = out_k + dot(slope, query_own)
            at = head * HEAD_DIM
            acc[at : at + HEAD_DIM] += dot(key_t[at : at + HEAD_DIM], slope)
        return out_k.astype(BF16), out_v.astype(BF16)

    if count > 1:
        per = count // groups
        for chunk in range(count):
            out_k, out_v = step(chunk, keys[chunk][...], values[chunk][...])
            grad_k[chunk // per][chunk % per] = out_k
            grad_v[chunk // per][chunk % per] = out_v
    else:

        @pl.loop(0, chunks)
        def _(chunk):
            out_k, out_v = step(chunk, keys[0][chunk], values[0][chunk])
            grad_k[0][chunk] = out_k
            grad_v[0][chunk] = out_v

    grad_q[...] = (acc[...].T * 0.125).astype(BF16)


def attend_back(query, keys, values, grad, attended, total, feature_q, feature_k, docs):
    count = len(keys)
    groups = 2 if count > 1 else 1
    chunks = feature_k.shape[0]
    grad_q = jax.ShapeDtypeStruct((ROWS, D), BF16)
    grad_kv = jax.ShapeDtypeStruct((chunks // groups, ROWS, D), BF16)
    outs = (grad_q,) + (grad_kv,) * (2 * groups)
    made = call(
        functools.partial(attend_back_kernel, count, docs, groups),
        "attend_back",
        grid=(HEADS // 2,),
        out_shape=outs,
        in_specs=[pair_spec(a) for a in (query, grad, attended, total)]
        + [fixed_spec(feature_q), fixed_spec(feature_k)]
        + [pair_spec(block) for block in (*keys, *values)],
        out_specs=tuple(pair_spec(a) for a in outs),
        scratch_shapes=[pltpu.VMEM((PAIR, ROWS), F32)],
    )(query, grad, attended, total, feature_q, feature_k, *keys, *values)
    return made[0], made[1 : 1 + groups], made[1 + groups :]


def normalise(value):
    centred = value - jnp.mean(value, axis=-1, keepdims=True)
    inverse = lax.rsqrt(jnp.mean(centred * centred, axis=-1, keepdims=True) + EPSILON)
    return centred * inverse, inverse


def norm_back(grad, gain, unit, inverse):
    scaled = grad * gain
    return inverse * (
        scaled
        - jnp.mean(scaled, axis=-1, keepdims=True)
        - unit * jnp.mean(scaled * unit, axis=-1, keepdims=True)
    )


def erf(value):
    value = jnp.clip(value, -3.7439211627767994, 3.7439211627767994)
    square = value * value
    top = 0.00022905065861350646
    for factor in (0.0034082910107109506, 0.050955695062380861, 0.18520832239976145, 1.128379143519084):
        top = top * square + factor
    bottom = -1.1791602954361697e-7
    for factor in (
        0.000023547966471313185, 0.0010179625278914885, 0.014070470171167667,
        0.11098505178285362, 0.49746925110067538, 1.0,
    ):
        bottom = bottom * square + factor
    return value * top / bottom


def column_sum(value):
    return jnp.sum(value, axis=0, keepdims=True)


def first_kernel(count, docs, owners, *refs):
    groups = 2 if count > 1 else 1
    proj_blocks, up_blocks, down_blocks = (refs[k * count : (k + 1) * count] for k in range(3))
    refs = refs[3 * count :]
    attended, tokens, cotangent, table, place, labels, class_b = refs[:7]
    output, lines, docs_out, grad_second, unit, inverse, slope = refs[7:14]
    down_g = refs[14 : 14 + groups]
    both, up, down, active, wgrad, sems, out_sems = refs[14 + groups :]
    proj_copies = block_copies(owners, proj_blocks, both, sems.at[0])
    up_copies = block_copies(owners, up_blocks, up, sems.at[1])
    down_copies = block_copies(owners, down_blocks, down, sems.at[2])

    def row(at):
        return table[at : at + 1]

    wait(proj_copies)
    residual = tokens[...].astype(F32) + dot(attended[...].astype(BF16), both[0]) + row(PROJ_B)
    first_unit, first_inverse = normalise(residual)
    unit[...] = first_unit
    inverse[...] = first_inverse
    normed = first_unit * row(NORM_G) + row(NORM_S)
    normed_low = normed.astype(BF16)
    wait(up_copies)
    step = 384
    for at in range(0, FF, step):
        line, col = UP_B + at // D, at % D
        upward = dot(normed_low, up[:, at : at + step]) + table[line : line + 1, col : col + step]
        share = 0.5 + 0.5 * erf(upward * 0.7071067811865476)
        bell = jnp.exp(upward * upward * -0.5) * 0.3989422804014327
        active[:, at : at + step] = (upward * share).astype(BF16)
        slope[:, at : at + step] = share + upward * bell
    wait(down_copies)
    residual = normed + dot(active[...], down[...]) + row(DOWN_B)
    last_unit, last_inverse = normalise(residual)
    outcome = last_unit * row(FINAL_G) + row(FINAL_S)
    out_low = outcome.astype(BF16)
    output[...] = out_low

    at_row = place[...]
    here = jnp.logical_and(at_row >= 0, at_row < ROWS)
    pick = jnp.where(lax.broadcasted_iota(jnp.int32, (docs, ROWS), 1) == at_row, 1.0, 0.0)
    first_low = dot(pick.astype(BF16), out_low).astype(BF16)
    pooled = jnp.tanh(dot(first_low, both[1]) + row(POOL_B))
    pooled_low = pooled.astype(BF16).astype(F32)
    logits = [
        jnp.sum(pooled_low * row(CLASS_W + c), axis=1, keepdims=True) + class_b[0, c]
        for c in range(CLASSES)
    ]
    top = functools.reduce(jnp.maximum, logits)
    powers = [jnp.exp(logit - top) for logit in logits]
    whole = functools.reduce(jnp.add, powers)
    label = labels[...]
    grads = [powers[c] / whole - jnp.where(label == c, 1.0, 0.0) for c in range(CLASSES)]
    grad_pre = functools.reduce(jnp.add, [grads[c] * row(CLASS_W + c) for c in range(CLASSES)])
    grad_pre = grad_pre * (1.0 - pooled * pooled)
    parts = jnp.concatenate(split3(grad_pre), axis=0).astype(BF16)
    made = dot(parts, both[1], ((1,), (1,)))
    grad_first = made[:docs] + made[docs : 2 * docs] + made[2 * docs :]
    parts = jnp.concatenate(split3(grad_first), axis=0).astype(BF16)
    picks = jnp.concatenate([pick] * 3, axis=0).astype(BF16)
    grad_outcome = cotangent[...] + dot(picks, parts, ((0,), (0,)))
    lane = lax.broadcasted_iota(jnp.int32, (docs, 128), 1)
    small = jnp.zeros((docs, 128), F32)
    for c in range(CLASSES):
        small = jnp.where(lane == c, grads[c], jnp.where(lane == CLASSES + c, logits[c], small))
    docs_out[...] = jnp.where(
        here,
        jnp.concatenate([first_low.astype(F32), pooled_low, grad_pre, small], axis=1),
        0.0,
    )

    grad = norm_back(grad_outcome, row(FINAL_G), last_unit, last_inverse)
    grad_second[...] = grad
    lines[0:1] = column_sum(grad)
    lines[1:2] = column_sum(grad_outcome * last_unit)
    lines[2:3] = column_sum(grad_outcome)
    lines[3:8] = jnp.zeros((5, D), F32)
    grad_low = grad.astype(BF16)
    step = 512
    for at in range(0, FF, step):
        wgrad[at : at + step] = dot(active[:, at : at + step], grad_low, ((0,), (0,))).astype(BF16)
    slot_copies(owners, wgrad, [g.at[j] for g in down_g for j in range(g.shape[0])], out_sems)


def slot_copies(owners, source, targets, sems):
    copies = []
    for slot, target in enumerate(targets):
        rows = target.shape[0]
        start = pl.multiple_of(owners[1, slot] * rows, rows)
        copies.append(pltpu.make_async_copy(source.at[pl.ds(start, rows), :], target, sems.at[slot]))
    for copy in copies:
        copy.start()
    wait(copies)


def slot_shapes(count, rows):
    if count == 1:
        return (jax.ShapeDtypeStruct((1, rows, D), BF16),)
    return (jax.ShapeDtypeStruct((count // 2, rows // count, D), BF16),) * 2


def first_part(
    owners, proj_blocks, up_blocks, down_blocks, attended, tokens, cotangent, table, place, labels, class_b
):
    count, docs = len(proj_blocks), place.shape[0]
    down_shapes = slot_shapes(count, FF)
    shape = jax.ShapeDtypeStruct
    outs = (
        shape((ROWS, D), BF16),
        shape((8, D), F32),
        shape((docs, 3 * D + 128), F32),
        shape((ROWS, D), F32),
        shape((ROWS, D), F32),
        shape((ROWS, 1), F32),
        shape((ROWS, FF), F32),
    ) + down_shapes
    made = call(
        functools.partial(first_kernel, count, docs),
        "forward_and_head",
        out_shape=outs,
        in_specs=[SMEM] + [ANY] * (3 * count) + [VMEM] * 6 + [SMEM],
        out_specs=(VMEM,) * 7 + (ANY,) * len(down_shapes),
        scratch_shapes=[
            pltpu.VMEM((2, D, D), BF16),
            pltpu.VMEM((D, FF), BF16),
            pltpu.VMEM((FF, D), BF16),
            pltpu.VMEM((ROWS, FF), BF16),
            pltpu.VMEM((FF, D), BF16),
            pltpu.SemaphoreType.DMA((3, count)),
            pltpu.SemaphoreType.DMA((count,)),
        ],
    )(
        owners, *proj_blocks, *up_blocks, *down_blocks,
        attended, tokens, cotangent, table, place, labels, class_b,
    )
    return made[:7], made[7:]


def second_kernel(count, owners, *refs):
    groups = 2 if count > 1 else 1
    proj_blocks, up_blocks, down_blocks = (refs[k * count : (k + 1) * count] for k in range(3))
    refs = refs[3 * count :]
    attended, table, grad_second, unit, inverse, slope = refs[:6]
    lines, grad_first, grad_attended = refs[6:9]
    up_g = refs[9 : 9 + groups]
    both, up, down, grad_up, wgrad, pgrad, sems, out_sems = refs[9 + groups :]
    down_copies = block_copies(owners, down_blocks, down, sems.at[2])
    up_copies = block_copies(owners, up_blocks, up, sems.at[1])
    proj_copies = block_copies(owners, proj_blocks, both, sems.at[0], 0)

    def row(at):
        return table[at : at + 1]

    grad_low = grad_second[...].astype(BF16)
    normed_t = (unit[...] * row(NORM_G) + row(NORM_S)).T.astype(BF16)
    attended_t = attended[...].T.astype(BF16)
    wait(down_copies)
    step = 384
    for at in range(0, FF, step):
        grad = dot(grad_low, down[at : at + step], ((1,), (1,))).astype(BF16).astype(F32)
        grad = grad * slope[:, at : at + step]
        line, col = at // D, at % D
        lines[line : line + 1, col : col + step] = column_sum(grad)
        grad_up[:, at : at + step] = grad.astype(BF16)
    wait(up_copies)
    grad_normed = grad_second[...] + dot(grad_up[...], up[...], ((1,), (1,))).astype(BF16).astype(F32)
    lines[4:5] = column_sum(grad_normed * unit[...])
    lines[5:6] = column_sum(grad_normed)
    grad = norm_back(grad_normed, row(NORM_G), unit[...], inverse[...])
    grad_first[...] = grad
    lines[6:7] = column_sum(grad)
    lines[7:8] = jnp.zeros((1, D), F32)
    grad_low = grad.astype(BF16)
    wait(proj_copies)
    grad_attended[...] = dot(grad_low, both[...], ((1,), (1,))).astype(BF16)
    pgrad[...] = dot(attended_t, grad_low).astype(BF16)
    for at in range(0, FF, D):
        wgrad[at // D] = dot(normed_t, grad_up[:, at : at + D]).astype(BF16)
    copies = []
    slots = [g.at[j] for g in up_g for j in range(g.shape[0])]
    for slot, target in enumerate(slots):
        rows = target.shape[0] // 5
        start = pl.multiple_of(owners[1, slot] * rows, rows)
        for piece in range(4):
            copies.append((wgrad.at[piece, pl.ds(start, rows), :], target.at[piece * rows : (piece + 1) * rows]))
        copies.append((pgrad.at[pl.ds(start, rows), :], target.at[4 * rows :]))
    copies = [
        pltpu.make_async_copy(source, target, out_sems.at[k])
        for k, (source, target) in enumerate(copies)
    ]
    for copy in copies:
        copy.start()
    wait(copies)


def second_part(owners, proj_blocks, up_blocks, down_blocks, attended, table, grad_second, unit, inverse, slope):
    count = len(proj_blocks)
    up_shapes = slot_shapes(count, 5 * D)
    shape = jax.ShapeDtypeStruct
    outs = (shape((8, D), F32), shape((ROWS, D), F32), shape((ROWS, D), BF16)) + up_shapes
    made = call(
        functools.partial(second_kernel, count),
        "backward_to_attention",
        out_shape=outs,
        in_specs=[SMEM] + [ANY] * (3 * count) + [VMEM] * 6,
        out_specs=(VMEM,) * 3 + (ANY,) * len(up_shapes),
        scratch_shapes=[
            pltpu.VMEM((D, D), BF16),
            pltpu.VMEM((D, FF), BF16),
            pltpu.VMEM((FF, D), BF16),
            pltpu.VMEM((ROWS, FF), BF16),
            pltpu.VMEM((4, D, D), BF16),
            pltpu.VMEM((D, D), BF16),
            pltpu.SemaphoreType.DMA((3, count)),
            pltpu.SemaphoreType.DMA((5 * count,)),
        ],
    )(
        owners, *proj_blocks, *up_blocks, *down_blocks,
        attended, table, grad_second, unit, inverse, slope,
    )
    return made[:3], made[3:]


def last_kernel(count, owners, *refs):
    groups = 2 if count > 1 else 1
    blocks, refs = refs[:count], refs[count:]
    tokens, grad_q, grad_k, grad_v, grad_first = refs[:5]
    lines, input_grad = refs[5:7]
    outs = refs[7 : 7 + groups]
    weights, wgrad, sems, out_sems = refs[7 + groups :]
    copies = block_copies(owners, blocks, weights, sems)
    tokens_t = tokens[...].astype(F32).T.astype(BF16)
    grads = [grad_q[...], grad_k[...].astype(BF16), grad_v[...].astype(BF16)]
    for k in range(3):
        wgrad[k] = dot(tokens_t, grads[k]).astype(BF16)
    sends = []
    slots = [g.at[j] for g in outs for j in range(g.shape[0])]
    for slot, target in enumerate(slots):
        rows = target.shape[0] // 3
        start = pl.multiple_of(owners[1, slot] * rows, rows)
        for k in range(3):
            sends.append((wgrad.at[k, pl.ds(start, rows), :], target.at[k * rows : (k + 1) * rows]))
    sends = [
        pltpu.make_async_copy(source, target, out_sems.at[k])
        for k, (source, target) in enumerate(sends)
    ]
    for copy in sends:
        copy.start()
    lines[0:1] = column_sum(grads[0].astype(F32))
    lines[1:2] = column_sum(grads[2].astype(F32))
    lines[2:8] = jnp.zeros((6, D), F32)
    wait(copies)
    total = grad_first[...]
    for k in range(3):
        total = total + dot(grads[k], weights[k], ((1,), (1,)))
    input_grad[...] = total
    wait(sends)


def last_part(owners, blocks, tokens, grad_q, grad_k, grad_v, grad_first):
    count = len(blocks)
    shapes = slot_shapes(count, 3 * D)
    shape = jax.ShapeDtypeStruct
    outs = (shape((8, D), F32), shape((ROWS, D), F32)) + shapes
    made = call(
        functools.partial(last_kernel, count),
        "input_gradients",
        out_shape=outs,
        in_specs=[SMEM] + [ANY] * count + [VMEM] * 5,
        out_specs=(VMEM,) * 2 + (ANY,) * len(shapes),
        scratch_shapes=[
            pltpu.VMEM((3, D, D), BF16),
            pltpu.VMEM((3, D, D), BF16),
            pltpu.SemaphoreType.DMA((count,)),
            pltpu.SemaphoreType.DMA((3 * count,)),
        ],
    )(owners, *blocks, tokens, grad_q, grad_k, grad_v, grad_first)
    return made[0], made[1], made[2:]


def weight_slots(parts, pieces):
    if is_small():
        return parts
    seq = lax.axis_size("seq")
    (part,) = parts
    rows = part.shape[1] // pieces // seq
    part = part.reshape(pieces, seq, rows, D).transpose(1, 0, 2, 3)
    return (part.reshape(seq, pieces * rows, D),)


def features(positions, starts):
    docs = starts.shape[0]
    segment = jnp.sum((positions[..., None] >= starts).astype(jnp.int32), axis=-1) - 1
    lane = jnp.arange(PAIR, dtype=jnp.int32) % HEAD_DIM
    own = segment[..., None] == lane
    return own, lane, docs


def on_device(
    inputs,
    cotangent,
    doc_lengths,
    doc_labels,
    query_weight,
    query_bias,
    key_weight,
    value_weight,
    value_bias,
    proj_weight,
    proj_bias,
    norm_gain,
    norm_shift,
    up_weight,
    up_bias,
    down_weight,
    down_bias,
    final_gain,
    final_shift,
    pool_weight,
    pool_bias,
    class_weight,
    class_bias,
):
    me = lax.axis_index("seq")
    tokens = inputs[0]
    share = query_bias.shape[0]
    lengths = doc_lengths[0]
    docs = lengths.shape[0]
    order = jnp.arange(docs, dtype=jnp.int32)
    starts = jnp.sum(jnp.where(order[None, :] < order[:, None], lengths[None, :], 0), axis=1)

    qkv_blocks, qkv_owners = gather_shared(jnp.stack([query_weight, key_weight, value_weight]), 0)
    small = jnp.stack(
        [
            query_bias, value_bias, proj_bias, norm_gain, norm_shift, down_bias,
            final_gain, final_shift, pool_bias, *class_weight.T,
        ]
    )
    table = jnp.zeros((TABLE, D), BF16)
    table = lax.dynamic_update_slice(table, small, (0, me * share))
    wide = me * up_bias.shape[0]
    if up_bias.shape[0] <= D:
        table = lax.dynamic_update_slice(table, up_bias[None], (UP_B + wide // D, wide % D))
    table = sum_seq(table).astype(F32)
    proj_blocks, proj_owners = gather_shared(jnp.stack([proj_weight, pool_weight]), 1)
    up_blocks, up_owners = gather_shared(up_weight, 1)
    down_blocks, down_owners = gather_shared(down_weight, 1)
    slots = slot_owners()
    targets = slots if is_small() else jnp.zeros((1,), jnp.int32)
    qkv_owners = jnp.stack([jnp.stack(qkv_owners), targets])
    owners = jnp.stack([jnp.stack(proj_owners), targets])

    query, key, value = qkv_project(qkv_owners, qkv_blocks, tokens, table)
    keys, values = gather_own(key, (2, 4)), gather_own(value, (4, 2))
    line = jnp.arange(ROWS, dtype=jnp.int32)
    own, lane, _ = features(me * ROWS + line, starts)
    feature_q = jnp.where(own, FAR, 0.0).astype(BF16)
    own, lane, _ = features(slots[:, None] * ROWS + line, starts)
    feature_k = jnp.where(
        lane < docs, jnp.where(own, 0.0, 1.0), jnp.where(lane < docs + 3, 1.0, 0.0)
    ).astype(BF16)
    attended, total = attend(query, keys, values, feature_q, feature_k, docs)

    place = (starts - me * ROWS)[:, None]
    made, down_parts = first_part(
        owners, proj_blocks, up_blocks, down_blocks, attended, tokens, cotangent[0], table,
        place, doc_labels[0][:, None], class_bias.astype(F32)[None],
    )
    output, lines_one, docs_out, grad_second, unit, inverse, slope = made
    made, up_parts = second_part(
        owners, proj_blocks, up_blocks, down_blocks, attended, table, grad_second, unit, inverse, slope
    )
    lines_two, grad_first, grad_attended = made

    grad_q, grad_k, grad_v = attend_back(
        query, keys, values, grad_attended, attended, total, feature_q, feature_k, docs
    )
    grad_k = scatter_sum(grad_k, (2, 4))
    grad_v = scatter_sum(grad_v, (4, 2))
    lines_three, input_grad, qkv_parts = last_part(
        qkv_owners, qkv_blocks, tokens, grad_q, grad_k, grad_v, grad_first
    )

    down_wgrad = sum_dp(scatter_sum(weight_slots(down_parts, 1), (2, 4)))
    up_wgrad = sum_dp(scatter_sum(weight_slots(up_parts, 5), (4, 2)))
    qkv_wgrad = sum_dp(scatter_sum(weight_slots(qkv_parts, 3), (2, 4)))
    proj_wgrad = up_wgrad[4 * share :]
    up_wgrad = up_wgrad[: 4 * share].reshape(4, share, D).transpose(1, 0, 2).reshape(share, FF)
    qkv_wgrad = qkv_wgrad.reshape(3, share, D)
    lines = sum_all(jnp.concatenate([lines_one, lines_two, lines_three], axis=0))
    docs_sum = sum_seq(docs_out)
    logits = docs_sum[:, 3 * D + CLASSES : 3 * D + 2 * CLASSES]
    every_doc = stack_dp(docs_sum)
    at = me * share

    def my_share(vector):
        return lax.dynamic_slice_in_dim(vector, at, share, 0)

    first_all, pooled_all = (
        lax.dynamic_slice_in_dim(every_doc, k * D + at, share, 1) for k in range(2)
    )
    pre_all = every_doc[:, 2 * D : 3 * D]
    logit_all = every_doc[:, 3 * D : 3 * D + CLASSES]
    exact = functools.partial(jnp.dot, precision=lax.Precision.HIGHEST)
    return (
        output[None],
        logits[None],
        input_grad[None],
        qkv_wgrad[0],
        my_share(lines[16]),
        qkv_wgrad[1],
        qkv_wgrad[2],
        my_share(lines[17]),
        proj_wgrad,
        my_share(lines[14]),
        my_share(lines[12]),
        my_share(lines[13]),
        up_wgrad,
        lax.dynamic_slice_in_dim(lines[8:12].reshape(-1), wide, up_bias.shape[0], 0),
        down_wgrad,
        my_share(lines[0]),
        my_share(lines[1]),
        my_share(lines[2]),
        exact(first_all.T, pre_all),
        my_share(jnp.sum(pre_all, axis=0)),
        exact(pooled_all.T, logit_all),
        jnp.sum(logit_all, axis=0),
    )


def solution(mesh):
    rows, row, part = P("dp", "seq", None), P("seq", None), P("seq")
    per_sequence = P("dp", None)
    in_specs = (
        rows, rows, per_sequence, per_sequence, row, part, row, row, part, row, part, part,
        part, row, part, row, part, part, part, row, part, row, P(),
    )
    out_specs = (
        rows, P("dp", None, None), rows, row, part, row, row, part, row, part, part, part,
        row, part, row, part, part, part, row, part, row, P(),
    )
    return jax.shard_map(
        on_device, mesh=mesh, in_specs=in_specs, out_specs=out_specs, check_vma=False
    )
```

```python
import functools

import jax
import jax.numpy as jnp
from jax import lax
from jax.experimental import pallas as pl
from jax.experimental.pallas import tpu as pltpu
from jax.sharding import PartitionSpec as P

D = 768
HEADS = 12
HEAD_DIM = 64
FF = 3072
CLASSES = 3
PAIR = 2 * HEAD_DIM
ROWS = 256
EPSILON = 1e-06
FAR = -1e30
LIMIT = 56 * 1024 * 1024
F32, BF16 = jnp.float32, jnp.bfloat16

QUERY_B, VALUE_B, PROJ_B, NORM_G, NORM_S, DOWN_B, FINAL_G, FINAL_S, POOL_B, CLASS_W, UP_B = (
    0, 1, 2, 3, 4, 5, 6, 7, 8, 9, 12,
)
TABLE = 16


def swap(value, partner):
    dp, seq = lax.axis_size("dp"), lax.axis_size("seq")
    pairs = []
    for z in range(dp):
        for i in range(seq):
            to_z, to_i = partner(z, i)
            pairs.append((z * seq + i, to_z * seq + to_i))
    return lax.ppermute(value, ("dp", "seq"), pairs)


def along(bit):
    return lambda z, i: (z, i ^ bit)


def is_small():
    return lax.axis_size("seq") == 8 and lax.axis_size("dp") == 4


class Shared:
    def __init__(self, shard, role):
        self.shard, self.role = shard, role

    def near(self):
        role = self.role
        self.one = swap(self.shard, lambda z, i: (z, i ^ (2 if (z + role) % 2 == 0 else 4)))

    def far(self):
        role = self.role
        self.both = swap(self.one, lambda z, i: (z, i ^ (4 if (z + role) % 2 == 0 else 2)))
        self.blocks = [self.shard, self.one]
        self.crossed = [swap(block, along(1)) for block in self.blocks]

    def rest(self, *earlier):
        self.other = swap(after(self.one, *earlier), lambda z, i: (z ^ 1, i))

    def finish(self):
        late = [self.both, self.other]
        return self.blocks + late + self.crossed + [swap(block, along(1)) for block in late]

    def owners(self):
        me, z = lax.axis_index("seq"), lax.axis_index("dp")
        near = jnp.where((z + self.role) % 2 == 0, 2, 4)
        owners = [me, me ^ near, me ^ 6, me ^ (6 - near)]
        owners = [owners[k] for k in (0, 1, 2, 3)] + [owners[k] ^ 1 for k in (0, 1, 2, 3)]
        return jnp.stack(owners)


def gather_tokens(tokens):
    if not is_small():
        return [tokens]
    far = swap(tokens, along(6))
    return [tokens, swap(tokens, along(2)), swap(tokens, along(4)), far]


def exchange(pieces):
    return [pieces[0]] + [swap(pieces[s], along(2 * s)) for s in range(1, len(pieces))]


def slot_owners():
    if not is_small():
        return jnp.arange(lax.axis_size("seq"), dtype=jnp.int32)
    return lax.axis_index("seq") ^ jnp.array([0, 2, 4, 6, 1, 3, 5, 7], jnp.int32)


def add(*terms):
    return functools.reduce(jnp.add, [term.astype(F32) for term in terms])


class Scatter:
    def __init__(self, parts):
        self.firsts, self.seconds, self.own = parts[0:2], parts[2:4], parts[4]
        self.comes = [swap(a, along(bit)) for a, bit in zip(self.firsts, (2, 4))]

    def combine(self, *earlier):
        seconds = after(self.seconds, *earlier)
        self.sends = [add(a, come[1]).astype(BF16) for a, come in zip(seconds, self.comes)]

    def turn(self):
        self.lasts = [swap(a, along(bit)) for a, bit in zip(self.sends, (4, 2))]

    def total(self):
        half = self.own.shape[0] // 2
        owns = (self.own[:half], self.own[half:])
        return jnp.concatenate(
            [add(own, come[0], last) for own, come, last in zip(owns, self.comes, self.lasts)]
        )


def after(values, *others):
    return lax.optimization_barrier((values, others))[0]


class SumDp:
    def __init__(self, shard):
        z = lax.axis_index("dp")
        half = shard.shape[0] // 2
        self.low = jnp.logical_or(z == 0, z == 3)
        first, second = shard[:half], shard[half:]
        self.keep = jnp.where(self.low, first, second)
        self.come = swap(
            jnp.where(self.low, second, first).astype(BF16), lambda z, i: (z ^ 1, i)
        )

    def across(self):
        self.pair = add(self.keep, self.come).astype(BF16)
        self.cross = swap(self.pair, lambda z, i: (z ^ 3, i))

    def back(self):
        total = add(self.pair, self.cross).astype(BF16)
        come = swap(total, lambda z, i: (z ^ 1, i))
        low = self.low
        return jnp.concatenate(
            [jnp.where(low, total, come), jnp.where(low, come, total)], axis=0
        ).astype(F32)


def sum_dp(shard):
    if not is_small():
        return lax.psum(shard.astype(BF16), "dp").astype(F32)
    total = SumDp(shard)
    total.across()
    return total.back()


def sum_seq(value):
    if not is_small():
        return lax.psum(value, "seq")
    for bit in (1, 2, 4):
        value = value + swap(value, along(bit))
    return value


def sum_all(value):
    value = sum_seq(value)
    if not is_small():
        return lax.psum(value, "dp")
    for bit in (1, 2):
        value = value + swap(value, lambda z, i: (z ^ bit, i))
    return value


def stack_dp(value):
    if not is_small():
        return lax.all_gather(value, "dp", axis=0, tiled=True)
    for bit in (1, 2):
        value = jnp.concatenate([value, swap(value, lambda z, i: (z ^ bit, i))], axis=0)
    return value


def dot(left, right, contract=((1,), (0,))):
    return lax.dot_general(left, right, (contract, ((), ())), preferred_element_type=F32)


def call(body, name, micros, **kwargs):
    return pl.pallas_call(
        body,
        name=name,
        cost_estimate=pl.CostEstimate(
            flops=int(micros * 1.1e9), transcendentals=0, bytes_accessed=int(micros * 1e6)
        ),
        compiler_params=pltpu.CompilerParams(vmem_limit_bytes=LIMIT),
        **kwargs,
    )


VMEM = pl.BlockSpec(memory_space=pltpu.VMEM)
ANY = pl.BlockSpec(memory_space=pl.ANY)
SMEM = pl.BlockSpec(memory_space=pltpu.SMEM)


def start(copies):
    for copy in copies:
        copy.start()
    return copies


def wait(copies):
    for copy in copies:
        copy.wait()


def block_copies(places, line, refs, target, sems, part=None):
    copies = []
    for slot, ref in enumerate(refs):
        source = ref if part is None else ref.at[part]
        rows = source.shape[-2]
        first = pl.multiple_of(places[line, slot] * rows, rows)
        if len(source.shape) == 3:
            place = target.at[:, pl.ds(first, rows), :]
        else:
            place = target.at[pl.ds(first, rows), :]
        copies.append(pltpu.make_async_copy(source, place, sems.at[slot]))
    return start(copies)


def weight_refs(weights):
    return [ref.at[s] for ref in weights for s in range(ref.shape[0])]


def qkv_kernel(blocks, sides, places, *refs):
    tokens, refs = refs[:blocks], refs[blocks:]
    weights, (bias, query, keyval, held, sems) = refs[:sides], refs[sides:]
    wait(block_copies(places, 0, weight_refs(weights), held, sems))
    for s in range(query.shape[0]):
        rows = tokens[s][...]
        keyval[0, s] = dot(rows, held[1]).astype(BF16)
        keyval[1, s] = (dot(rows, held[2]) + bias[1:2]).astype(BF16)
        query[s] = (dot(rows, held[0]) + bias[0:1]).astype(BF16)


def qkv_project(places, tokens, weights, bias):
    slots = len(tokens)
    lanes = weights[0].shape[-1]
    out = jax.ShapeDtypeStruct((slots, ROWS, lanes), BF16)
    pair = jax.ShapeDtypeStruct((2, slots, ROWS, lanes), BF16)
    return call(
        functools.partial(qkv_kernel, len(tokens), len(weights)),
        "qkv",
        5,
        out_shape=(out, pair),
        in_specs=[SMEM] + [VMEM] * len(tokens) + [ANY] * len(weights) + [VMEM],
        out_specs=(VMEM,) * 2,
        scratch_shapes=[
            pltpu.VMEM((3, D, lanes), BF16),
            pltpu.SemaphoreType.DMA((len(weights) * weights[0].shape[0],)),
        ],
    )(places, *tokens, *weights, bias)


def left_half(shape):
    return lax.broadcasted_iota(jnp.int32, shape, len(shape) - 1) < HEAD_DIM


def split3(value):
    high = value.astype(BF16).astype(F32)
    middle = (value - high).astype(BF16).astype(F32)
    low = (value - high - middle).astype(BF16).astype(F32)
    return high, middle, low


def spread3(value, docs, shape):
    lane = lax.broadcasted_iota(jnp.int32, shape, 1) % HEAD_DIM
    high, middle, low = split3(value)
    return jnp.where(
        lane == docs, high, jnp.where(lane == docs + 1, middle, jnp.where(lane == docs + 2, low, 0.0))
    )


def chunks_of(refs):
    number = 0
    for ref in refs:
        for index in range(ref.shape[1]):
            yield ref, index, number
            number += 1


def over_chunks(refs, step):
    if len(refs) > 1:
        for at in chunks_of(refs):
            step(*at)
    else:
        pl.loop(0, refs[0].shape[1])(lambda index: step(refs[0], index, index))


def attend_kernel(sides, docs, odd, *refs):
    query, feature_q, feature_k = refs[:3]
    keyvals = refs[3 : 3 + sides]
    slots = feature_q.shape[0]
    rest = refs[3 + sides :]
    wide, total, lows, (scores, acc, most) = rest[0], rest[1], rest[2:-3], rest[-3:]
    tile, slot = pl.program_id(0), pl.program_id(1)
    left = left_half((ROWS, PAIR))
    rows = query[0] * 0.125
    spare = feature_q[slot]

    def one_head(head):
        mine = left if head == 0 else jnp.logical_not(left)
        aug = jnp.where(mine, rows, spare)
        most[...] = jnp.full_like(most, FAR)

        def score_step(ref, index, number):
            full = jnp.where(mine, ref[0, index], feature_k[number])
            made = dot(aug, full, ((1,), (1,)))
            scores[number] = made
            most[...] = jnp.maximum(most[...], jnp.maximum(made[:, :PAIR], made[:, PAIR:]))

        over_chunks(keyvals, score_step)
        top = jnp.max(most[...], axis=1, keepdims=True)
        acc[...] = jnp.zeros_like(acc)

        def value_step(ref, index, number):
            full = jnp.where(mine, ref[1, index], feature_k[number])
            acc[...] += dot(jnp.exp(scores[number] - top).astype(BF16), full)

        over_chunks(keyvals, value_step)
        found = acc[...]
        lane = docs + (HEAD_DIM if head == 0 else 0)
        weight = found[:, lane : lane + 1]
        return found / weight, top + jnp.log(weight)

    result, sums = one_head(0)
    wide[0] = result
    total[0] = jnp.broadcast_to(sums, (ROWS, PAIR))

    def second_head():
        result, sums = one_head(1)
        wide[0] = jnp.where(left, wide[0], result)
        total[0] = jnp.where(left, total[0], sums)

    if odd:
        pl.when(tile < pl.num_programs(0) - 1)(second_head)
    else:
        second_head()
    for s in range(slots):

        @pl.when(slot == s)
        def _(s=s):
            lows[s][...] = wide[0].astype(BF16)


def slot_spec(array, base=0):
    return pl.BlockSpec((1, ROWS, PAIR), lambda tile, slot: (slot, 0, tile + base))


def tile_spec(array, base=0):
    lead = array.shape[:-1]
    return pl.BlockSpec(lead + (PAIR,), lambda tile, slot: (0,) * len(lead) + (tile + base,))


def fixed_spec(array):
    return pl.BlockSpec(array.shape, lambda tile, slot: (0,) * array.ndim)


def attend(query, keyvals, feature_q, feature_k, docs):
    slots, tiles = query.shape[0], query.shape[-1] // PAIR
    wide = jax.ShapeDtypeStruct(query.shape, F32)
    low = jax.ShapeDtypeStruct(wide.shape[1:], BF16)
    chunks = feature_k.shape[0]
    made = call(
        functools.partial(attend_kernel, len(keyvals), docs, slots > 1),
        "attend",
        15,
        grid=(tiles, slots),
        out_shape=(wide, wide) + (low,) * slots,
        in_specs=[slot_spec(query), fixed_spec(feature_q), fixed_spec(feature_k)]
        + [tile_spec(a) for a in keyvals],
        out_specs=(slot_spec(wide),) * 2 + (tile_spec(low),) * slots,
        scratch_shapes=[
            pltpu.VMEM((chunks, ROWS, ROWS), F32),
            pltpu.VMEM((ROWS, PAIR), F32),
            pltpu.VMEM((ROWS, PAIR), F32),
        ],
    )(query, feature_q, feature_k, *keyvals)
    return made[0], made[1], list(made[2:])


def attend_back_kernel(sides, docs, single, *refs):
    query, wide, total, feature_q, feature_k = refs[:5]
    slots = feature_q.shape[0]
    grads_in, keyvals = refs[5 : 5 + slots], refs[5 + slots : 5 + slots + sides]
    rest = refs[5 + slots + sides :]
    grad_q, outs, (grad, acc_q, acc_k, acc_v) = rest[0], rest[1 : 1 + sides], rest[1 + sides :]
    slot = pl.program_id(1)
    left = left_half((ROWS, PAIR))
    for s in range(slots):

        @pl.when(slot == s)
        def _(s=s):
            grad[...] = grads_in[s][...]

    @pl.when(slot == 0)
    def _():
        acc_k[...] = jnp.zeros_like(acc_k)
        acc_v[...] = jnp.zeros_like(acc_v)

    rows = query[0] * 0.125
    grads = grad[...]
    product = grads.astype(F32) * wide[0]
    spare = feature_q[slot].astype(F32)
    zero = jnp.zeros_like(rows)
    acc_q[...] = jnp.zeros_like(acc_q)

    def one_head(head):
        mine = left if head == 0 else jnp.logical_not(left)
        at = head * HEAD_DIM
        delta = jnp.sum(jnp.where(mine, product, 0.0), axis=1, keepdims=True)
        sums = total[0, :, at : at + 1]
        query_t = jnp.where(
            mine, rows.astype(F32), spare + spread3(-sums, docs, (ROWS, PAIR))
        ).T.astype(BF16)
        grad_t = jnp.where(
            mine, grads.astype(F32), spread3(-delta, docs, (ROWS, PAIR))
        ).T.astype(BF16)
        query_own, grad_own = jnp.where(mine, rows, zero), jnp.where(mine, grads, zero)

        def step(ref, index, number):
            key, value, feature = ref[0, index], ref[1, index], feature_k[number]
            soft = jnp.exp(dot(jnp.where(mine, key, feature), query_t))
            change = dot(jnp.where(mine, value, feature), grad_t)
            slope = (soft * change).astype(BF16)
            acc_v[number] += dot(soft.astype(BF16), grad_own)
            acc_k[number] += dot(slope, query_own)
            key_t = key.astype(F32).T[at : at + HEAD_DIM].astype(BF16)
            acc_q[at : at + HEAD_DIM] += dot(key_t, slope)

        over_chunks(keyvals, step)

    one_head(0)
    if not single:
        one_head(1)
    grad_q[0] = (acc_q[...].T * 0.125).astype(BF16)

    @pl.when(slot == slots - 1)
    def _():
        number = 0
        for out in outs:
            count = out.shape[1]
            out[0] = acc_k[number : number + count].astype(BF16)
            out[1] = acc_v[number : number + count].astype(BF16)
            number += count


def attend_back(query, keyvals, grads, wide, total, feature_q, feature_k, docs, base, tiles, single):
    slots = query.shape[0]
    chunks = feature_k.shape[0]
    outs = tuple(
        jax.ShapeDtypeStruct(a.shape[:-1] + (tiles * PAIR,), BF16) for a in (query, *keyvals)
    )
    made = call(
        functools.partial(attend_back_kernel, len(keyvals), docs, single),
        "attend_back",
        10 if single else 21,
        grid=(tiles, slots),
        out_shape=outs,
        in_specs=[slot_spec(a, base) for a in (query, wide, total)]
        + [fixed_spec(feature_q), fixed_spec(feature_k)]
        + [tile_spec(a, base) for a in (*grads, *keyvals)],
        out_specs=(slot_spec(outs[0]),) + tuple(tile_spec(a) for a in outs[1:]),
        scratch_shapes=[
            pltpu.VMEM((ROWS, PAIR), BF16),
            pltpu.VMEM((PAIR, ROWS), F32),
            pltpu.VMEM((chunks, ROWS, PAIR), F32),
            pltpu.VMEM((chunks, ROWS, PAIR), F32),
        ],
    )(query, wide, total, feature_q, feature_k, *grads, *keyvals)
    return made[0], list(made[1:])


def normalise(value):
    centred = value - jnp.mean(value, axis=-1, keepdims=True)
    inverse = lax.rsqrt(jnp.mean(centred * centred, axis=-1, keepdims=True) + EPSILON)
    return centred * inverse, inverse


def norm_back(grad, gain, unit, inverse):
    scaled = grad * gain
    return inverse * (
        scaled
        - jnp.mean(scaled, axis=-1, keepdims=True)
        - unit * jnp.mean(scaled * unit, axis=-1, keepdims=True)
    )


def erf(value):
    value = jnp.clip(value, -3.7439211627767994, 3.7439211627767994)
    square = value * value
    top = 0.00022905065861350646
    for factor in (0.0034082910107109506, 0.050955695062380861, 0.18520832239976145, 1.128379143519084):
        top = top * square + factor
    bottom = -1.1791602954361697e-7
    for factor in (
        0.000023547966471313185, 0.0010179625278914885, 0.014070470171167667,
        0.11098505178285362, 0.49746925110067538, 1.0,
    ):
        bottom = bottom * square + factor
    return value * top / bottom


def column_sum(value):
    return jnp.sum(value, axis=0, keepdims=True)


def first_kernel(count, slots, places, *refs):
    blocks, refs = refs[:count], refs[count:]
    attended, refs = refs[:slots], refs[slots:]
    tokens, table = refs[:2]
    unit, inverse, active, slope, sides = *refs[2:6], refs[6:-3]
    weights, turned, sems = refs[-3:]
    copies = block_copies(places, 1, blocks, weights, sems)
    width = D // slots

    def row(at):
        return table[at : at + 1]

    def put(target, s, value):
        target[s] = value

    core = places[0, 0] % 2 if slots > 1 else 0
    per = width // 2 if slots > 1 else width
    rows_of = [a[...] for a in attended]
    for s in range(slots):
        turned[0 : rows_of[s].shape[1]] = rows_of[s].astype(F32).T.astype(BF16)
        if slots > 1:
            sides[0][slots + s] = turned[pl.ds(pl.multiple_of(core * per, per), per)]
            sides[1][slots + s] = turned[pl.ds(pl.multiple_of((1 - core) * per, per), per)]
        else:
            sides[0][1] = turned[...]
    wait(copies)
    residual = tokens[...].astype(F32) + row(PROJ_B)
    for s in range(slots):
        first = pl.multiple_of((places[0, s] // 2) * width, width)
        residual = residual + dot(rows_of[s][:, :width], weights[0, pl.ds(first, width), :])
    first_unit, first_inverse = normalise(residual)
    unit[...] = first_unit
    inverse[...] = first_inverse
    normed = first_unit * row(NORM_G) + row(NORM_S)
    normed_low = normed.astype(BF16)
    turned[...] = normed.T.astype(BF16)
    for side, target in enumerate(sides[:2] if slots > 1 else sides[:1]):
        for s in range(slots):
            rows = target.shape[1]
            first = pl.multiple_of(places[0, side * slots + s] * rows, rows)
            target[s] = turned[pl.ds(first, rows)]
    step = 384
    for at in range(0, FF, step):
        line, col = at // D, at % D
        upward = (
            dot(normed_low, weights[1 + line, :, col : col + step])
            + table[UP_B + line : UP_B + line + 1, col : col + step]
        )
        share = 0.5 + 0.5 * erf(upward * 0.7071067811865476)
        bell = jnp.exp(upward * upward * -0.5) * 0.3989422804014327
        active[:, at : at + step] = (upward * share).astype(BF16)
        slope[:, at : at + step] = share + upward * bell
    for side, target in enumerate(sides[2:] if slots > 1 else sides[1:]):
        for s in range(slots):
            rows = target.shape[1]
            if slots > 1:
                first = pl.multiple_of(places[0, side * slots + s] * rows, rows)
                target[s] = active[:, pl.ds(first, rows)].astype(F32).T.astype(BF16)
            else:
                for at in range(0, FF, D):
                    target[s, at : at + D] = active[:, at : at + D].astype(F32).T.astype(BF16)


def first_part(places, blocks, attended, tokens, table):
    slots = len(attended)
    shape = jax.ShapeDtypeStruct
    sides = 2 if slots > 1 else 1
    outs = (
        shape((ROWS, D), F32), shape((ROWS, 1), F32), shape((ROWS, FF), BF16), shape((ROWS, FF), F32),
    )
    outs += (shape((2 * slots, D // sides // slots, ROWS), BF16),) * sides
    outs += (shape((slots, FF // sides // slots, ROWS), BF16),) * sides
    made = call(
        functools.partial(first_kernel, len(blocks), slots),
        "forward_up",
        11,
        out_shape=outs,
        in_specs=[SMEM] + [ANY] * len(blocks) + [VMEM] * (slots + 2),
        out_specs=(VMEM,) * len(outs),
        scratch_shapes=[
            pltpu.VMEM((5, D, D), BF16),
            pltpu.VMEM((D, ROWS), BF16),
            pltpu.SemaphoreType.DMA((len(blocks),)),
        ],
    )(places, *blocks, *attended, tokens, table)
    return made[:4], made[4 : 4 + sides], made[4 + sides :]


def head_kernel(count, docs, places, *refs):
    blocks, refs = refs[:count], refs[count:]
    unit, active, cotangent, table, place, labels, class_b = refs[:7]
    output, lines, docs_out, grad_second, grad_out = refs[7:12]
    pool, down, sems = refs[12:]
    down_copies = block_copies(places, 2, blocks, down, sems.at[1], slice(0, FF // count))
    pool_copies = block_copies(places, 2, blocks, pool, sems.at[0], slice(FF // count, (FF + D) // count))

    def row(at):
        return table[at : at + 1]

    normed = unit[...] * row(NORM_G) + row(NORM_S)
    wait(down_copies)
    residual = normed + dot(active[...], down[...]) + row(DOWN_B)
    last_unit, last_inverse = normalise(residual)
    outcome = last_unit * row(FINAL_G) + row(FINAL_S)
    out_low = outcome.astype(BF16)
    output[...] = out_low

    at_row = place[...]
    here = jnp.logical_and(at_row >= 0, at_row < ROWS)
    pick = jnp.where(lax.broadcasted_iota(jnp.int32, (docs, ROWS), 1) == at_row, 1.0, 0.0)
    first_low = dot(pick.astype(BF16), out_low).astype(BF16)
    wait(pool_copies)
    pooled = jnp.tanh(dot(first_low, pool[...]) + row(POOL_B))
    pooled_low = pooled.astype(BF16).astype(F32)
    logits = [
        jnp.sum(pooled_low * row(CLASS_W + c), axis=1, keepdims=True) + class_b[0, c]
        for c in range(CLASSES)
    ]
    top = functools.reduce(jnp.maximum, logits)
    powers = [jnp.exp(logit - top) for logit in logits]
    whole = functools.reduce(jnp.add, powers)
    label = labels[...]
    grads = [powers[c] / whole - jnp.where(label == c, 1.0, 0.0) for c in range(CLASSES)]
    grad_pre = functools.reduce(jnp.add, [grads[c] * row(CLASS_W + c) for c in range(CLASSES)])
    grad_pre = grad_pre * (1.0 - pooled * pooled)
    parts = jnp.concatenate(split3(grad_pre), axis=0).astype(BF16)
    made = dot(parts, pool[...], ((1,), (1,)))
    grad_first = made[:docs] + made[docs : 2 * docs] + made[2 * docs :]
    parts = jnp.concatenate(split3(grad_first), axis=0).astype(BF16)
    picks = jnp.concatenate([pick] * 3, axis=0).astype(BF16)
    grad_outcome = cotangent[...] + dot(picks, parts, ((0,), (0,)))
    lane = lax.broadcasted_iota(jnp.int32, (docs, 128), 1)
    small = jnp.zeros((docs, 128), F32)
    for c in range(CLASSES):
        small = jnp.where(lane == c, grads[c], jnp.where(lane == CLASSES + c, logits[c], small))
    docs_out[...] = jnp.where(
        here,
        jnp.concatenate([first_low.astype(F32), pooled_low, grad_pre, small], axis=1),
        0.0,
    )

    grad = norm_back(grad_outcome, row(FINAL_G), last_unit, last_inverse)
    grad_second[...] = grad
    grad_out[...] = grad.astype(BF16)
    lines[0:1] = column_sum(grad)
    lines[1:2] = column_sum(grad_outcome * last_unit)
    lines[2:3] = column_sum(grad_outcome)
    lines[3:8] = jnp.zeros((5, D), F32)


def head_part(places, blocks, unit, active, cotangent, table, place, labels, class_b):
    count, docs = len(blocks), place.shape[0]
    shape = jax.ShapeDtypeStruct
    outs = (
        shape((ROWS, D), BF16),
        shape((8, D), F32),
        shape((docs, 3 * D + 128), F32),
        shape((ROWS, D), F32),
        shape((ROWS, D), BF16),
    )
    return call(
        functools.partial(head_kernel, count, docs),
        "head",
        7,
        out_shape=outs,
        in_specs=[SMEM] + [ANY] * count + [VMEM] * 6 + [SMEM],
        out_specs=(VMEM,) * len(outs),
        scratch_shapes=[
            pltpu.VMEM((D, D), BF16),
            pltpu.VMEM((FF, D), BF16),
            pltpu.SemaphoreType.DMA((2, count)),
        ],
    )(places, *blocks, unit, active, cotangent, table, place, labels, class_b)


def second_kernel(count, places, *refs):
    downs, (grad_down, slope, lines, grad_up, down, sems) = refs[:count], refs[count:]
    wait(block_copies(places, 2, downs, down, sems, slice(0, FF // count)))
    grad_low = grad_down[...]
    step = 384
    for at in range(0, FF, step):
        grad = dot(grad_low, down[at : at + step], ((1,), (1,))).astype(BF16).astype(F32)
        grad = grad * slope[:, at : at + step]
        line, col = at // D, at % D
        lines[line : line + 1, col : col + step] = column_sum(grad)
        grad_up[line, :, col : col + step] = grad.astype(BF16)
    lines[4:8] = jnp.zeros((4, D), F32)


def second_part(places, down_blocks, grad_down, slope):
    count, shape = len(down_blocks), jax.ShapeDtypeStruct
    outs = (shape((8, D), F32), shape((4, ROWS, D), BF16))
    return call(
        functools.partial(second_kernel, count),
        "backward_down",
        5,
        out_shape=outs,
        in_specs=[SMEM] + [ANY] * count + [VMEM] * 2,
        out_specs=(VMEM,) * 2,
        scratch_shapes=[pltpu.VMEM((FF, D), BF16), pltpu.SemaphoreType.DMA((count,))],
    )(places, *down_blocks, grad_down, slope)


def third_kernel(count, slots, places, *refs):
    blocks, refs = refs[:count], refs[count:]
    table, grad_second, grad_up, unit, inverse = refs[:5]
    lines, grad_first, grad_out = refs[5:8]
    grad_attended = refs[8 : 8 + slots]
    weights, sems = refs[8 + slots :]
    wait(block_copies(places, 1, blocks, weights, sems))
    width = D // slots

    def row(at):
        return table[at : at + 1]

    back = dot(grad_up[0], weights[1], ((1,), (1,)))
    for line in range(1, 4):
        back = back + dot(grad_up[line], weights[1 + line], ((1,), (1,)))
    grad_normed = grad_second[...] + back.astype(BF16).astype(F32)
    lines[0:4] = jnp.zeros((4, D), F32)
    lines[4:5] = column_sum(grad_normed * unit[...])
    lines[5:6] = column_sum(grad_normed)
    grad = norm_back(grad_normed, row(NORM_G), unit[...], inverse[...])
    grad_first[...] = grad
    lines[6:7] = column_sum(grad)
    lines[7:8] = jnp.zeros((1, D), F32)
    grad_low = grad.astype(BF16)
    grad_out[...] = grad_low
    for s in range(slots):
        first = pl.multiple_of((places[0, s] // 2) * width, width)
        made = dot(grad_low, weights[0, pl.ds(first, width), :], ((1,), (1,))).astype(BF16)
        if width < grad_attended[s].shape[1]:
            grad_attended[s][:, PAIR:] = jnp.zeros((ROWS, PAIR), BF16)
        grad_attended[s][:, :width] = made


def third_part(places, blocks, table, grad_second, grad_up, unit, inverse, slots, lanes):
    count = len(blocks)
    shape = jax.ShapeDtypeStruct
    outs = (shape((8, D), F32), shape((ROWS, D), F32), shape((ROWS, D), BF16))
    outs += (shape((ROWS, lanes), BF16),) * slots
    made = call(
        functools.partial(third_kernel, count, slots),
        "backward_up",
        7,
        out_shape=outs,
        in_specs=[SMEM] + [ANY] * count + [VMEM] * 5,
        out_specs=(VMEM,) * len(outs),
        scratch_shapes=[pltpu.VMEM((5, D, D), BF16), pltpu.SemaphoreType.DMA((count,))],
    )(places, *blocks, table, grad_second, grad_up, unit, inverse)
    return made[:3], list(made[3:])


def wgrad_outs(slots, rows):
    shape = jax.ShapeDtypeStruct
    if slots == 1:
        return (shape((1, rows, D), BF16),)
    half = rows // 2
    return (shape((2, half, D), BF16),) * 2 + (shape((half, D), BF16),) * 2 + (shape((rows, D), F32),)


def put_slot(outs, s, first, value):
    if len(outs) == 1:
        outs[0][0, first : first + value.shape[0]] = value.astype(BF16)
        return
    if s == 0:
        outs[4][first : first + value.shape[0]] = value
        return
    half = outs[2].shape[0]
    for k, order in enumerate(((1, 3, 2), (2, 3, 1))):
        low, high = max(first, k * half), min(first + value.shape[0], (k + 1) * half)
        if low >= high:
            continue
        rows, part = slice(low - k * half, high - k * half), value[low - first : high - first]
        if s == order[2]:
            outs[2 + k][rows] = part.astype(BF16)
        else:
            outs[k][order.index(s), rows] = part.astype(BF16)


def down_kernel(sides, *refs):
    lefts, rights, outs = refs[:sides], refs[sides : 2 * sides], refs[2 * sides :]
    step = min(lefts[0].shape[1], 384)
    for s in range(lefts[0].shape[0]):
        for at in range(0, lefts[0].shape[1], step):
            made = dot(lefts[0][s, at : at + step], rights[0][...])
            for side in range(1, sides):
                made = made + dot(lefts[side][s, at : at + step], rights[side][...])
            put_slot(outs, s, at, made)


def down_gradient(lefts, rights):
    sides, (slots, rows, _) = len(lefts), lefts[0].shape
    outs = wgrad_outs(slots, rows)
    return call(
        functools.partial(down_kernel, sides),
        "down_gradient",
        3,
        out_shape=outs,
        in_specs=[VMEM] * (2 * sides),
        out_specs=(VMEM,) * len(outs),
    )(*lefts, *rights)


def up_kernel(sides, *refs):
    lefts, ups, projs = (refs[k * sides : (k + 1) * sides] for k in range(3))
    outs = refs[3 * sides :]
    slots, rows = lefts[0].shape[0] // 2, lefts[0].shape[1]
    for line in range(5):
        at = 0 if line < 4 else slots
        made = 0.0
        for left, up, proj in zip(lefts, ups, projs):
            left = left[at : at + slots].reshape(slots * rows, ROWS)
            made = made + dot(left, up[line] if line < 4 else proj[...])
        for s in range(slots):
            put_slot(outs, s, line * rows, made[s * rows : (s + 1) * rows])


def up_gradient(lefts, ups, projs):
    sides, (slots, rows, _) = len(lefts), lefts[0].shape
    outs = wgrad_outs(slots // 2, 5 * rows)
    return call(
        functools.partial(up_kernel, sides),
        "up_gradient",
        4,
        out_shape=outs,
        in_specs=[VMEM] * (3 * sides),
        out_specs=(VMEM,) * len(outs),
    )(*lefts, *ups, *projs)


def last_kernel(blocks, sides, groups, parts, places, *refs):
    tokens, refs = refs[:blocks], refs[blocks:]
    weights, refs = refs[:sides], refs[sides:]
    grad_qs, refs = refs[:groups], refs[groups:]
    changes, refs = refs[: groups * parts], refs[groups * parts :]
    grad_first, lines, own, outs = *refs[:3], refs[3:-6]
    held, turned, grads, made, sems, out_sems = refs[-6:]
    slots = grad_qs[0].shape[0]
    copies = block_copies(places, 0, weight_refs(weights), held, sems)
    sums = [0.0, 0.0]
    for s in range(slots):
        rows = slice(s * ROWS, (s + 1) * ROWS)
        turned[:, rows] = tokens[s][...].astype(F32).T.astype(BF16)
        lane = 0
        for group in range(groups):
            lanes = slice(lane, lane + grad_qs[group].shape[2])
            lane = lanes.stop
            grads[0, rows, lanes] = grad_qs[group][s]
            for k in range(2):
                total = changes[group * parts][k, s].astype(F32)
                for change in changes[group * parts + 1 : (group + 1) * parts]:
                    total = total + change[k, s].astype(F32)
                grads[1 + k, rows, lanes] = total.astype(BF16)
        sums[0] = sums[0] + column_sum(grads[0, rows].astype(F32))
        sums[1] = sums[1] + column_sum(grads[2, rows].astype(F32))
    lines[0:1], lines[1:2] = sums
    lines[2:8] = jnp.zeros((6, lines.shape[1]), F32)
    for k in range(3):
        made[k] = dot(turned[...], grads[k]).astype(BF16)
    sends = []
    for side, out in enumerate(outs[:sides]):
        for s in range(out.shape[0]):
            rows = out.shape[2]
            first = pl.multiple_of(places[0, side * out.shape[0] + s] * rows, rows)
            sends.append((made.at[:, pl.ds(first, rows), :], out.at[s]))
    sends = start(
        [pltpu.make_async_copy(a, b, out_sems.at[k]) for k, (a, b) in enumerate(sends)]
    )
    wait(copies)

    def partial(s):
        rows = slice(s * ROWS, (s + 1) * ROWS)
        total = dot(grads[0, rows], held[0], ((1,), (1,)))
        for k in range(1, 3):
            total = total + dot(grads[k, rows], held[k], ((1,), (1,)))
        return total

    if slots > 1:
        a_first, b_first, a_last, b_last = outs[sides:]
        half = ROWS // 2
        for s in (3, 1, 2):
            total = partial(s).astype(BF16)
            if s in (1, 3):
                a_first[s // 2] = total[:half]
            else:
                a_last[...] = total[:half]
            if s in (2, 3):
                b_first[s - 2] = total[half:]
            else:
                b_last[...] = total[half:]
    own[...] = grad_first[...] + partial(0)
    wait(sends)


def last_part(places, tokens, weights, grad_qs, changes, grad_first):
    slots, lanes = grad_qs[0].shape[0], sum(grad.shape[2] for grad in grad_qs)
    groups, parts = len(grad_qs), len(changes) // len(grad_qs)
    sides, shape = len(weights), jax.ShapeDtypeStruct
    outs = (shape((8, lanes), F32), shape((ROWS, D), F32))
    outs += tuple(shape(a.shape, BF16) for a in weights)
    if slots > 1:
        half = ROWS // 2
        outs += (shape((2, half, D), BF16),) * 2 + (shape((half, D), BF16),) * 2
    blocks = sides * weights[0].shape[0]
    made = call(
        functools.partial(last_kernel, len(tokens), sides, groups, parts),
        "input_gradients",
        8,
        out_shape=outs,
        in_specs=[SMEM] + [VMEM] * len(tokens) + [ANY] * sides
        + [VMEM] * (1 + groups + len(changes)),
        out_specs=(VMEM,) * 2 + (ANY,) * sides + (VMEM,) * (len(outs) - 2 - sides),
        scratch_shapes=[
            pltpu.VMEM((3, D, lanes), BF16),
            pltpu.VMEM((D, slots * ROWS), BF16),
            pltpu.VMEM((3, slots * ROWS, lanes), BF16),
            pltpu.VMEM((3, D, lanes), BF16),
            pltpu.SemaphoreType.DMA((blocks,)),
            pltpu.SemaphoreType.DMA((blocks,)),
        ],
    )(places, *tokens, *weights, *grad_qs, *changes, grad_first)
    return made[0], made[1], list(made[2 : 2 + sides]), made[2 + sides :]


def whole_scatter(part, pieces):
    seq = lax.axis_size("seq")
    rows = part.shape[1] // pieces // seq
    part = part.reshape(pieces, seq, rows, D).transpose(1, 0, 2, 3)
    part = part.reshape(seq, pieces * rows, D)
    return lax.psum_scatter(part, "seq", scatter_dimension=0, tiled=True)[0].astype(F32)


def by_chip(pieces):
    me = lax.axis_index("seq")
    for bit in (1, 2):
        odd = (me & (2 * bit)) != 0
        pieces = [jnp.where(odd, pieces[s ^ bit], pieces[s]) for s in range(len(pieces))]
    return pieces


def features(positions, starts):
    docs = starts.shape[0]
    segment = jnp.sum((positions[..., None] >= starts).astype(jnp.int32), axis=-1) - 1
    lane = jnp.arange(PAIR, dtype=jnp.int32) % HEAD_DIM
    own = segment[..., None] == lane
    return own, lane, docs


def on_device(
    inputs,
    cotangent,
    doc_lengths,
    doc_labels,
    query_weight,
    query_bias,
    key_weight,
    value_weight,
    value_bias,
    proj_weight,
    proj_bias,
    norm_gain,
    norm_shift,
    up_weight,
    up_bias,
    down_weight,
    down_bias,
    final_gain,
    final_shift,
    pool_weight,
    pool_bias,
    class_weight,
    class_bias,
):
    me = lax.axis_index("seq")
    tokens = inputs[0]
    share = query_bias.shape[0]
    lengths = doc_lengths[0]
    docs = lengths.shape[0]
    order = jnp.arange(docs, dtype=jnp.int32)
    starts = jnp.sum(jnp.where(order[None, :] < order[:, None], lengths[None, :], 0), axis=1)

    small_mesh = is_small()
    slot_list = slot_owners()
    chip, core = me // 2, me % 2
    width = D // 4
    slots = 4 if small_mesh else 1
    line = jnp.arange(ROWS, dtype=jnp.int32)
    mine = slot_list[:slots] if small_mesh else me[None]
    own, lane, _ = features(mine[:, None] * ROWS + line, starts)
    feature_q = jnp.where(own, FAR, 0.0).astype(BF16)
    own, lane, _ = features(slot_list[:, None] * ROWS + line, starts)
    feature_k = jnp.where(
        lane < docs, jnp.where(own, 0.0, 1.0), jnp.where(lane < docs + 3, 1.0, 0.0)
    ).astype(BF16)

    matrices = jnp.stack([query_weight, key_weight, value_weight])
    bias = jnp.stack([query_bias, value_bias])
    small = jnp.stack(
        [
            query_bias, value_bias, proj_bias, norm_gain, norm_shift, down_bias,
            final_gain, final_shift, pool_bias, *class_weight.T,
        ]
    )
    table = jnp.zeros((TABLE, D), BF16)
    table = lax.dynamic_update_slice(table, small, (0, me * share))
    wide = me * up_bias.shape[0]
    table = lax.dynamic_update_slice(table, up_bias[None], (UP_B + wide // D, wide % D))
    proj_up = jnp.concatenate([proj_weight[None], up_weight.reshape(share, 4, D).transpose(1, 0, 2)])
    down_pool = jnp.concatenate([down_weight, pool_weight])
    token_blocks = gather_tokens(tokens)
    if small_mesh:
        pieces = [
            lax.dynamic_slice_in_dim(matrices, (chip ^ s) * width, width, 2) for s in range(4)
        ]
        own = jnp.pad(jnp.stack(exchange(pieces)), ((0, 0), (0, 0), (0, 0), (0, PAIR * 2 - width)))
        weights = [own, swap(own, along(1))]
        come = swap(bias, along(1))
        bias = jnp.where(
            core == 0, jnp.concatenate([bias, come], axis=1), jnp.concatenate([come, bias], axis=1)
        )
        bias = jnp.pad(bias, ((0, 0), (0, PAIR * 2 - width))).astype(F32)
        early, late = Shared(proj_up, 0), Shared(down_pool, 1)
        places = jnp.stack([slot_list, early.owners(), late.owners()])
        early.near()
        late.near()
    else:
        weights = [lax.all_gather(matrices, "seq", axis=1, tiled=True)[None]]
        table = sum_seq(table).astype(F32)
        bias = table[:2]
        blocks = [lax.all_gather(proj_up, "seq", axis=1, tiled=True)]
        whole = lax.all_gather(down_pool, "seq", axis=0)
        down_blocks = [
            jnp.concatenate([whole[:, : 4 * share].reshape(FF, D), whole[:, 4 * share :].reshape(D, D)])
        ]
        places = jnp.zeros((3, 1), jnp.int32)

    query, keyval = qkv_project(places, token_blocks, weights, bias)
    if small_mesh:
        keyval = after(keyval, early.one, late.one)
        keyvals = [keyval, swap(keyval, along(1))]
        early.far()
        early.rest()
        late.far()
        table = after(table, keyval)
        come = swap(table, along(1))
    else:
        keyvals = [lax.all_gather(keyval, "seq", axis=1, tiled=True)]
    attended, total, lows = attend(query, keyvals, feature_q, feature_k, docs)
    if small_mesh:
        late.rest(lows)
        lows, table = after((lows, table), come, early.both, late.both)
        table = table + come
        lows = exchange(lows)
        table = table + swap(table, along(2))
        table = (table + swap(table, along(4))).astype(F32)
        blocks, down_blocks = early.finish(), late.finish()
    else:
        lows = exchange(lows)

    place = (starts - me * ROWS)[:, None]
    made, turned, active_t = first_part(places, blocks, lows, tokens, table)
    unit, inverse, active, slope = made
    output, lines_one, docs_out, grad_second, grad_down = head_part(
        places, down_blocks, unit, active, cotangent[0], table,
        place, doc_labels[0][:, None], class_bias.astype(F32)[None],
    )

    def both(keep, *away):
        return [keep] + [swap(a, along(1)) for a in away]

    def own_and_other(value):
        return both(value, *([value] if small_mesh else []))

    down_parts = down_gradient(both(*active_t), own_and_other(grad_down))
    if small_mesh:
        down_sum = Scatter(down_parts)
    grad_down = after(grad_down, down_parts)
    lines_two, grad_up = second_part(places, down_blocks, grad_down, slope)
    grad_second = after(grad_second, grad_up)
    made, grads = third_part(
        places, blocks, table, grad_second, grad_up, unit, inverse, slots, query.shape[-1]
    )
    lines_three, grad_first, grad_proj = made
    lines_two = lines_two + lines_three
    pack = jnp.concatenate([docs_out, lines_one, lines_two], axis=1)
    ups = own_and_other(grad_up)
    if small_mesh:
        grad_proj, grads, turned = after((grad_proj, grads, turned), down_sum.comes)
        down_sum.combine()
        down_sum.turn()
        grads = exchange(grads)
    up_parts = up_gradient(both(*turned), ups, own_and_other(grad_proj))

    back = functools.partial(
        attend_back, keyvals=keyvals, wide=attended, total=total,
        feature_q=feature_q, feature_k=feature_k, docs=docs,
    )
    if small_mesh:
        up_parts, pack, grads, down_sum.lasts = after(
            (up_parts, pack, grads, down_sum.lasts), up_parts
        )
        down_dp = SumDp(down_sum.total())
        up_sum = Scatter(up_parts)
        come = swap(pack, along(1))
        grad_q, changes = back(query, grads=grads, base=0, tiles=1, single=False)
        changes, pack, come, up_sum.seconds, down_dp.come = after(
            (changes, pack, come, up_sum.seconds, down_dp.come), grad_q, up_sum.comes
        )
        grad_qs, changes = [grad_q], both(*changes)
        up_sum.combine()
        up_sum.turn()
        down_dp.across()
        pack = pack + come
        come = swap(pack, along(2))
        rows = after(query, grad_q, up_sum.sends, down_dp.pair, pack)
        grad_q, more = back(rows, grads=grads, base=1, tiles=1, single=True)
        more, pack, come, up_sum.lasts, down_dp.cross = after(
            (more, pack, come, up_sum.lasts, down_dp.cross), grad_q
        )
        grad_qs, changes = grad_qs + [grad_q], changes + both(*more)
        up_dp = SumDp(up_sum.total())
        pack = pack + come
        come = swap(pack, along(4))
        changes = after(changes, up_dp.keep, pack)
    else:
        grad_q, changes = back(
            query, grads=grads, base=0, tiles=HEADS // 2, single=False
        )
        grad_qs = [grad_q]
        change = changes[0].transpose(1, 0, 2, 3)
        change = lax.psum_scatter(change, "seq", scatter_dimension=0, tiled=True)
        changes = [change.transpose(1, 0, 2, 3)]
        pack = sum_seq(pack)
    ends, input_grad, qkv_parts, sums = last_part(
        places, token_blocks, weights, grad_qs, changes, grad_first
    )

    if small_mesh:
        qkv_parts, ends, pack, come, up_dp.come, down_dp.cross = after(
            (qkv_parts, ends, pack, come, up_dp.come, down_dp.cross), input_grad
        )
        keep, away = both(*qkv_parts)
        ends = ends + swap(ends, along(1))
        rows_sum = Scatter((*sums, input_grad))
        up_dp.across()
        away, pack, come, down_dp.cross = after((away, pack, come, down_dp.cross), away)
        pieces = [add(keep[s], away[s])[..., :width].astype(BF16) for s in range(4)]
        pieces = exchange(pieces)
        down_wgrad = down_dp.back()
        pieces, pack, come, rows_sum.comes, up_dp.cross = after(
            (pieces, pack, come, rows_sum.comes, up_dp.cross), pieces
        )
        qkv_wgrad = jnp.concatenate(by_chip(pieces), axis=2).reshape(3 * share, D)
        ends = jnp.pad(
            lax.dynamic_slice_in_dim(ends[:2], core * share, share, 1),
            ((0, 30), (0, D - share)),
        )
        qkv_dp = SumDp(jnp.concatenate([qkv_wgrad.astype(F32), ends]))
        rows_sum.combine()
        rows_sum.turn()
        pack = pack + come
        qkv_dp.come, up_dp.cross, pack = after((qkv_dp.come, up_dp.cross, pack), qkv_dp.come)
        qkv_dp.across()
        up_wgrad = up_dp.back()
        input_grad = rows_sum.total()
        qkv_wgrad = qkv_dp.back()
    else:
        qkv_wgrad = whole_scatter(qkv_parts[0].reshape(1, 3 * D, D), 3)
        ends = lax.dynamic_slice_in_dim(sum_seq(ends)[:2], me * share, share, 1)
        qkv_wgrad = sum_dp(jnp.concatenate([qkv_wgrad, jnp.pad(ends, ((0, 30), (0, D - share)))]))
        down_wgrad = sum_dp(whole_scatter(down_parts[0], 1))
        up_wgrad = sum_dp(whole_scatter(up_parts[0], 5))
    proj_wgrad = up_wgrad[4 * share :]
    up_wgrad = up_wgrad[: 4 * share].reshape(4, share, D).transpose(1, 0, 2).reshape(share, FF)
    ends = qkv_wgrad[3 * share : 3 * share + 2, :share]
    qkv_wgrad = qkv_wgrad[: 3 * share].reshape(3, share, D)
    logits = pack[:, 3 * D + CLASSES : 3 * D + 2 * CLASSES]
    every_doc = stack_dp(pack)
    lines = jnp.sum(every_doc[:, 3 * D + 128 :].reshape(-1, docs, 2, D), axis=0)
    lines = jnp.concatenate([lines[:, 0], lines[:, 1]])
    at = me * share

    def my_share(vector):
        return lax.dynamic_slice_in_dim(vector, at, share, 0)

    first_all, pooled_all = (
        lax.dynamic_slice_in_dim(every_doc, k * D + at, share, 1) for k in range(2)
    )
    pre_all = every_doc[:, 2 * D : 3 * D]
    logit_all = every_doc[:, 3 * D : 3 * D + CLASSES]
    exact = functools.partial(jnp.dot, precision=lax.Precision.HIGHEST)
    return (
        output[None],
        logits[None],
        input_grad[None],
        qkv_wgrad[0],
        ends[0],
        qkv_wgrad[1],
        qkv_wgrad[2],
        ends[1],
        proj_wgrad,
        my_share(lines[14]),
        my_share(lines[12]),
        my_share(lines[13]),
        up_wgrad,
        lax.dynamic_slice_in_dim(lines[8:12].reshape(-1), wide, up_bias.shape[0], 0),
        down_wgrad,
        my_share(lines[0]),
        my_share(lines[1]),
        my_share(lines[2]),
        exact(first_all.T, pre_all),
        my_share(jnp.sum(pre_all, axis=0)),
        exact(pooled_all.T, logit_all),
        jnp.sum(logit_all, axis=0),
    )


def solution(mesh):
    rows, row, part = P("dp", "seq", None), P("seq", None), P("seq")
    per_sequence = P("dp", None)
    in_specs = (
        rows, rows, per_sequence, per_sequence, row, part, row, row, part, row, part, part,
        part, row, part, row, part, part, part, row, part, row, P(),
    )
    out_specs = (
        rows, P("dp", None, None), rows, row, part, row, row, part, row, part, part, part,
        row, part, row, part, part, part, row, part, row, P(),
    )
    return jax.shard_map(
        on_device, mesh=mesh, in_specs=in_specs, out_specs=out_specs, check_vma=False
    )
```

```python
import functools

import jax
import jax.numpy as jnp
from jax import lax
from jax.experimental import pallas as pl
from jax.experimental.pallas import tpu as pltpu
from jax.sharding import PartitionSpec as P

D = 768
HEADS = 12
HEAD_DIM = 64
FF = 3072
CLASSES = 3
PAIR = 2 * HEAD_DIM
ROWS = 256
EPSILON = 1e-06
FAR = -1e30
LIMIT = 56 * 1024 * 1024
F32, BF16 = jnp.float32, jnp.bfloat16

QUERY_B, VALUE_B, PROJ_B, NORM_G, NORM_S, DOWN_B, FINAL_G, FINAL_S, POOL_B, CLASS_W, UP_B = (
    0, 1, 2, 3, 4, 5, 6, 7, 8, 9, 12,
)
TABLE = 16


def swap(value, partner):
    dp, seq = lax.axis_size("dp"), lax.axis_size("seq")
    pairs = []
    for z in range(dp):
        for i in range(seq):
            to_z, to_i = partner(z, i)
            pairs.append((z * seq + i, to_z * seq + to_i))
    return lax.ppermute(value, ("dp", "seq"), pairs)


def along(bit):
    return lambda z, i: (z, i ^ bit)


def is_small():
    return lax.axis_size("seq") == 8 and lax.axis_size("dp") == 4


class Shared:
    def __init__(self, shard, role):
        self.shard, self.role = shard, role

    def near(self):
        role = self.role
        self.one = swap(self.shard, lambda z, i: (z, i ^ (2 if (z + role) % 2 == 0 else 4)))

    def far(self):
        role = self.role
        self.both = swap(self.one, lambda z, i: (z, i ^ (4 if (z + role) % 2 == 0 else 2)))
        self.blocks = [self.shard, self.one]
        self.crossed = [swap(block, along(1)) for block in self.blocks]

    def rest(self, *earlier):
        self.other = swap(after(self.one, *earlier), lambda z, i: (z ^ 1, i))

    def finish(self):
        late = [self.both, self.other]
        return self.blocks + late + self.crossed + [swap(block, along(1)) for block in late]

    def owners(self):
        me, z = lax.axis_index("seq"), lax.axis_index("dp")
        near = jnp.where((z + self.role) % 2 == 0, 2, 4)
        owners = [me, me ^ near, me ^ 6, me ^ (6 - near)]
        owners = [owners[k] for k in (0, 1, 2, 3)] + [owners[k] ^ 1 for k in (0, 1, 2, 3)]
        return jnp.stack(owners)


def gather_tokens(tokens):
    if not is_small():
        return [tokens]
    far = swap(tokens, along(6))
    return [tokens, swap(tokens, along(2)), swap(tokens, along(4)), far]


def exchange(pieces):
    return [pieces[0]] + [swap(pieces[s], along(2 * s)) for s in range(1, len(pieces))]


def slot_owners():
    if not is_small():
        return jnp.arange(lax.axis_size("seq"), dtype=jnp.int32)
    return lax.axis_index("seq") ^ jnp.array([0, 2, 4, 6, 1, 3, 5, 7], jnp.int32)


def add(*terms):
    return functools.reduce(jnp.add, [term.astype(F32) for term in terms])


class Scatter:
    def __init__(self, parts):
        self.firsts, self.seconds, self.own = parts[0:2], parts[2:4], parts[4]
        self.comes = [swap(a, along(bit)) for a, bit in zip(self.firsts, (2, 4))]

    def combine(self, *earlier):
        seconds = after(self.seconds, *earlier)
        self.sends = [add(a, come[1]).astype(BF16) for a, come in zip(seconds, self.comes)]

    def turn(self):
        self.lasts = [swap(a, along(bit)) for a, bit in zip(self.sends, (4, 2))]

    def total(self):
        half = self.own.shape[0] // 2
        owns = (self.own[:half], self.own[half:])
        return jnp.concatenate(
            [add(own, come[0], last) for own, come, last in zip(owns, self.comes, self.lasts)]
        )


def after(values, *others):
    return lax.optimization_barrier((values, others))[0]


class SumDp:
    def __init__(self, shard):
        z = lax.axis_index("dp")
        half = shard.shape[0] // 2
        self.low = jnp.logical_or(z == 0, z == 3)
        first, second = shard[:half], shard[half:]
        self.keep = jnp.where(self.low, first, second)
        self.come = swap(
            jnp.where(self.low, second, first).astype(BF16), lambda z, i: (z ^ 1, i)
        )

    def across(self):
        self.pair = add(self.keep, self.come).astype(BF16)
        self.cross = swap(self.pair, lambda z, i: (z ^ 3, i))

    def finish(self):
        self.whole = add(self.pair, self.cross).astype(BF16)
        self.last = swap(self.whole, lambda z, i: (z ^ 1, i))

    def back(self):
        total, come = self.whole, self.last
        low = self.low
        return jnp.concatenate(
            [jnp.where(low, total, come), jnp.where(low, come, total)], axis=0
        ).astype(F32)


def sum_dp(shard):
    if not is_small():
        return lax.psum(shard.astype(BF16), "dp").astype(F32)
    total = SumDp(shard)
    total.across()
    total.finish()
    return total.back()


def sum_seq(value):
    if not is_small():
        return lax.psum(value, "seq")
    for bit in (1, 2, 4):
        value = value + swap(value, along(bit))
    return value


def sum_all(value):
    value = sum_seq(value)
    if not is_small():
        return lax.psum(value, "dp")
    for bit in (1, 2):
        value = value + swap(value, lambda z, i: (z ^ bit, i))
    return value


def stack_dp(value):
    if not is_small():
        return lax.all_gather(value, "dp", axis=0, tiled=True)
    for bit in (1, 2):
        value = jnp.concatenate([value, swap(value, lambda z, i: (z ^ bit, i))], axis=0)
    return value


def dot(left, right, contract=((1,), (0,))):
    return lax.dot_general(left, right, (contract, ((), ())), preferred_element_type=F32)


def call(body, name, micros, **kwargs):
    return pl.pallas_call(
        body,
        name=name,
        cost_estimate=pl.CostEstimate(
            flops=int(micros * 1.1e9), transcendentals=0, bytes_accessed=int(micros * 1e6)
        ),
        compiler_params=pltpu.CompilerParams(vmem_limit_bytes=LIMIT),
        **kwargs,
    )


VMEM = pl.BlockSpec(memory_space=pltpu.VMEM)
ANY = pl.BlockSpec(memory_space=pl.ANY)
SMEM = pl.BlockSpec(memory_space=pltpu.SMEM)


def start(copies):
    for copy in copies:
        copy.start()
    return copies


def wait(copies):
    for copy in copies:
        copy.wait()


def block_copies(places, line, refs, target, sems, part=None):
    copies = []
    for slot, ref in enumerate(refs):
        source = ref if part is None else ref.at[part]
        rows = source.shape[-2]
        first = pl.multiple_of(places[line, slot] * rows, rows)
        if len(source.shape) == 3:
            place = target.at[:, pl.ds(first, rows), :]
        else:
            place = target.at[pl.ds(first, rows), :]
        copies.append(pltpu.make_async_copy(source, place, sems.at[slot]))
    return start(copies)


def weight_refs(weights):
    return [ref.at[s] for ref in weights for s in range(ref.shape[0])]


def qkv_kernel(blocks, sides, places, *refs):
    tokens, refs = refs[:blocks], refs[blocks:]
    weights, (bias, query, keyval, turned, held, sems) = refs[:sides], refs[sides:]
    wait(block_copies(places, 0, weight_refs(weights), held, sems))
    for s in range(query.shape[0]):
        rows = tokens[s][...]
        keyval[0, s] = dot(rows, held[1]).astype(BF16)
        keyval[1, s] = (dot(rows, held[2]) + bias[1:2]).astype(BF16)
        query[s] = (dot(rows, held[0]) + bias[0:1]).astype(BF16)
        turned[:, s * ROWS : (s + 1) * ROWS] = rows.astype(F32).T.astype(BF16)


def qkv_project(places, tokens, weights, bias):
    slots = len(tokens)
    lanes = weights[0].shape[-1]
    out = jax.ShapeDtypeStruct((slots, ROWS, lanes), BF16)
    pair = jax.ShapeDtypeStruct((2, slots, ROWS, lanes), BF16)
    return call(
        functools.partial(qkv_kernel, len(tokens), len(weights)),
        "qkv",
        5,
        out_shape=(out, pair, jax.ShapeDtypeStruct((D, slots * ROWS), BF16)),
        in_specs=[SMEM] + [VMEM] * len(tokens) + [ANY] * len(weights) + [VMEM],
        out_specs=(VMEM,) * 3,
        scratch_shapes=[
            pltpu.VMEM((3, D, lanes), BF16),
            pltpu.SemaphoreType.DMA((len(weights) * weights[0].shape[0],)),
        ],
    )(places, *tokens, *weights, bias)


def left_half(shape):
    return lax.broadcasted_iota(jnp.int32, shape, len(shape) - 1) < HEAD_DIM


def split3(value):
    high = value.astype(BF16).astype(F32)
    middle = (value - high).astype(BF16).astype(F32)
    low = (value - high - middle).astype(BF16).astype(F32)
    return high, middle, low


def spread3(value, docs, shape):
    lane = lax.broadcasted_iota(jnp.int32, shape, 1) % HEAD_DIM
    high, middle, low = split3(value)
    return jnp.where(
        lane == docs, high, jnp.where(lane == docs + 1, middle, jnp.where(lane == docs + 2, low, 0.0))
    )


def chunks_of(refs):
    number = 0
    for ref in refs:
        for index in range(ref.shape[1]):
            yield ref, index, number
            number += 1


def over_chunks(refs, step):
    if len(refs) > 1:
        for at in chunks_of(refs):
            step(*at)
    else:
        pl.loop(0, refs[0].shape[1])(lambda index: step(refs[0], index, index))


def attend_kernel(sides, docs, odd, *refs):
    query, feature_q, feature_k = refs[:3]
    keyvals = refs[3 : 3 + sides]
    slots = feature_q.shape[0]
    rest = refs[3 + sides :]
    wide, total, lows, (scores, acc, most) = rest[0], rest[1], rest[2:-3], rest[-3:]
    tile, slot = pl.program_id(0), pl.program_id(1)
    left = left_half((ROWS, PAIR))
    rows = query[0] * 0.125
    spare = feature_q[slot]

    def one_head(head):
        mine = left if head == 0 else jnp.logical_not(left)
        aug = jnp.where(mine, rows, spare)
        most[...] = jnp.full_like(most, FAR)

        def score_step(ref, index, number):
            full = jnp.where(mine, ref[0, index], feature_k[number])
            made = dot(aug, full, ((1,), (1,)))
            scores[number] = made
            most[...] = jnp.maximum(most[...], jnp.maximum(made[:, :PAIR], made[:, PAIR:]))

        over_chunks(keyvals, score_step)
        top = jnp.max(most[...], axis=1, keepdims=True)
        acc[...] = jnp.zeros_like(acc)

        def value_step(ref, index, number):
            full = jnp.where(mine, ref[1, index], feature_k[number])
            acc[...] += dot(jnp.exp(scores[number] - top).astype(BF16), full)

        over_chunks(keyvals, value_step)
        found = acc[...]
        lane = docs + (HEAD_DIM if head == 0 else 0)
        weight = found[:, lane : lane + 1]
        return found / weight, top + jnp.log(weight)

    result, sums = one_head(0)
    wide[0] = result
    total[0] = jnp.broadcast_to(sums, (ROWS, PAIR))

    def second_head():
        result, sums = one_head(1)
        wide[0] = jnp.where(left, wide[0], result)
        total[0] = jnp.where(left, total[0], sums)

    if odd:
        pl.when(tile < pl.num_programs(0) - 1)(second_head)
    else:
        second_head()
    for s in range(slots):

        @pl.when(slot == s)
        def _(s=s):
            lows[s][...] = wide[0].astype(BF16)


def slot_spec(array, base=0):
    return pl.BlockSpec((1, ROWS, PAIR), lambda tile, slot: (slot, 0, tile + base))


def tile_spec(array, base=0):
    lead = array.shape[:-1]
    return pl.BlockSpec(lead + (PAIR,), lambda tile, slot: (0,) * len(lead) + (tile + base,))


def fixed_spec(array):
    return pl.BlockSpec(array.shape, lambda tile, slot: (0,) * array.ndim)


def attend(query, keyvals, feature_q, feature_k, docs):
    slots, tiles = query.shape[0], query.shape[-1] // PAIR
    wide = jax.ShapeDtypeStruct(query.shape, F32)
    low = jax.ShapeDtypeStruct(wide.shape[1:], BF16)
    chunks = feature_k.shape[0]
    made = call(
        functools.partial(attend_kernel, len(keyvals), docs, slots > 1),
        "attend",
        15,
        grid=(tiles, slots),
        out_shape=(wide, wide) + (low,) * slots,
        in_specs=[slot_spec(query), fixed_spec(feature_q), fixed_spec(feature_k)]
        + [tile_spec(a) for a in keyvals],
        out_specs=(slot_spec(wide),) * 2 + (tile_spec(low),) * slots,
        scratch_shapes=[
            pltpu.VMEM((chunks, ROWS, ROWS), F32),
            pltpu.VMEM((ROWS, PAIR), F32),
            pltpu.VMEM((ROWS, PAIR), F32),
        ],
    )(query, feature_q, feature_k, *keyvals)
    return made[0], made[1], list(made[2:])


def attend_back_kernel(sides, docs, single, *refs):
    query, wide, total, feature_q, feature_k = refs[:5]
    slots = feature_q.shape[0]
    grads_in, keyvals = refs[5 : 5 + slots], refs[5 + slots : 5 + slots + sides]
    rest = refs[5 + slots + sides :]
    grad_q, outs, (grad, acc_q, acc_k, acc_v) = rest[0], rest[1 : 1 + sides], rest[1 + sides :]
    slot = pl.program_id(1)
    left = left_half((ROWS, PAIR))
    for s in range(slots):

        @pl.when(slot == s)
        def _(s=s):
            grad[...] = grads_in[s][...]

    @pl.when(slot == 0)
    def _():
        acc_k[...] = jnp.zeros_like(acc_k)
        acc_v[...] = jnp.zeros_like(acc_v)

    rows = query[0] * 0.125
    grads = grad[...]
    product = grads.astype(F32) * wide[0]
    spare = feature_q[slot].astype(F32)
    zero = jnp.zeros_like(rows)
    acc_q[...] = jnp.zeros_like(acc_q)

    def one_head(head):
        mine = left if head == 0 else jnp.logical_not(left)
        at = head * HEAD_DIM
        delta = jnp.sum(jnp.where(mine, product, 0.0), axis=1, keepdims=True)
        sums = total[0, :, at : at + 1]
        query_t = jnp.where(
            mine, rows.astype(F32), spare + spread3(-sums, docs, (ROWS, PAIR))
        ).T.astype(BF16)
        grad_t = jnp.where(
            mine, grads.astype(F32), spread3(-delta, docs, (ROWS, PAIR))
        ).T.astype(BF16)
        query_own, grad_own = jnp.where(mine, rows, zero), jnp.where(mine, grads, zero)

        def step(ref, index, number):
            key, value, feature = ref[0, index], ref[1, index], feature_k[number]
            soft = jnp.exp(dot(jnp.where(mine, key, feature), query_t))
            change = dot(jnp.where(mine, value, feature), grad_t)
            slope = (soft * change).astype(BF16)
            acc_v[number] += dot(soft.astype(BF16), grad_own)
            acc_k[number] += dot(slope, query_own)
            key_t = key.astype(F32).T[at : at + HEAD_DIM].astype(BF16)
            acc_q[at : at + HEAD_DIM] += dot(key_t, slope)

        over_chunks(keyvals, step)

    one_head(0)
    if not single:
        one_head(1)
    grad_q[0] = (acc_q[...].T * 0.125).astype(BF16)

    @pl.when(slot == slots - 1)
    def _():
        number = 0
        for out in outs:
            count = out.shape[1]
            out[0] = acc_k[number : number + count].astype(BF16)
            out[1] = acc_v[number : number + count].astype(BF16)
            number += count


def attend_back(query, keyvals, grads, wide, total, feature_q, feature_k, docs, base, tiles, single):
    slots = query.shape[0]
    chunks = feature_k.shape[0]
    outs = tuple(
        jax.ShapeDtypeStruct(a.shape[:-1] + (tiles * PAIR,), BF16) for a in (query, *keyvals)
    )
    made = call(
        functools.partial(attend_back_kernel, len(keyvals), docs, single),
        "attend_back",
        10 if single else 21,
        grid=(tiles, slots),
        out_shape=outs,
        in_specs=[slot_spec(a, base) for a in (query, wide, total)]
        + [fixed_spec(feature_q), fixed_spec(feature_k)]
        + [tile_spec(a, base) for a in (*grads, *keyvals)],
        out_specs=(slot_spec(outs[0]),) + tuple(tile_spec(a) for a in outs[1:]),
        scratch_shapes=[
            pltpu.VMEM((ROWS, PAIR), BF16),
            pltpu.VMEM((PAIR, ROWS), F32),
            pltpu.VMEM((chunks, ROWS, PAIR), F32),
            pltpu.VMEM((chunks, ROWS, PAIR), F32),
        ],
    )(query, wide, total, feature_q, feature_k, *grads, *keyvals)
    return made[0], list(made[1:])


def normalise(value):
    centred = value - jnp.mean(value, axis=-1, keepdims=True)
    inverse = lax.rsqrt(jnp.mean(centred * centred, axis=-1, keepdims=True) + EPSILON)
    return centred * inverse, inverse


def norm_back(grad, gain, unit, inverse):
    scaled = grad * gain
    return inverse * (
        scaled
        - jnp.mean(scaled, axis=-1, keepdims=True)
        - unit * jnp.mean(scaled * unit, axis=-1, keepdims=True)
    )


def erf(value):
    value = jnp.clip(value, -3.7439211627767994, 3.7439211627767994)
    square = value * value
    top = 0.00022905065861350646
    for factor in (0.0034082910107109506, 0.050955695062380861, 0.18520832239976145, 1.128379143519084):
        top = top * square + factor
    bottom = -1.1791602954361697e-7
    for factor in (
        0.000023547966471313185, 0.0010179625278914885, 0.014070470171167667,
        0.11098505178285362, 0.49746925110067538, 1.0,
    ):
        bottom = bottom * square + factor
    return value * top / bottom


def column_sum(value):
    return jnp.sum(value, axis=0, keepdims=True)


def early_copies(places, blocks, weights, sems):
    if len(blocks) == 1:
        return block_copies(places, 1, blocks, weights, sems)
    copies = []
    rows = D // len(blocks)
    for slot, ref in enumerate(blocks):
        first = pl.multiple_of(places[1, slot] * rows, rows)
        for piece in range(5):
            copies.append(
                pltpu.make_async_copy(
                    ref.at[piece * rows : (piece + 1) * rows],
                    weights.at[piece, pl.ds(first, rows), :],
                    sems.at[5 * slot + piece],
                )
            )
    return start(copies)


def fill_table(places, smalls, table):
    count, share = smalls.shape[0], D // smalls.shape[0]
    line = lax.broadcasted_iota(jnp.int32, (PAIR, D), 0)
    lane = lax.broadcasted_iota(jnp.int32, (PAIR, D), 1)
    made = 0.0
    for slot in range(count):
        spread = jnp.where(jnp.logical_and(lane == line + places[1, slot] * share, line < share), 1.0, 0.0)
        made = made + dot(smalls[slot, :, :PAIR], spread.astype(BF16))
    table[0:UP_B] = made[0:UP_B]
    for slot in range(count):
        at = places[1, slot]
        table[pl.ds(UP_B + at // 2, 1), pl.ds(pl.multiple_of(at % 2 * 4 * share, 4 * share), 4 * share)] = (
            smalls[slot, UP_B : UP_B + 1, : 4 * share].astype(F32)
        )


def first_kernel(count, slots, groups, places, *refs):
    blocks, refs = refs[:count], refs[count:]
    attended, refs = refs[: slots * groups], refs[slots * groups :]
    tokens, given = refs[:2]
    table, unit, inverse, active, slope, sides = *refs[2:7], refs[7:-5]
    weights, turned, smalls, sems, small_sems = refs[-5:]
    copies = early_copies(places, blocks, weights, sems)
    if count > 1:
        more = start(
            [
                pltpu.make_async_copy(ref.at[5 * D // count :], smalls.at[slot], small_sems.at[slot])
                for slot, ref in enumerate(blocks)
            ]
        )
    width = D // slots

    def row(at):
        return table[at : at + 1]

    core = places[0, 0] % 2 if slots > 1 else 0
    per = width // 2 if slots > 1 else width
    rows_of = [
        jnp.concatenate([a[...] for a in attended[s * groups : (s + 1) * groups]], axis=1)
        for s in range(slots)
    ]
    far = 4 * FF // 8

    for s in range(slots):
        turned[0 : rows_of[s].shape[1]] = rows_of[s].astype(F32).T.astype(BF16)
        if slots > 1:
            first = far + (slots + s) * per
            sides[0][first : first + per] = turned[pl.ds(pl.multiple_of(core * per, per), per)]
            sides[1][first : first + per] = turned[pl.ds(pl.multiple_of((1 - core) * per, per), per)]
        else:
            sides[0][FF + D :] = turned[...]
    if count > 1:
        wait(more)
        fill_table(places, smalls, table)
    else:
        table[...] = given[...]
    wait(copies)
    residual = tokens[...].astype(F32) + row(PROJ_B)
    for s in range(slots):
        first = pl.multiple_of((places[0, s] // 2) * width, width)
        residual = residual + dot(rows_of[s][:, :width], weights[0, pl.ds(first, width), :])
    first_unit, first_inverse = normalise(residual)
    unit[...] = first_unit
    inverse[...] = first_inverse
    normed = first_unit * row(NORM_G) + row(NORM_S)
    normed_low = normed.astype(BF16)
    turned[...] = normed.T.astype(BF16)
    for side, target in enumerate(sides):
        if slots == 1:
            target[FF : FF + D] = turned[...]
            continue
        for s in range(slots):
            first = pl.multiple_of(places[0, side * slots + s] * per, per)
            target[far + s * per : far + (s + 1) * per] = turned[pl.ds(first, per)]
    step = 384
    for at in range(0, FF, step):
        line, col = at // D, at % D
        upward = (
            dot(normed_low, weights[1 + line, :, col : col + step])
            + table[UP_B + line : UP_B + line + 1, col : col + step]
        )
        share = 0.5 + 0.5 * erf(upward * 0.7071067811865476)
        bell = jnp.exp(upward * upward * -0.5) * 0.3989422804014327
        active[:, at : at + step] = (upward * share).astype(BF16)
        slope[:, at : at + step] = share + upward * bell
    for side, target in enumerate(sides):
        if slots == 1:
            for at in range(0, FF, D):
                target[at : at + D] = active[:, at : at + D].astype(F32).T.astype(BF16)
            continue
        rows = FF // 8
        for s in range(slots):
            first = pl.multiple_of(places[0, side * slots + s] * rows, rows)
            target[s * rows : (s + 1) * rows] = active[:, pl.ds(first, rows)].astype(F32).T.astype(BF16)


def first_part(places, blocks, attended, tokens, table):
    count = len(blocks)
    slots = 4 if count > 1 else 1
    groups = len(attended) // slots
    shape = jax.ShapeDtypeStruct
    sides = 2 if slots > 1 else 1
    outs = (
        shape((TABLE, D), F32), shape((ROWS, D), F32), shape((ROWS, 1), F32),
        shape((ROWS, FF), BF16), shape((ROWS, FF), F32),
    )
    outs += (shape(((FF + 2 * D) // sides, ROWS), BF16),) * sides
    made = call(
        functools.partial(first_kernel, count, slots, groups),
        "forward_up",
        11,
        out_shape=outs,
        in_specs=[SMEM] + [ANY] * count + [VMEM] * (slots * groups + 2),
        out_specs=(VMEM,) * len(outs),
        scratch_shapes=[
            pltpu.VMEM((5, D, D), BF16),
            pltpu.VMEM((D, ROWS), BF16),
            pltpu.VMEM((count, TABLE, D), BF16),
            pltpu.SemaphoreType.DMA((5 * count,)),
            pltpu.SemaphoreType.DMA((count,)),
        ],
    )(places, *blocks, *attended, tokens, table)
    return made[:5], made[5:]


def head_kernel(count, docs, places, *refs):
    blocks, refs = refs[:count], refs[count:]
    unit, active, cotangent, table, place, labels, class_b = refs[:7]
    output, lines, docs_out, grad_second, grad_out = refs[7:12]
    pool, down, sems = refs[12:]
    down_copies = block_copies(places, 2, blocks, down, sems.at[1], slice(0, FF // count))
    pool_copies = block_copies(places, 2, blocks, pool, sems.at[0], slice(FF // count, (FF + D) // count))

    def row(at):
        return table[at : at + 1]

    normed = unit[...] * row(NORM_G) + row(NORM_S)
    wait(down_copies)
    residual = normed + dot(active[...], down[...]) + row(DOWN_B)
    last_unit, last_inverse = normalise(residual)
    outcome = last_unit * row(FINAL_G) + row(FINAL_S)
    out_low = outcome.astype(BF16)
    output[...] = out_low

    at_row = place[...]
    here = jnp.logical_and(at_row >= 0, at_row < ROWS)
    pick = jnp.where(lax.broadcasted_iota(jnp.int32, (docs, ROWS), 1) == at_row, 1.0, 0.0)
    first_low = dot(pick.astype(BF16), out_low).astype(BF16)
    wait(pool_copies)
    pooled = jnp.tanh(dot(first_low, pool[...]) + row(POOL_B))
    pooled_low = pooled.astype(BF16).astype(F32)
    logits = [
        jnp.sum(pooled_low * row(CLASS_W + c), axis=1, keepdims=True) + class_b[0, c]
        for c in range(CLASSES)
    ]
    top = functools.reduce(jnp.maximum, logits)
    powers = [jnp.exp(logit - top) for logit in logits]
    whole = functools.reduce(jnp.add, powers)
    label = labels[...]
    grads = [powers[c] / whole - jnp.where(label == c, 1.0, 0.0) for c in range(CLASSES)]
    grad_pre = functools.reduce(jnp.add, [grads[c] * row(CLASS_W + c) for c in range(CLASSES)])
    grad_pre = grad_pre * (1.0 - pooled * pooled)
    parts = jnp.concatenate(split3(grad_pre), axis=0).astype(BF16)
    made = dot(parts, pool[...], ((1,), (1,)))
    grad_first = made[:docs] + made[docs : 2 * docs] + made[2 * docs :]
    parts = jnp.concatenate(split3(grad_first), axis=0).astype(BF16)
    picks = jnp.concatenate([pick] * 3, axis=0).astype(BF16)
    grad_outcome = cotangent[...] + dot(picks, parts, ((0,), (0,)))
    lane = lax.broadcasted_iota(jnp.int32, (docs, 128), 1)
    small = jnp.zeros((docs, 128), F32)
    for c in range(CLASSES):
        small = jnp.where(lane == c, grads[c], jnp.where(lane == CLASSES + c, logits[c], small))
    docs_out[...] = jnp.where(
        here,
        jnp.concatenate([first_low.astype(F32), pooled_low, grad_pre, small], axis=1),
        0.0,
    )

    grad = norm_back(grad_outcome, row(FINAL_G), last_unit, last_inverse)
    grad_second[...] = grad
    grad_out[...] = grad.astype(BF16)
    lines[0:1] = column_sum(grad)
    lines[1:2] = column_sum(grad_outcome * last_unit)
    lines[2:3] = column_sum(grad_outcome)
    lines[3:8] = jnp.zeros((5, D), F32)


def head_part(places, late, unit, active, cotangent, table, place, labels, class_b):
    count, docs = len(late), place.shape[0]
    shape = jax.ShapeDtypeStruct
    outs = (
        shape((ROWS, D), BF16),
        shape((8, D), F32),
        shape((docs, 3 * D + 128), F32),
        shape((ROWS, D), F32),
        shape((ROWS, D), BF16),
    )
    return call(
        functools.partial(head_kernel, count, docs),
        "head",
        7,
        out_shape=outs,
        in_specs=[SMEM] + [ANY] * count + [VMEM] * 6 + [SMEM],
        out_specs=(VMEM,) * len(outs),
        scratch_shapes=[
            pltpu.VMEM((D, D), BF16),
            pltpu.VMEM((FF, D), BF16),
            pltpu.SemaphoreType.DMA((2, count)),
        ],
    )(places, *late, unit, active, cotangent, table, place, labels, class_b)


def second_kernel(count, places, *refs):
    downs, (grad_down, slope, lines, grad_up, down, sems) = refs[:count], refs[count:]
    wait(block_copies(places, 2, downs, down, sems, slice(0, FF // count)))
    grad_low = grad_down[...]
    step = 384
    for at in range(0, FF, step):
        grad = dot(grad_low, down[at : at + step], ((1,), (1,))).astype(BF16).astype(F32)
        grad = grad * slope[:, at : at + step]
        line, col = at // D, at % D
        lines[line : line + 1, col : col + step] = column_sum(grad)
        grad_up[line, :, col : col + step] = grad.astype(BF16)
    lines[4:8] = jnp.zeros((4, D), F32)


def second_part(places, late, grad_down, slope):
    count, shape = len(late), jax.ShapeDtypeStruct
    outs = (shape((8, D), F32), shape((4, ROWS, D), BF16))
    return call(
        functools.partial(second_kernel, count),
        "backward_down",
        5,
        out_shape=outs,
        in_specs=[SMEM] + [ANY] * count + [VMEM] * 2,
        out_specs=(VMEM,) * 2,
        scratch_shapes=[pltpu.VMEM((FF, D), BF16), pltpu.SemaphoreType.DMA((count,))],
    )(places, *late, grad_down, slope)


def third_kernel(count, slots, places, *refs):
    blocks, refs = refs[:count], refs[count:]
    table, grad_second, grad_up, unit, inverse = refs[:5]
    lines, grad_first, grad_out = refs[5:8]
    grad_attended = refs[8 : 8 + slots]
    weights, sems = refs[8 + slots :]
    wait(early_copies(places, blocks, weights, sems))
    width = D // slots

    def row(at):
        return table[at : at + 1]

    back = dot(grad_up[0], weights[1], ((1,), (1,)))
    for line in range(1, 4):
        back = back + dot(grad_up[line], weights[1 + line], ((1,), (1,)))
    grad_normed = grad_second[...] + back.astype(BF16).astype(F32)
    lines[0:4] = jnp.zeros((4, D), F32)
    lines[4:5] = column_sum(grad_normed * unit[...])
    lines[5:6] = column_sum(grad_normed)
    grad = norm_back(grad_normed, row(NORM_G), unit[...], inverse[...])
    grad_first[...] = grad
    lines[6:7] = column_sum(grad)
    lines[7:8] = jnp.zeros((1, D), F32)
    grad_low = grad.astype(BF16)
    grad_out[...] = grad_low
    for s in range(slots):
        first = pl.multiple_of((places[0, s] // 2) * width, width)
        made = dot(grad_low, weights[0, pl.ds(first, width), :], ((1,), (1,))).astype(BF16)
        if width < grad_attended[s].shape[1]:
            grad_attended[s][:, PAIR:] = jnp.zeros((ROWS, PAIR), BF16)
        grad_attended[s][:, :width] = made


def third_part(places, blocks, table, grad_second, grad_up, unit, inverse, slots, lanes):
    count = len(blocks)
    shape = jax.ShapeDtypeStruct
    outs = (shape((8, D), F32), shape((ROWS, D), F32), shape((ROWS, D), BF16))
    outs += (shape((ROWS, lanes), BF16),) * slots
    made = call(
        functools.partial(third_kernel, count, slots),
        "backward_up",
        7,
        out_shape=outs,
        in_specs=[SMEM] + [ANY] * count + [VMEM] * 5,
        out_specs=(VMEM,) * len(outs),
        scratch_shapes=[pltpu.VMEM((5, D, D), BF16), pltpu.SemaphoreType.DMA((5 * count,))],
    )(places, *blocks, table, grad_second, grad_up, unit, inverse)
    return made[:3], list(made[3:])


def wgrad_outs(slots, rows):
    shape = jax.ShapeDtypeStruct
    if slots == 1:
        return (shape((1, rows, D), BF16),)
    half = rows // 2
    return (shape((2, half, D), BF16),) * 2 + (shape((half, D), BF16),) * 2 + (shape((rows, D), F32),)


def put_slot(outs, s, first, value):
    if len(outs) == 1:
        outs[0][0, first : first + value.shape[0]] = value.astype(BF16)
        return
    if s == 0:
        outs[4][first : first + value.shape[0]] = value
        return
    half = outs[2].shape[0]
    for k, order in enumerate(((1, 3, 2), (2, 3, 1))):
        low, high = max(first, k * half), min(first + value.shape[0], (k + 1) * half)
        if low >= high:
            continue
        rows, part = slice(low - k * half, high - k * half), value[low - first : high - first]
        if s == order[2]:
            outs[2 + k][rows] = part.astype(BF16)
        else:
            outs[k][order.index(s), rows] = part.astype(BF16)


def down_kernel(slots, sides, *refs):
    lefts, rights, outs = refs[:sides], refs[sides : 2 * sides], refs[2 * sides :]
    rows = FF // sides // slots
    step = min(rows, 384)
    for s in range(slots):
        for at in range(0, rows, step):
            first = s * rows + at
            made = dot(lefts[0][first : first + step], rights[0][...])
            for side in range(1, sides):
                made = made + dot(lefts[side][first : first + step], rights[side][...])
            put_slot(outs, s, at, made)


def down_gradient(lefts, rights, slots):
    sides = len(lefts)
    outs = wgrad_outs(slots, FF // sides // slots)
    return call(
        functools.partial(down_kernel, slots, sides),
        "down_gradient",
        3,
        out_shape=outs,
        in_specs=[VMEM] * (2 * sides),
        out_specs=(VMEM,) * len(outs),
    )(*lefts, *rights)


def up_kernel(slots, sides, *refs):
    lefts, ups, projs = (refs[k * sides : (k + 1) * sides] for k in range(3))
    outs = refs[3 * sides :]
    whole = D // sides
    rows = whole // slots
    for line in range(5):
        at = FF // sides + (0 if line < 4 else whole)
        made = 0.0
        for left, up, proj in zip(lefts, ups, projs):
            made = made + dot(left[at : at + whole], up[line] if line < 4 else proj[...])
        for s in range(slots):
            put_slot(outs, s, line * rows, made[s * rows : (s + 1) * rows])


def up_gradient(lefts, ups, projs, slots):
    sides = len(lefts)
    outs = wgrad_outs(slots, 5 * D // sides // slots)
    return call(
        functools.partial(up_kernel, slots, sides),
        "up_gradient",
        4,
        out_shape=outs,
        in_specs=[VMEM] * (3 * sides),
        out_specs=(VMEM,) * len(outs),
    )(*lefts, *ups, *projs)


def input_kernel(groups, sides, places, *refs):
    turned, refs = refs[:sides], refs[sides:]
    grad_qs, refs = refs[:groups], refs[groups:]
    changes, refs = refs[: groups * sides], refs[groups * sides :]
    lines, outs, (made, grads, sems) = refs[0], refs[1:-3], refs[-3:]
    rows = turned[0].shape[1]
    sums = [None, None, None]
    for k in range(3):
        total, line = 0.0, 0.0
        for side in range(sides if k else 1):
            lane = 0
            for group in range(groups):
                source = changes[group * sides + side].at[k - 1] if k else grad_qs[group]
                lanes = slice(lane, lane + source.shape[2])
                lane = lanes.stop
                grads[:, lanes] = source[...].reshape(rows, source.shape[2])
            total = total + dot(turned[side][...], grads[...])
            if k != 1:
                line = line + dot(jnp.ones((8, rows), BF16), grads[...])
        made[k] = total.astype(BF16)
        sums[k] = line
    lines[...] = jnp.concatenate([sums[0][:1], sums[2]], axis=0)[:8]
    sends = []
    for side, out in enumerate(outs):
        for s in range(out.shape[0]):
            count = out.shape[2]
            first = pl.multiple_of(places[0, side * out.shape[0] + s] * count, count)
            sends.append((made.at[:, pl.ds(first, count), :], out.at[s]))
    wait(start([pltpu.make_async_copy(a, b, sems.at[k]) for k, (a, b) in enumerate(sends)]))


def input_gradient(places, turned, grad_qs, changes, like):
    lanes = sum(grad.shape[2] for grad in grad_qs)
    sides, groups, shape = len(like), len(grad_qs), jax.ShapeDtypeStruct
    outs = (shape((8, lanes), F32),) + tuple(shape(a.shape, BF16) for a in like)
    made = call(
        functools.partial(input_kernel, groups, sides),
        "input_weights",
        5,
        out_shape=outs,
        in_specs=[SMEM] + [VMEM] * (sides + groups + groups * sides),
        out_specs=(VMEM,) + (ANY,) * sides,
        scratch_shapes=[
            pltpu.VMEM((3, D, lanes), BF16),
            pltpu.VMEM((turned[0].shape[1], lanes), BF16),
            pltpu.SemaphoreType.DMA((sides * like[0].shape[0],)),
        ],
    )(places, *turned, *grad_qs, *changes)
    return made[0], list(made[1:])


def last_kernel(sides, groups, parts, places, *refs):
    weights, refs = refs[:sides], refs[sides:]
    grad_qs, refs = refs[:groups], refs[groups:]
    changes, refs = refs[: groups * parts], refs[groups * parts :]
    grad_first, own, outs = *refs[:2], refs[2:-3]
    held, grads, sems = refs[-3:]
    slots = grad_qs[0].shape[0]
    copies = block_copies(places, 0, weight_refs(weights), held, sems)
    for s in range(slots):
        rows = slice(s * ROWS, (s + 1) * ROWS)
        lane = 0
        for group in range(groups):
            lanes = slice(lane, lane + grad_qs[group].shape[2])
            lane = lanes.stop
            grads[0, rows, lanes] = grad_qs[group][s]
            for k in range(2):
                total = changes[group * parts][k, s].astype(F32)
                for change in changes[group * parts + 1 : (group + 1) * parts]:
                    total = total + change[k, s].astype(F32)
                grads[1 + k, rows, lanes] = total.astype(BF16)
    wait(copies)

    def partial(s):
        rows = slice(s * ROWS, (s + 1) * ROWS)
        total = dot(grads[0, rows], held[0], ((1,), (1,)))
        for k in range(1, 3):
            total = total + dot(grads[k, rows], held[k], ((1,), (1,)))
        return total

    for s in range(1, slots):
        outs[s - 1][...] = partial(s).astype(BF16)
    own[...] = grad_first[...] + partial(0)


def last_part(places, weights, grad_qs, changes, grad_first):
    slots, lanes = grad_qs[0].shape[0], sum(grad.shape[2] for grad in grad_qs)
    groups, parts = len(grad_qs), len(changes) // len(grad_qs)
    sides, shape = len(weights), jax.ShapeDtypeStruct
    outs = (shape((ROWS, D), F32),) + (shape((ROWS, D), BF16),) * (slots - 1)
    blocks = sides * weights[0].shape[0]
    made = call(
        functools.partial(last_kernel, sides, groups, parts),
        "input_gradients",
        5,
        out_shape=outs,
        in_specs=[SMEM] + [ANY] * sides + [VMEM] * (1 + groups + len(changes)),
        out_specs=(VMEM,) * len(outs),
        scratch_shapes=[
            pltpu.VMEM((3, D, lanes), BF16),
            pltpu.VMEM((3, slots * ROWS, lanes), BF16),
            pltpu.SemaphoreType.DMA((blocks,)),
        ],
    )(places, *weights, *grad_qs, *changes, grad_first)
    return made[0], made[1:]


def whole_scatter(part, pieces):
    seq = lax.axis_size("seq")
    rows = part.shape[1] // pieces // seq
    part = part.reshape(pieces, seq, rows, D).transpose(1, 0, 2, 3)
    part = part.reshape(seq, pieces * rows, D)
    return lax.psum_scatter(part, "seq", scatter_dimension=0, tiled=True)[0].astype(F32)


def by_chip(pieces):
    me = lax.axis_index("seq")
    for bit in (1, 2):
        odd = (me & (2 * bit)) != 0
        pieces = [jnp.where(odd, pieces[s ^ bit], pieces[s]) for s in range(len(pieces))]
    return pieces


def features(positions, starts):
    docs = starts.shape[0]
    segment = jnp.sum((positions[..., None] >= starts).astype(jnp.int32), axis=-1) - 1
    lane = jnp.arange(PAIR, dtype=jnp.int32) % HEAD_DIM
    own = segment[..., None] == lane
    return own, lane, docs


def on_device(
    inputs,
    cotangent,
    doc_lengths,
    doc_labels,
    query_weight,
    query_bias,
    key_weight,
    value_weight,
    value_bias,
    proj_weight,
    proj_bias,
    norm_gain,
    norm_shift,
    up_weight,
    up_bias,
    down_weight,
    down_bias,
    final_gain,
    final_shift,
    pool_weight,
    pool_bias,
    class_weight,
    class_bias,
):
    me = lax.axis_index("seq")
    tokens = inputs[0]
    share = query_bias.shape[0]
    lengths = doc_lengths[0]
    docs = lengths.shape[0]
    order = jnp.arange(docs, dtype=jnp.int32)
    starts = jnp.sum(jnp.where(order[None, :] < order[:, None], lengths[None, :], 0), axis=1)

    small_mesh = is_small()
    slot_list = slot_owners()
    chip, core = me // 2, me % 2
    width = D // 4
    slots = 4 if small_mesh else 1
    line = jnp.arange(ROWS, dtype=jnp.int32)
    mine = slot_list[:slots] if small_mesh else me[None]
    own, lane, _ = features(mine[:, None] * ROWS + line, starts)
    feature_q = jnp.where(own, FAR, 0.0).astype(BF16)
    own, lane, _ = features(slot_list[:, None] * ROWS + line, starts)
    feature_k = jnp.where(
        lane < docs, jnp.where(own, 0.0, 1.0), jnp.where(lane < docs + 3, 1.0, 0.0)
    ).astype(BF16)

    matrices = jnp.stack([query_weight, key_weight, value_weight])
    bias = jnp.stack([query_bias, value_bias])
    small = jnp.stack(
        [
            query_bias, value_bias, proj_bias, norm_gain, norm_shift, down_bias,
            final_gain, final_shift, pool_bias, *class_weight.T,
        ]
    )
    wide = me * up_bias.shape[0]
    up_pieces = up_weight.reshape(share, 4, D).transpose(1, 0, 2)
    proj_up = jnp.concatenate([proj_weight[None], up_pieces])
    down_pool = jnp.concatenate([down_weight, pool_weight])
    token_blocks = gather_tokens(tokens)
    if small_mesh:
        pieces = [
            lax.dynamic_slice_in_dim(matrices, (chip ^ s) * width, width, 2) for s in range(4)
        ]
        own = jnp.pad(jnp.stack(exchange(pieces)), ((0, 0), (0, 0), (0, 0), (0, PAIR * 2 - width)))
        weights = [own, swap(own, along(1))]
        come = swap(bias, along(1))
        bias = jnp.where(
            core == 0, jnp.concatenate([bias, come], axis=1), jnp.concatenate([come, bias], axis=1)
        )
        bias = jnp.pad(bias, ((0, 0), (0, PAIR * 2 - width))).astype(F32)
        small = jnp.pad(small, ((0, TABLE - small.shape[0]), (0, D - share)))
        small = lax.dynamic_update_slice(small, up_bias[None], (UP_B, 0))
        early = Shared(jnp.concatenate([proj_up.reshape(5 * share, D), small]), 0)
        token_blocks = after(token_blocks, feature_q, feature_k)
        late = Shared(down_pool, 1)
        places = jnp.stack([slot_list, early.owners(), late.owners()])
        early.near()
        late.near()
        table = jnp.zeros((TABLE, D), F32)
    else:
        weights = [lax.all_gather(matrices, "seq", axis=1, tiled=True)[None]]
        table = jnp.zeros((TABLE, D), BF16)
        table = lax.dynamic_update_slice(table, small, (0, me * share))
        table = lax.dynamic_update_slice(table, up_bias[None], (UP_B + wide // D, wide % D))
        table = sum_seq(table).astype(F32)
        bias = table[:2]
        blocks = [lax.all_gather(proj_up, "seq", axis=1, tiled=True)]
        whole = lax.all_gather(down_pool, "seq", axis=0)
        whole = [whole[:, : 4 * share].reshape(FF, D), whole[:, 4 * share :].reshape(D, D)]
        late_blocks = [jnp.concatenate(whole)]
        places = jnp.zeros((3, 1), jnp.int32)

    query, keyval, tokens_t = qkv_project(places, token_blocks, weights, bias)
    if small_mesh:
        keyval = after(keyval, early.one, late.one)
        keyvals = [keyval, swap(keyval, along(1))]
        early.far()
        early.rest()
        late.far()
    else:
        keyvals = [lax.all_gather(keyval, "seq", axis=1, tiled=True)]
    attended, total, lows = attend(query, keyvals, feature_q, feature_k, docs)
    if small_mesh:
        late.rest(lows)
        lows, tokens_t, early.both, early.other, late.both = after(
            (lows, tokens_t, early.both, early.other, late.both), lows
        )
        tokens_t = [tokens_t, swap(tokens_t, along(1))]
        blocks = early.finish()
    else:
        tokens_t = [tokens_t]
    lows = exchange(lows)

    place = (starts - me * ROWS)[:, None]
    made, turned = first_part(places, blocks, lows, tokens, table)
    table, unit, inverse, active, slope = made
    if small_mesh:
        late.other, tokens_t, turned = after((late.other, tokens_t, turned), active)
        late_blocks = late.finish()
    output, lines_one, docs_out, grad_second, grad_down = head_part(
        places, late_blocks, unit, active, cotangent[0], table,
        place, doc_labels[0][:, None], class_bias.astype(F32)[None],
    )

    def both(keep, *away):
        return [keep] + [swap(a, along(1)) for a in away]

    def own_and_other(value):
        return both(value, *([value] if small_mesh else []))

    turned = both(*turned)
    down_parts = down_gradient(turned, own_and_other(grad_down), slots)
    if small_mesh:
        down_sum = Scatter(down_parts)
    grad_down = after(grad_down, down_parts)
    lines_two, grad_up = second_part(places, late_blocks, grad_down, slope)
    grad_second = after(grad_second, grad_up)
    made, grads = third_part(
        places, blocks, table, grad_second, grad_up, unit, inverse, slots, query.shape[-1]
    )
    lines_three, grad_first, grad_proj = made
    lines_two = lines_two + lines_three
    pack = jnp.concatenate([docs_out, lines_one, lines_two], axis=1)
    ups = own_and_other(grad_up)
    if small_mesh:
        grad_proj, grads = after((grad_proj, grads), down_sum.comes)
        down_sum.combine()
        down_sum.turn()
        grads = exchange(grads)
    up_parts = up_gradient(turned, ups, own_and_other(grad_proj), slots)

    back = functools.partial(
        attend_back, keyvals=keyvals,
        feature_q=feature_q, feature_k=feature_k, docs=docs,
    )
    if small_mesh:
        up_parts, pack, grads, down_sum.lasts = after(
            (up_parts, pack, grads, down_sum.lasts), up_parts
        )
        down_dp = SumDp(down_sum.total())
        up_sum = Scatter(up_parts)
        come = swap(pack, along(1))
        grad_q, changes = back(
            query, grads=grads, wide=attended, total=total, base=0, tiles=1, single=False
        )
        changes, pack, come, up_sum.seconds, down_dp.come = after(
            (changes, pack, come, up_sum.seconds, down_dp.come), grad_q, up_sum.comes
        )
        grad_qs, partial, changes = [grad_q], list(changes), both(*changes)
        up_sum.combine()
        up_sum.turn()
        down_dp.across()
        pack = pack + come
        come = swap(pack, along(2))
        rows = after(query, grad_q, up_sum.sends, down_dp.pair, pack)
        grad_q, more = back(
            rows, grads=grads, wide=attended, total=total, base=1, tiles=1, single=True
        )
        more, pack, come, up_sum.lasts, down_dp.cross = after(
            (more, pack, come, up_sum.lasts, down_dp.cross), grad_q
        )
        grad_qs, partial = grad_qs + [grad_q], partial + list(more)
        changes = changes + both(*more)
        up_dp = SumDp(up_sum.total())
        pack = pack + come
        come = swap(pack, along(4))
    else:
        grad_q, changes = back(
            query, grads=grads, wide=attended, total=total,
            base=0, tiles=HEADS // 2, single=False,
        )
        grad_qs, partial = [grad_q], changes
        change = changes[0].transpose(1, 0, 2, 3)
        change = lax.psum_scatter(change, "seq", scatter_dimension=0, tiled=True)
        changes = [change.transpose(1, 0, 2, 3)]
        partial = changes
        pack = sum_seq(pack)
    def own_shares(pack):
        at = me * share
        lines = pack[:, 3 * D + PAIR :].reshape(docs, 2, D).transpose(1, 0, 2).reshape(2 * docs, D)
        own = jnp.concatenate(
            [
                lax.dynamic_slice_in_dim(lines, at, share, 1),
                lax.dynamic_slice_in_dim(lines[8:12].reshape(-1), wide, 4 * share, 0).reshape(4, share),
                jnp.zeros((4, share), F32),
            ]
        )
        parts = [
            pack[:, 2 * D : 3 * D],
            lax.dynamic_slice_in_dim(pack, at, share, 1),
            lax.dynamic_slice_in_dim(pack, D + at, share, 1),
            pack[:, 3 * D : 3 * D + PAIR],
            own.reshape(docs, 3 * share),
        ]
        logits = pack[:, 3 * D + CLASSES : 3 * D + 2 * CLASSES]
        return jnp.concatenate(parts, axis=1), logits

    ends, qkv_parts = input_gradient(places, tokens_t, grad_qs, partial, weights)
    if small_mesh:
        qkv_parts, ends, changes, pack, come, up_dp.come = after(
            (qkv_parts, ends, changes, pack, come, up_dp.come), ends
        )
        keep, away = both(*qkv_parts)
        ends = ends + swap(ends, along(1))
        pieces = [add(keep[s], away[s])[..., :width].astype(BF16) for s in range(4)]
        pieces = exchange(pieces)
        up_dp.across()
        pack = own_shares(pack + come)
        logits = pack[1]
        come = swap(pack[0], lambda z, i: (z ^ 1, i))
        changes = after(changes, pieces[0], up_dp.pair, pack)
    input_grad, sums = last_part(places, weights, grad_qs, changes, grad_first)

    if small_mesh:
        pieces, up_dp.cross, down_dp.cross, pack, come = after(
            (pieces, up_dp.cross, down_dp.cross, pack[0], come), input_grad
        )
        qkv_wgrad = jnp.concatenate(by_chip(pieces), axis=2).reshape(3 * share, D)
        ends = jnp.pad(
            lax.dynamic_slice_in_dim(ends[:2], core * share, share, 1),
            ((0, 30), (0, D - share)),
        )
        qkv_dp = SumDp(jnp.concatenate([qkv_wgrad.astype(F32), ends]))
        pack = jnp.concatenate([pack, come], axis=0)
        come = swap(pack, lambda z, i: (z ^ 2, i))
        sums = exchange([input_grad, *sums])
        qkv_dp.come, up_dp.cross, down_dp.cross = after(
            (qkv_dp.come, up_dp.cross, down_dp.cross), qkv_dp.come
        )
        qkv_dp.across()
        up_dp.finish()
        down_dp.finish()
        every_doc = jnp.concatenate([pack, come], axis=0)
        qkv_dp.cross, sums, every_doc = after((qkv_dp.cross, sums, every_doc), qkv_dp.cross)
        qkv_dp.finish()
        down_wgrad, up_wgrad = down_dp.back(), up_dp.back()
        input_grad = add(*sums)
        qkv_wgrad = qkv_dp.back()
    else:
        qkv_wgrad = whole_scatter(qkv_parts[0].reshape(1, 3 * D, D), 3)
        ends = lax.dynamic_slice_in_dim(sum_seq(ends)[:2], me * share, share, 1)
        qkv_wgrad = sum_dp(jnp.concatenate([qkv_wgrad, jnp.pad(ends, ((0, 30), (0, D - share)))]))
        down_wgrad = sum_dp(whole_scatter(down_parts[0], 1))
        up_wgrad = sum_dp(whole_scatter(up_parts[0], 5))
    proj_wgrad = up_wgrad[4 * share :]
    up_wgrad = up_wgrad[: 4 * share].reshape(4, share, D).transpose(1, 0, 2).reshape(share, FF)
    ends = qkv_wgrad[3 * share : 3 * share + 2, :share]
    qkv_wgrad = qkv_wgrad[: 3 * share].reshape(3, share, D)
    if not small_mesh:
        pack, logits = own_shares(pack)
        every_doc = stack_dp(pack)
    pre_all, first_all, pooled_all = (
        every_doc[:, at : at + size] for at, size in ((0, D), (D, share), (D + share, share))
    )
    logit_all = every_doc[:, D + 2 * share : D + 2 * share + CLASSES]
    lines = jnp.sum(every_doc[:, D + 2 * share + PAIR :].reshape(-1, docs, 3 * share), axis=0)
    lines = lines.reshape(3 * docs, share)

    def my_share(vector):
        return lax.dynamic_slice_in_dim(vector, me * share, share, 0)

    exact = functools.partial(jnp.dot, precision=lax.Precision.HIGHEST)
    return (
        output[None],
        logits[None],
        input_grad[None],
        qkv_wgrad[0],
        ends[0],
        qkv_wgrad[1],
        qkv_wgrad[2],
        ends[1],
        proj_wgrad,
        lines[14],
        lines[12],
        lines[13],
        up_wgrad,
        lines[16:20].reshape(-1),
        down_wgrad,
        lines[0],
        lines[1],
        lines[2],
        exact(first_all.T, pre_all),
        my_share(jnp.sum(pre_all, axis=0)),
        exact(pooled_all.T, logit_all),
        jnp.sum(logit_all, axis=0),
    )


def solution(mesh):
    rows, row, part = P("dp", "seq", None), P("seq", None), P("seq")
    per_sequence = P("dp", None)
    in_specs = (
        rows, rows, per_sequence, per_sequence, row, part, row, row, part, row, part, part,
        part, row, part, row, part, part, part, row, part, row, P(),
    )
    out_specs = (
        rows, P("dp", None, None), rows, row, part, row, row, part, row, part, part, part,
        row, part, row, part, part, part, row, part, row, P(),
    )
    return jax.shard_map(
        on_device, mesh=mesh, in_specs=in_specs, out_specs=out_specs, check_vma=False
    )
```

```python
import functools

import jax
import jax.numpy as jnp
from jax import lax
from jax.experimental import pallas as pl
from jax.experimental.pallas import tpu as pltpu
from jax.sharding import PartitionSpec as P

D = 768
HEADS = 12
HEAD_DIM = 64
FF = 3072
CLASSES = 3
PAIR = 2 * HEAD_DIM
ROWS = 256
EPSILON = 1e-06
FAR = -1e30
LIMIT = 56 * 1024 * 1024
F32, BF16 = jnp.float32, jnp.bfloat16

QUERY_B, VALUE_B, PROJ_B, NORM_G, NORM_S, DOWN_B, FINAL_G, FINAL_S, POOL_B, CLASS_W, UP_B = (
    0, 1, 2, 3, 4, 5, 6, 7, 8, 9, 12,
)
TABLE = 16


def swap(value, partner):
    dp, seq = lax.axis_size("dp"), lax.axis_size("seq")
    pairs = []
    for z in range(dp):
        for i in range(seq):
            to_z, to_i = partner(z, i)
            pairs.append((z * seq + i, to_z * seq + to_i))
    return lax.ppermute(value, ("dp", "seq"), pairs)


def along(bit):
    return lambda z, i: (z, i ^ bit)


def is_small():
    return lax.axis_size("seq") == 8 and lax.axis_size("dp") == 4


class Shared:
    def __init__(self, shard, role):
        self.shard, self.role = shard, role

    def near(self):
        role = self.role
        self.one = swap(self.shard, lambda z, i: (z, i ^ (2 if (z + role) % 2 == 0 else 4)))

    def far(self):
        role = self.role
        self.both = swap(self.one, lambda z, i: (z, i ^ (4 if (z + role) % 2 == 0 else 2)))

    def cross(self):
        self.crossed = [swap(block, along(1)) for block in (self.shard, self.one)]

    def cross_both(self):
        self.middle = swap(self.both, along(1))

    def rest(self):
        self.other = swap(self.one, lambda z, i: (z ^ 1, i))

    def rest_direct(self):
        role = self.role
        self.other = swap(self.shard, lambda z, i: (z, i ^ (4 if (z + role) % 2 == 0 else 2)))

    def finish(self):
        last = swap(self.other, along(1))
        return [self.shard, self.one, self.both, self.other, *self.crossed, self.middle, last]

    def owners(self):
        me, z = lax.axis_index("seq"), lax.axis_index("dp")
        near = jnp.where((z + self.role) % 2 == 0, 2, 4)
        owners = [me, me ^ near, me ^ 6, me ^ (6 - near)]
        owners = [owners[k] for k in (0, 1, 2, 3)] + [owners[k] ^ 1 for k in (0, 1, 2, 3)]
        return jnp.stack(owners)


def gather_tokens(tokens):
    if not is_small():
        return [tokens]
    far = swap(tokens, along(6))
    return [tokens, swap(tokens, along(2)), swap(tokens, along(4)), far]


def exchange(pieces):
    return [pieces[0]] + [swap(pieces[s], along(2 * s)) for s in range(1, len(pieces))]


def slot_owners():
    if not is_small():
        return jnp.arange(lax.axis_size("seq"), dtype=jnp.int32)
    return lax.axis_index("seq") ^ jnp.array([0, 2, 4, 6, 1, 3, 5, 7], jnp.int32)


def add(*terms):
    return functools.reduce(jnp.add, [term.astype(F32) for term in terms])


class Scatter:
    def __init__(self, parts):
        self.firsts, self.seconds, self.own = parts[0:2], parts[2:4], parts[4]
        self.comes = [swap(a, along(bit)) for a, bit in zip(self.firsts, (2, 4))]

    def combine(self, *earlier):
        seconds = after(self.seconds, *earlier)
        self.sends = [add(a, come[1]).astype(BF16) for a, come in zip(seconds, self.comes)]

    def turn(self):
        self.lasts = [swap(a, along(bit)) for a, bit in zip(self.sends, (4, 2))]

    def total(self):
        half = self.own.shape[0] // 2
        owns = (self.own[:half], self.own[half:])
        return jnp.concatenate(
            [add(own, come[0], last) for own, come, last in zip(owns, self.comes, self.lasts)]
        )


def after(values, *others):
    return lax.optimization_barrier((values, others))[0]


class SumDp:
    def __init__(self, shard):
        z = lax.axis_index("dp")
        half = shard.shape[0] // 2
        self.low = jnp.logical_or(z == 0, z == 3)
        first, second = shard[:half], shard[half:]
        self.keep = jnp.where(self.low, first, second)
        self.come = swap(
            jnp.where(self.low, second, first).astype(BF16), lambda z, i: (z ^ 1, i)
        )

    def across(self):
        self.pair = add(self.keep, self.come).astype(BF16)
        self.cross = swap(self.pair, lambda z, i: (z ^ 3, i))

    def finish(self):
        self.whole = add(self.pair, self.cross).astype(BF16)
        self.last = swap(self.whole, lambda z, i: (z ^ 1, i))

    def back(self):
        total, come = self.whole, self.last
        low = self.low
        return jnp.concatenate(
            [jnp.where(low, total, come), jnp.where(low, come, total)], axis=0
        ).astype(F32)


def sum_dp(shard):
    if not is_small():
        return lax.psum(shard.astype(BF16), "dp").astype(F32)
    total = SumDp(shard)
    total.across()
    total.finish()
    return total.back()


def sum_seq(value):
    if not is_small():
        return lax.psum(value, "seq")
    for bit in (1, 2, 4):
        value = value + swap(value, along(bit))
    return value


def sum_all(value):
    value = sum_seq(value)
    if not is_small():
        return lax.psum(value, "dp")
    for bit in (1, 2):
        value = value + swap(value, lambda z, i: (z ^ bit, i))
    return value


def stack_dp(value):
    if not is_small():
        return lax.all_gather(value, "dp", axis=0, tiled=True)
    for bit in (1, 2):
        value = jnp.concatenate([value, swap(value, lambda z, i: (z ^ bit, i))], axis=0)
    return value


def dot(left, right, contract=((1,), (0,))):
    return lax.dot_general(left, right, (contract, ((), ())), preferred_element_type=F32)


def call(body, name, micros, **kwargs):
    return pl.pallas_call(
        body,
        name=name,
        cost_estimate=pl.CostEstimate(
            flops=int(micros * 1.1e9), transcendentals=0, bytes_accessed=int(micros * 1e6)
        ),
        compiler_params=pltpu.CompilerParams(vmem_limit_bytes=LIMIT),
        **kwargs,
    )


VMEM = pl.BlockSpec(memory_space=pltpu.VMEM)
ANY = pl.BlockSpec(memory_space=pl.ANY)
SMEM = pl.BlockSpec(memory_space=pltpu.SMEM)


def start(copies):
    for copy in copies:
        copy.start()
    return copies


def wait(copies):
    for copy in copies:
        copy.wait()


def like(arrays):
    return [pltpu.VMEM(a.shape, a.dtype) for a in arrays]


def block_copies(places, line, refs, target, sems, part=None):
    copies = []
    for slot, ref in enumerate(refs):
        source = ref if part is None else ref.at[part]
        rows = source.shape[-2]
        first = pl.multiple_of(places[line, slot] * rows, rows)
        if len(source.shape) == 3:
            place = target.at[:, pl.ds(first, rows), :]
        else:
            place = target.at[pl.ds(first, rows), :]
        copies.append(pltpu.make_async_copy(source, place, sems.at[slot]))
    return start(copies)


def weight_refs(weights):
    return [ref.at[s] for ref in weights for s in range(ref.shape[0])]


def qkv_kernel(blocks, sides, places, *refs):
    tokens, refs = refs[:blocks], refs[blocks:]
    weights, (bias, query, keyval, held, sems) = refs[:sides], refs[sides:]
    wait(block_copies(places, 0, weight_refs(weights), held, sems))
    for s in range(query.shape[0]):
        rows = tokens[s][...]
        keyval[0, s] = dot(rows, held[1]).astype(BF16)
        keyval[1, s] = (dot(rows, held[2]) + bias[1:2]).astype(BF16)
        query[s] = (dot(rows, held[0]) + bias[0:1]).astype(BF16)


def qkv_project(places, tokens, weights, bias):
    slots = len(tokens)
    lanes = weights[0].shape[-1]
    out = jax.ShapeDtypeStruct((slots, ROWS, lanes), BF16)
    pair = jax.ShapeDtypeStruct((2, slots, ROWS, lanes), BF16)
    return call(
        functools.partial(qkv_kernel, len(tokens), len(weights)),
        "qkv",
        5,
        out_shape=(out, pair),
        in_specs=[SMEM] + [VMEM] * len(tokens) + [ANY] * len(weights) + [VMEM],
        out_specs=(VMEM,) * 2,
        scratch_shapes=[
            pltpu.VMEM((3, D, lanes), BF16),
            pltpu.SemaphoreType.DMA((len(weights) * weights[0].shape[0],)),
        ],
    )(places, *tokens, *weights, bias)


def turn_kernel(*refs):
    for s, ref in enumerate(refs[:-1]):
        turn_wide(ref, refs[-1].at[:, s * ROWS : (s + 1) * ROWS])


def turn_tokens(tokens):
    return call(
        turn_kernel,
        "turn_tokens",
        2,
        out_shape=jax.ShapeDtypeStruct((D, len(tokens) * ROWS), BF16),
        in_specs=[VMEM] * len(tokens),
        out_specs=VMEM,
    )(*tokens)


def left_half(shape):
    return lax.broadcasted_iota(jnp.int32, shape, len(shape) - 1) < HEAD_DIM


def split3(value):
    high = value.astype(BF16).astype(F32)
    middle = (value - high).astype(BF16).astype(F32)
    low = (value - high - middle).astype(BF16).astype(F32)
    return high, middle, low


def spread3(value, docs, shape):
    lane = lax.broadcasted_iota(jnp.int32, shape, 1) % HEAD_DIM
    high, middle, low = split3(value)
    return jnp.where(
        lane == docs, high, jnp.where(lane == docs + 1, middle, jnp.where(lane == docs + 2, low, 0.0))
    )


STEP = 512


def eye(size):
    shape = (size, size)
    same = lax.broadcasted_iota(jnp.int32, shape, 0) == lax.broadcasted_iota(jnp.int32, shape, 1)
    return jnp.where(same, 1.0, 0.0).astype(BF16)


def turn(value):
    return dot(eye(value.shape[1]), value, ((1,), (1,))).astype(BF16)


def turn_wide(value, target, first=0):
    for at in range(0, value.shape[1], PAIR * 2):
        block = value[:, at : at + PAIR * 2]
        target[first + at : first + at + block.shape[1]] = turn(block)


def fill_keys(keyvals, feature_k, keys, values, mine):
    at = 0
    for ref in keyvals:
        for index in range(ref.shape[1]):
            rows = slice(at, at + ROWS)
            keys[rows] = jnp.where(mine, ref[0, index], feature_k[at // ROWS])
            values[rows] = jnp.where(mine, ref[1, index], feature_k[at // ROWS])
            at += ROWS


def for_heads(odd, body):
    if not odd:
        body(2)
        return
    tile = pl.program_id(0)
    pl.when(tile < pl.num_programs(0) - 1)(lambda: body(2))
    pl.when(tile == pl.num_programs(0) - 1)(lambda: body(1))


def attend_kernel(sides, docs, odd, *refs):
    query, feature_q, feature_k = refs[:3]
    keyvals = refs[3 : 3 + sides]
    slots, length = feature_q.shape[0], feature_k.shape[0] * ROWS
    rest = refs[3 + sides :]
    wide, total, lows, (keys, values, scores) = rest[0], rest[1], rest[2:-3], rest[-3:]
    left = left_half((ROWS, PAIR))
    sides_of = (left, jnp.logical_not(left))

    def body(heads):
        for head in range(heads):
            fill_keys(keyvals, feature_k, keys.at[head], values.at[head], sides_of[head])
        units = [(slot, head) for slot in range(slots) for head in range(heads)]

        def queries(unit):
            slot, head = unit
            return jnp.where(sides_of[head], query[slot] * 0.125, feature_q[slot])

        def score(unit, number, rows, at, most):
            made = dot(rows, keys[unit[1], at : at + STEP], ((1,), (1,)))
            scores[number % 2, :, at : at + STEP] = made
            for lane in range(0, STEP, PAIR):
                part = made[:, lane : lane + PAIR]
                most = part if most is None else jnp.maximum(most, part)
            return most

        most, rows = None, queries(units[0])
        for at in range(0, length, STEP):
            most = score(units[0], 0, rows, at, most)
        done = {}
        for number, (slot, head) in enumerate(units):
            top = jnp.max(most, axis=1, keepdims=True)
            following = units[number + 1] if number + 1 < len(units) else None
            most, acc = None, 0.0
            if following:
                rows = queries(following)
            for at in range(0, length, STEP):
                if following:
                    most = score(following, number + 1, rows, at, most)
                weights = jnp.exp(scores[number % 2, :, at : at + STEP] - top).astype(BF16)
                acc = acc + dot(weights, values[head, at : at + STEP])
            lane = docs + (HEAD_DIM if head == 0 else 0)
            weight = acc[:, lane : lane + 1]
            done[head] = (acc / weight, top + jnp.log(weight))
            if head == heads - 1:
                result, sums = done[0]
                sums = jnp.broadcast_to(sums, (ROWS, PAIR))
                if heads > 1:
                    result = jnp.where(left, result, done[1][0])
                    sums = jnp.where(left, sums, done[1][1])
                wide[slot] = result
                total[slot] = sums
                lows[slot][...] = result.astype(BF16)

    for_heads(odd, body)


def tile_spec(array, base=0):
    lead = array.shape[:-1]
    return pl.BlockSpec(lead + (PAIR,), lambda tile: (0,) * len(lead) + (tile + base,))


def fixed_spec(array):
    return pl.BlockSpec(array.shape, lambda tile: (0,) * array.ndim)


def attend(query, keyvals, feature_q, feature_k, docs):
    slots, tiles = query.shape[0], query.shape[-1] // PAIR
    wide = jax.ShapeDtypeStruct(query.shape, F32)
    low = jax.ShapeDtypeStruct(wide.shape[1:], BF16)
    length = feature_k.shape[0] * ROWS
    made = call(
        functools.partial(attend_kernel, len(keyvals), docs, slots > 1),
        "attend",
        12,
        grid=(tiles,),
        out_shape=(wide, wide) + (low,) * slots,
        in_specs=[tile_spec(query), fixed_spec(feature_q), fixed_spec(feature_k)]
        + [tile_spec(a) for a in keyvals],
        out_specs=(tile_spec(wide),) * 2 + (tile_spec(low),) * slots,
        scratch_shapes=[
            pltpu.VMEM((2, length, PAIR), BF16),
            pltpu.VMEM((2, length, PAIR), BF16),
            pltpu.VMEM((2, ROWS, length), F32),
        ],
    )(query, feature_q, feature_k, *keyvals)
    return made[0], made[1], list(made[2:])


def attend_back_kernel(sides, docs, heads, *refs):
    query, wide, total, feature_q, feature_k = refs[:5]
    slots, length = feature_q.shape[0], feature_k.shape[0] * ROWS
    grads_in, keyvals = refs[5 : 5 + slots], refs[5 + slots : 5 + slots + sides]
    rest = refs[5 + slots + sides :]
    grad_q, outs = rest[0], rest[1 : 1 + sides]
    keys, values, queries_t, grads_t, query_own, grad_own, softs, slopes, acc = rest[1 + sides :]
    left = left_half((ROWS, PAIR))
    sides_of = (left, jnp.logical_not(left))
    zero = jnp.zeros((ROWS, PAIR), BF16)
    for head in range(heads):
        fill_keys(keyvals, feature_k, keys.at[head], values.at[head], sides_of[head])
    units = [(slot, head) for head in range(heads) for slot in range(slots)]
    for unit, (slot, head) in enumerate(units):
        mine, at = sides_of[head], head * HEAD_DIM
        rows, grads = query[slot] * 0.125, grads_in[slot][...]
        product = jnp.where(mine, grads.astype(F32) * wide[slot], 0.0)
        delta = jnp.sum(product, axis=1, keepdims=True)
        sums = total[slot, :, at : at + 1]
        spare = feature_q[slot].astype(F32) + spread3(-sums, docs, (ROWS, PAIR))
        queries_t[unit] = turn(jnp.where(mine, rows, spare.astype(BF16)))
        spare = spread3(-delta, docs, (ROWS, PAIR)).astype(BF16)
        grads_t[unit] = turn(jnp.where(mine, grads, spare))
        line = slice(unit * ROWS, (unit + 1) * ROWS)
        query_own[line] = jnp.where(mine, rows, zero)
        grad_own[line] = jnp.where(mine, grads, zero)
    per = slots * ROWS
    pieces = [(ref, index) for ref in keyvals for index in range(ref.shape[1])]
    places = [(ref, index) for ref in outs for index in range(ref.shape[1])]
    for step, at in enumerate(range(0, length, STEP)):
        which = step % 2
        for unit, (slot, head) in enumerate(units):
            line = slice(unit * ROWS, (unit + 1) * ROWS)
            soft = jnp.exp(dot(keys[head, at : at + STEP], queries_t[unit]))
            change = dot(values[head, at : at + STEP], grads_t[unit])
            softs[which, :, line] = soft.astype(BF16)
            slopes[which, :, line] = (soft * change).astype(BF16)
        out_v = dot(softs[which], grad_own[...])
        out_k = dot(slopes[which], query_own[...])
        first = at // ROWS
        for k in range(STEP // ROWS):
            ref, index = places[first + k]
            ref[0, index] = out_k[k * ROWS : (k + 1) * ROWS].astype(BF16)
            ref[1, index] = out_v[k * ROWS : (k + 1) * ROWS].astype(BF16)
        key = jnp.concatenate(
            [pieces[first + k][0][0, pieces[first + k][1]] for k in range(STEP // ROWS)], axis=0
        )
        key_t = turn(key)
        for head in range(heads):
            part = slice(head * HEAD_DIM, (head + 1) * HEAD_DIM)
            made = dot(key_t[part], slopes[which, :, head * per : (head + 1) * per])
            if step == 0:
                acc[part] = made
            else:
                acc[part] += made
    if heads == 1:
        acc[HEAD_DIM:] = jnp.zeros((PAIR - HEAD_DIM, per), F32)
    for slot in range(slots):
        made = (acc[:, slot * ROWS : (slot + 1) * ROWS] * 0.125).astype(BF16)
        grad_q[slot] = turn(made)


def attend_back(query, keyvals, grads, wide, total, feature_q, feature_k, docs, base, tiles, single):
    slots, heads = query.shape[0], 1 if single else 2
    length = feature_k.shape[0] * ROWS
    outs = tuple(
        jax.ShapeDtypeStruct(a.shape[:-1] + (tiles * PAIR,), BF16) for a in (query, *keyvals)
    )
    units = slots * heads
    made = call(
        functools.partial(attend_back_kernel, len(keyvals), docs, heads),
        "attend_back",
        8 if single else 15,
        grid=(tiles,),
        out_shape=outs,
        in_specs=[tile_spec(a, base) for a in (query, wide, total)]
        + [fixed_spec(feature_q), fixed_spec(feature_k)]
        + [tile_spec(a, base) for a in (*grads, *keyvals)],
        out_specs=tuple(tile_spec(a) for a in outs),
        scratch_shapes=[
            pltpu.VMEM((heads, length, PAIR), BF16),
            pltpu.VMEM((heads, length, PAIR), BF16),
            pltpu.VMEM((units, PAIR, ROWS), BF16),
            pltpu.VMEM((units, PAIR, ROWS), BF16),
            pltpu.VMEM((units * ROWS, PAIR), BF16),
            pltpu.VMEM((units * ROWS, PAIR), BF16),
            pltpu.VMEM((2, STEP, units * ROWS), BF16),
            pltpu.VMEM((2, STEP, units * ROWS), BF16),
            pltpu.VMEM((PAIR, slots * ROWS), F32),
        ],
    )(query, wide, total, feature_q, feature_k, *grads, *keyvals)
    return made[0], list(made[1:])


def normalise(value):
    centred = value - jnp.mean(value, axis=-1, keepdims=True)
    inverse = lax.rsqrt(jnp.mean(centred * centred, axis=-1, keepdims=True) + EPSILON)
    return centred * inverse, inverse


def norm_back(grad, gain, unit, inverse):
    scaled = grad * gain
    return inverse * (
        scaled
        - jnp.mean(scaled, axis=-1, keepdims=True)
        - unit * jnp.mean(scaled * unit, axis=-1, keepdims=True)
    )


def erf(value):
    value = jnp.clip(value, -3.7439211627767994, 3.7439211627767994)
    square = value * value
    top = 0.00022905065861350646
    for factor in (0.0034082910107109506, 0.050955695062380861, 0.18520832239976145, 1.128379143519084):
        top = top * square + factor
    bottom = -1.1791602954361697e-7
    for factor in (
        0.000023547966471313185, 0.0010179625278914885, 0.014070470171167667,
        0.11098505178285362, 0.49746925110067538, 1.0,
    ):
        bottom = bottom * square + factor
    return value * top / bottom


def column_sum(value):
    return jnp.sum(value, axis=0, keepdims=True)


def early_copies(places, blocks, weights, sems):
    if len(blocks) == 1:
        return [block_copies(places, 1, blocks, weights, sems)] + [[]] * 4
    rows = D // len(blocks)
    copies = []
    for piece in range(5):
        copies.append([])
        for slot, ref in enumerate(blocks):
            first = pl.multiple_of(places[1, slot] * rows, rows)
            copies[piece].append(
                pltpu.make_async_copy(
                    ref.at[piece * rows : (piece + 1) * rows],
                    weights.at[piece, pl.ds(first, rows), :],
                    sems.at[5 * slot + piece],
                )
            )
    return copies


def start_all(groups):
    for copies in groups:
        start(copies)


def late_rows(places, blocks, down, sems):
    rows = FF // len(blocks)
    found = []
    for slot, ref in enumerate(blocks):
        part = slice(slot * rows, (slot + 1) * rows)
        copy = pltpu.make_async_copy(ref.at[:rows], down.at[part], sems.at[slot])
        copy.start()
        found.append((pl.multiple_of(places[2, slot] * rows, rows), part, copy))
    return found


def fill_table(places, smalls, table):
    count, share = smalls.shape[0], D // smalls.shape[0]
    line = lax.broadcasted_iota(jnp.int32, (PAIR, D), 0)
    lane = lax.broadcasted_iota(jnp.int32, (PAIR, D), 1)
    made = 0.0
    for slot in range(count):
        spread = jnp.where(jnp.logical_and(lane == line + places[1, slot] * share, line < share), 1.0, 0.0)
        made = made + dot(smalls[slot, :, :PAIR], spread.astype(BF16))
    table[0:UP_B] = made[0:UP_B]
    for slot in range(count):
        at = places[1, slot]
        table[pl.ds(UP_B + at // 2, 1), pl.ds(pl.multiple_of(at % 2 * 4 * share, 4 * share), 4 * share)] = (
            smalls[slot, UP_B : UP_B + 1, : 4 * share].astype(F32)
        )


def first_kernel(count, slots, groups, places, *refs):
    blocks, refs = refs[:count], refs[count:]
    attended, refs = refs[: slots * groups], refs[slots * groups :]
    tokens, given, refs = refs[0], refs[1] if count == 1 else None, refs[1 if count > 1 else 2 :]
    many = 2 if slots > 1 else 1
    table, unit, inverse, active, slope_out, sides_out = *refs[:5], refs[5 : 5 + many]
    slope, sides = refs[5 + many], refs[6 + many : 6 + 2 * many]
    weights, turned, smalls, sems, small_sems, out_sems = refs[-6:]
    sent = []

    def leave_part(source, target):
        copy = pltpu.make_async_copy(source, target, out_sems.at[len(sent)])
        copy.start()
        sent.append(copy)

    copies = early_copies(places, blocks, weights, sems)
    if count > 1:
        start_all(copies)
        more = start(
            [
                pltpu.make_async_copy(ref.at[5 * D // count :], smalls.at[slot], small_sems.at[slot])
                for slot, ref in enumerate(blocks)
            ]
        )
    width = D // slots

    def row(at):
        return table[at : at + 1]

    core = places[0, 0] % 2 if slots > 1 else 0
    per = width // 2 if slots > 1 else width
    rows_of = [
        jnp.concatenate([a[...] for a in attended[s * groups : (s + 1) * groups]], axis=1)
        for s in range(slots)
    ]
    far = 4 * FF // 8

    for s in range(slots):
        turn_wide(rows_of[s].astype(BF16), turned)
        if slots > 1:
            first = far + (slots + s) * per
            sides[0][first : first + per] = turned[pl.ds(pl.multiple_of(core * per, per), per)]
            sides[1][first : first + per] = turned[pl.ds(pl.multiple_of((1 - core) * per, per), per)]
        else:
            sides[0][FF + D :] = turned[...]
    if count > 1:
        wait(more)
        fill_table(places, smalls, table)
    else:
        table[...] = given[...]
    wait(copies[0])
    residual = tokens[...].astype(F32) + row(PROJ_B)
    for s in range(slots):
        first = pl.multiple_of((places[0, s] // 2) * width, width)
        residual = residual + dot(rows_of[s][:, :width], weights[0, pl.ds(first, width), :])
    first_unit, first_inverse = normalise(residual)
    unit[...] = first_unit
    inverse[...] = first_inverse
    normed = first_unit * row(NORM_G) + row(NORM_S)
    normed_low = normed.astype(BF16)
    turn_wide(normed_low, turned)
    for side, target in enumerate(sides):
        if slots == 1:
            target[FF : FF + D] = turned[...]
            continue
        for s in range(slots):
            first = pl.multiple_of(places[0, side * slots + s] * per, per)
            target[far + s * per : far + (s + 1) * per] = turned[pl.ds(first, per)]
    for side, target in enumerate(sides):
        rows = slice(FF // len(sides), None)
        leave_part(target.at[rows], sides_out[side].at[rows])
    step = 384
    for at in range(0, FF, step):
        line, col = at // D, at % D
        if col == 0:
            wait(copies[1 + line])
        upward = (
            dot(normed_low, weights[1 + line, :, col : col + step])
            + table[UP_B + line : UP_B + line + 1, col : col + step]
        )
        share = 0.5 + 0.5 * erf(upward * 0.7071067811865476)
        bell = jnp.exp(upward * upward * -0.5) * 0.3989422804014327
        active[:, at : at + step] = (upward * share).astype(BF16)
        slope[:, at : at + step] = (share + upward * bell).astype(BF16)
        if (at + step) % D == 0:
            lanes = slice(at + step - D, at + step)
            leave_part(slope.at[:, lanes], slope_out.at[:, lanes])
    for side, target in enumerate(sides):
        if slots == 1:
            turn_wide(active, target)
            leave_part(target.at[:FF], sides_out[side].at[:FF])
            continue
        rows = FF // 8
        for s in range(slots):
            first = pl.multiple_of(places[0, side * slots + s] * rows, rows)
            for at in range(0, rows, PAIR):
                block = active[:, pl.ds(pl.multiple_of(first + at, PAIR), PAIR)]
                target[s * rows + at : s * rows + at + PAIR] = turn(block)
            part = slice(s * rows, (s + 1) * rows)
            leave_part(target.at[part], sides_out[side].at[part])
    wait(sent)


def first_part(places, blocks, attended, tokens, table):
    count = len(blocks)
    slots = 4 if count > 1 else 1
    groups = len(attended) // slots
    given = [table] if count == 1 else []
    shape = jax.ShapeDtypeStruct
    sides = 2 if slots > 1 else 1
    outs = (
        shape((TABLE, D), F32), shape((ROWS, D), F32), shape((ROWS, 1), F32),
        shape((ROWS, FF), BF16), shape((ROWS, FF), BF16),
    )
    outs += (shape(((FF + 2 * D) // sides, ROWS), BF16),) * sides
    made = call(
        functools.partial(first_kernel, count, slots, groups),
        "forward_up",
        11,
        out_shape=outs,
        in_specs=[SMEM] + [ANY] * count + [VMEM] * (slots * groups + 1 + len(given)),
        out_specs=(VMEM,) * 4 + (ANY,) * (1 + sides),
        scratch_shapes=like(outs[4:])
        + [
            pltpu.VMEM((5, D, D), BF16),
            pltpu.VMEM((D, ROWS), BF16),
            pltpu.VMEM((count, TABLE, D), BF16),
            pltpu.SemaphoreType.DMA((5 * count,)),
            pltpu.SemaphoreType.DMA((count,)),
            pltpu.SemaphoreType.DMA((16,)),
        ],
    )(places, *blocks, *attended, tokens, *given)
    return made[:5], made[5:]


def head_kernel(count, docs, places, *refs):
    blocks, refs = refs[:count], refs[count:]
    unit, active, cotangent, table, numbers = refs[:5]
    output, lines, docs_out, grad_second, grad_out = refs[5:10]
    pool, down, sems = refs[10:]
    down_parts = late_rows(places, blocks, down, sems.at[1])
    pool_copies = block_copies(places, 2, blocks, pool, sems.at[0], slice(FF // count, (FF + D) // count))

    def row(at):
        return table[at : at + 1]

    normed = unit[...] * row(NORM_G) + row(NORM_S)
    residual = normed + row(DOWN_B)
    for first, part, copy in down_parts:
        copy.wait()
        residual = residual + dot(active[:, pl.ds(first, FF // count)], down[part])
    last_unit, last_inverse = normalise(residual)
    outcome = last_unit * row(FINAL_G) + row(FINAL_S)
    out_low = outcome.astype(BF16)
    output[...] = out_low

    at_row, label = numbers[:, 0:1], numbers[:, 1:2]
    here = jnp.logical_and(at_row >= 0.0, at_row < float(ROWS))
    line = lax.broadcasted_iota(jnp.int32, (docs, ROWS), 1).astype(F32)
    pick = jnp.where(line == at_row, 1.0, 0.0)
    first_low = dot(pick.astype(BF16), out_low).astype(BF16)
    wait(pool_copies)
    pooled = jnp.tanh(dot(first_low, pool[...]) + row(POOL_B))
    pooled_low = pooled.astype(BF16).astype(F32)
    logits = [
        jnp.sum(pooled_low * row(CLASS_W + c), axis=1, keepdims=True)
        + numbers[:, 2 + c : 3 + c]
        for c in range(CLASSES)
    ]
    top = functools.reduce(jnp.maximum, logits)
    powers = [jnp.exp(logit - top) for logit in logits]
    whole = functools.reduce(jnp.add, powers)
    grads = [powers[c] / whole - jnp.where(label == float(c), 1.0, 0.0) for c in range(CLASSES)]
    grad_pre = functools.reduce(jnp.add, [grads[c] * row(CLASS_W + c) for c in range(CLASSES)])
    grad_pre = grad_pre * (1.0 - pooled * pooled)
    parts = jnp.concatenate(split3(grad_pre), axis=0).astype(BF16)
    made = dot(parts, pool[...], ((1,), (1,)))
    grad_first = made[:docs] + made[docs : 2 * docs] + made[2 * docs :]
    parts = jnp.concatenate(split3(grad_first), axis=0).astype(BF16)
    picks = jnp.concatenate([pick] * 3, axis=0).astype(BF16)
    grad_outcome = cotangent[...] + dot(picks, parts, ((0,), (0,)))
    lane = lax.broadcasted_iota(jnp.int32, (docs, 128), 1)
    small = jnp.zeros((docs, 128), F32)
    for c in range(CLASSES):
        small = jnp.where(lane == c, grads[c], jnp.where(lane == CLASSES + c, logits[c], small))
    docs_out[...] = jnp.where(
        here,
        jnp.concatenate([first_low.astype(F32), pooled_low, grad_pre, small], axis=1),
        0.0,
    )

    grad = norm_back(grad_outcome, row(FINAL_G), last_unit, last_inverse)
    grad_second[...] = grad
    grad_out[...] = grad.astype(BF16)
    lines[0:1] = column_sum(grad)
    lines[1:2] = column_sum(grad_outcome * last_unit)
    lines[2:3] = column_sum(grad_outcome)
    lines[3:8] = jnp.zeros((5, D), F32)


def head_part(places, late, unit, active, cotangent, table, numbers):
    count, docs = len(late), numbers.shape[0]
    shape = jax.ShapeDtypeStruct
    outs = (
        shape((ROWS, D), BF16),
        shape((8, D), F32),
        shape((docs, 3 * D + 128), F32),
        shape((ROWS, D), F32),
        shape((ROWS, D), BF16),
    )
    return call(
        functools.partial(head_kernel, count, docs),
        "head",
        7,
        out_shape=outs,
        in_specs=[SMEM] + [ANY] * count + [VMEM] * 5,
        out_specs=(VMEM,) * len(outs),
        scratch_shapes=[
            pltpu.VMEM((D, D), BF16),
            pltpu.VMEM((FF, D), BF16),
            pltpu.SemaphoreType.DMA((2, count)),
        ],
    )(places, *late, unit, active, cotangent, table, numbers)


def second_kernel(count, places, *refs):
    downs, (grad_down, slope, lines, grad_up, down, sems) = refs[:count], refs[count:]
    grad_low = grad_down[...]
    whole = FF // count
    step = min(whole, 384)
    for first, part, copy in late_rows(places, downs, down, sems):
        copy.wait()
        for at in range(0, whole, step):
            rows = down[part.start + at : part.start + at + step]
            grad = dot(grad_low, rows, ((1,), (1,))).astype(BF16).astype(F32)
            here = pl.multiple_of(first + at, step)
            grad = grad * slope[:, pl.ds(here, step)].astype(F32)
            line, col = here // D, pl.multiple_of(here % D, step)
            lines[pl.ds(line, 1), pl.ds(col, step)] = column_sum(grad)
            grad_up[line, :, pl.ds(col, step)] = grad.astype(BF16)
    lines[4:8] = jnp.zeros((4, D), F32)


def second_part(places, late, grad_down, slope):
    count, shape = len(late), jax.ShapeDtypeStruct
    outs = (shape((8, D), F32), shape((4, ROWS, D), BF16))
    return call(
        functools.partial(second_kernel, count),
        "backward_down",
        5,
        out_shape=outs,
        in_specs=[SMEM] + [ANY] * count + [VMEM] * 2,
        out_specs=(VMEM,) * 2,
        scratch_shapes=[pltpu.VMEM((FF, D), BF16), pltpu.SemaphoreType.DMA((count,))],
    )(places, *late, grad_down, slope)


def third_kernel(count, slots, places, *refs):
    blocks, refs = refs[:count], refs[count:]
    table, grad_second, grad_up, unit, inverse = refs[:5]
    lines, grad_first, grad_out = refs[5:8]
    grad_attended = refs[8 : 8 + slots]
    weights, sems = refs[8 + slots :]
    copies = early_copies(places, blocks, weights, sems)
    if count > 1:
        start_all(copies[1:] + copies[:1])
    else:
        wait(copies[0])
    width = D // slots

    def row(at):
        return table[at : at + 1]

    back = 0.0
    for line in range(4):
        wait(copies[1 + line])
        back = back + dot(grad_up[line], weights[1 + line], ((1,), (1,)))
    grad_normed = grad_second[...] + back.astype(BF16).astype(F32)
    lines[0:4] = jnp.zeros((4, D), F32)
    lines[4:5] = column_sum(grad_normed * unit[...])
    lines[5:6] = column_sum(grad_normed)
    grad = norm_back(grad_normed, row(NORM_G), unit[...], inverse[...])
    grad_first[...] = grad
    lines[6:7] = column_sum(grad)
    lines[7:8] = jnp.zeros((1, D), F32)
    grad_low = grad.astype(BF16)
    grad_out[...] = grad_low
    if count > 1:
        wait(copies[0])
    for s in range(slots):
        first = pl.multiple_of((places[0, s] // 2) * width, width)
        made = dot(grad_low, weights[0, pl.ds(first, width), :], ((1,), (1,))).astype(BF16)
        if width < grad_attended[s].shape[1]:
            grad_attended[s][:, PAIR:] = jnp.zeros((ROWS, PAIR), BF16)
        grad_attended[s][:, :width] = made


def third_part(places, blocks, table, grad_second, grad_up, unit, inverse, slots, lanes):
    count = len(blocks)
    shape = jax.ShapeDtypeStruct
    outs = (shape((8, D), F32), shape((ROWS, D), F32), shape((ROWS, D), BF16))
    outs += (shape((ROWS, lanes), BF16),) * slots
    made = call(
        functools.partial(third_kernel, count, slots),
        "backward_up",
        7,
        out_shape=outs,
        in_specs=[SMEM] + [ANY] * count + [VMEM] * 5,
        out_specs=(VMEM,) * len(outs),
        scratch_shapes=[pltpu.VMEM((5, D, D), BF16), pltpu.SemaphoreType.DMA((5 * count,))],
    )(places, *blocks, table, grad_second, grad_up, unit, inverse)
    return made[:3], list(made[3:])


def wgrad_outs(slots, rows):
    shape = jax.ShapeDtypeStruct
    if slots == 1:
        return (shape((1, rows, D), BF16),)
    half = rows // 2
    return (shape((2, half, D), BF16),) * 2 + (shape((half, D), BF16),) * 2 + (shape((rows, D), F32),)


def put_slot(outs, s, first, value):
    if len(outs) == 1:
        outs[0][0, first : first + value.shape[0]] = value.astype(BF16)
        return
    if s == 0:
        outs[4][first : first + value.shape[0]] = value
        return
    half = outs[2].shape[0]
    for k, order in enumerate(((1, 3, 2), (2, 3, 1))):
        low, high = max(first, k * half), min(first + value.shape[0], (k + 1) * half)
        if low >= high:
            continue
        rows, part = slice(low - k * half, high - k * half), value[low - first : high - first]
        if s == order[2]:
            outs[2 + k][rows] = part.astype(BF16)
        else:
            outs[k][order.index(s), rows] = part.astype(BF16)


def gradient_call(body, name, micros, ins, outs, scratch, waits):
    return call(
        body,
        name,
        micros,
        out_shape=outs,
        in_specs=[ANY] * len(ins),
        out_specs=(ANY,) * len(outs),
        scratch_shapes=[pltpu.VMEM(a.shape, a.dtype) for a in outs]
        + scratch
        + [pltpu.SemaphoreType.DMA((waits,)), pltpu.SemaphoreType.DMA((len(outs),))],
    )(*ins)


def leave(kept, outs, sems, which):
    return start([pltpu.make_async_copy(kept[k], outs[k], sems.at[k]) for k in which])


def down_kernel(slots, sides, *refs):
    lefts, rights, refs = refs[:sides], refs[sides : 2 * sides], refs[2 * sides :]
    count = 5 if slots > 1 else 1
    outs, kept, (left, right, sems, out_sems) = refs[:count], refs[count : 2 * count], refs[-4:]
    rows = FF // sides // slots
    step = min(rows, 384)
    copies = {}
    for side in range(sides):
        copies[side] = pltpu.make_async_copy(rights[side], right.at[side], sems.at[side])
    order = (3, 1, 2, 0) if slots > 1 else (0,)
    for s in order:
        for side in range(sides):
            part = slice(s * rows, (s + 1) * rows)
            copies[s, side] = pltpu.make_async_copy(
                lefts[side].at[part], left.at[side, part], sems.at[sides + s * sides + side]
            )
    start(copies.values())
    wait([copies[side] for side in range(sides)])
    sent = []
    for s in order:
        wait([copies[s, side] for side in range(sides)])
        for at in range(0, rows, step):
            first = s * rows + at
            made = dot(left[0, first : first + step], right[0])
            for side in range(1, sides):
                made = made + dot(left[side, first : first + step], right[side])
            put_slot(kept, s, at, made)
        if slots > 1:
            sent += leave(kept, outs, out_sems, {3: (), 1: (0, 3), 2: (1, 2), 0: (4,)}[s])
        else:
            sent += leave(kept, outs, out_sems, (0,))
    wait(sent)


def down_gradient(lefts, rights, slots):
    sides = len(lefts)
    outs = wgrad_outs(slots, FF // sides // slots)
    scratch = [pltpu.VMEM((sides, FF // sides, ROWS), BF16), pltpu.VMEM((sides, ROWS, D), BF16)]
    body = functools.partial(down_kernel, slots, sides)
    return gradient_call(
        body, "down_gradient", 3, (*lefts, *rights), outs, scratch, sides * (slots + 1)
    )


def up_kernel(slots, sides, *refs):
    lefts, ups, projs, refs = *(refs[k * sides : (k + 1) * sides] for k in range(3)), refs[3 * sides :]
    count = 5 if slots > 1 else 1
    outs, kept, (left, right, sems, out_sems) = refs[:count], refs[count : 2 * count], refs[-4:]
    whole = D // sides
    rows = whole // slots
    copies = {}
    for side in range(sides):
        copies[side] = pltpu.make_async_copy(
            lefts[side].at[FF // sides :], left.at[side], sems.at[side]
        )
    for line in range(5):
        for side in range(sides):
            copies[line, side] = pltpu.make_async_copy(
                ups[side].at[line] if line < 4 else projs[side],
                right.at[side, line],
                sems.at[sides + line * sides + side],
            )
    start(copies.values())
    wait([copies[side] for side in range(sides)])
    sent = []
    for line in range(5):
        wait([copies[line, side] for side in range(sides)])
        at = 0 if line < 4 else whole
        made = dot(left[0, at : at + whole], right[0, line])
        for side in range(1, sides):
            made = made + dot(left[side, at : at + whole], right[side, line])
        for s in range(slots):
            put_slot(kept, s, line * rows, made[s * rows : (s + 1) * rows])
        if slots > 1:
            sent += leave(kept, outs, out_sems, {2: (0, 2), 4: (1, 3, 4)}.get(line, ()))
        elif line == 4:
            sent += leave(kept, outs, out_sems, (0,))
    wait(sent)


def up_gradient(lefts, ups, projs, slots):
    sides = len(lefts)
    outs = wgrad_outs(slots, 5 * D // sides // slots)
    scratch = [pltpu.VMEM((sides, 2 * D // sides, ROWS), BF16), pltpu.VMEM((sides, 5, ROWS, D), BF16)]
    body = functools.partial(up_kernel, slots, sides)
    return gradient_call(body, "up_gradient", 4, (*lefts, *ups, *projs), outs, scratch, 6 * sides)


def input_kernel(groups, sides, places, *refs):
    turned, refs = refs[:sides], refs[sides:]
    grad_qs, refs = refs[:groups], refs[groups:]
    changes, refs = refs[: groups * sides], refs[groups * sides :]
    outs, (made, lines, grads, sems) = refs[:-4], refs[-4:]
    rows = turned[0].shape[1]
    count = outs[0].shape[0] // 3 // (D // (8 if sides > 1 else 1))
    share = D // (8 if sides > 1 else 1)
    sums, sends = [], []
    for k in range(3):
        total, line = None, None
        for side in range(sides if k else 1):
            lane = 0
            for group in range(groups):
                source = changes[group * sides + side].at[k - 1] if k else grad_qs[group]
                lanes = slice(lane, lane + source.shape[2])
                lane = lanes.stop
                grads[:, lanes] = source[...].reshape(rows, source.shape[2])
            part = dot(turned[side][...], grads[...])
            total = part if total is None else total + part
            if k != 1:
                part = dot(jnp.ones((8, rows), BF16), grads[...])
                line = part if line is None else line + part
        made[k] = total.astype(BF16)
        if k != 1:
            sums.append(line[:1])
        for side, out in enumerate(outs):
            for s in range(count):
                first = pl.multiple_of(places[0, side * count + s] * share, share)
                target = out.at[(3 * s + k) * share : (3 * s + k + 1) * share]
                sends.append((made.at[k, pl.ds(first, share), :], target))
                pltpu.make_async_copy(*sends[-1], sems.at[len(sends) - 1]).start()
    lines[...] = jnp.concatenate([*sums, jnp.zeros((14, lines.shape[1]), F32)], axis=0).astype(BF16)
    for out in outs:
        sends.append((lines, out.at[3 * count * share :]))
        pltpu.make_async_copy(*sends[-1], sems.at[len(sends) - 1]).start()
    wait([pltpu.make_async_copy(a, b, sems.at[k]) for k, (a, b) in enumerate(sends)])


def input_gradient(places, turned, grad_qs, changes, slots):
    lanes = sum(grad.shape[2] for grad in grad_qs)
    sides, groups = len(turned), len(grad_qs)
    out = jax.ShapeDtypeStruct((3 * D // sides + 16, lanes), BF16)
    made = call(
        functools.partial(input_kernel, groups, sides),
        "input_weights",
        5,
        out_shape=(out,) * sides,
        in_specs=[SMEM] + [VMEM] * (sides + groups + groups * sides),
        out_specs=(ANY,) * sides,
        scratch_shapes=[
            pltpu.VMEM((3, D, lanes), BF16),
            pltpu.VMEM((16, lanes), BF16),
            pltpu.VMEM((turned[0].shape[1], lanes), BF16),
            pltpu.SemaphoreType.DMA((sides * (3 * slots + 1),)),
        ],
    )(places, *turned, *grad_qs, *changes)
    return list(made)


def last_kernel(sides, groups, parts, places, *refs):
    weights, refs = refs[:sides], refs[sides:]
    grad_qs, refs = refs[:groups], refs[groups:]
    changes, refs = refs[: groups * parts], refs[groups * parts :]
    grad_first, own, outs = *refs[:2], refs[2:-3]
    held, grads, sems = refs[-3:]
    slots = grad_qs[0].shape[0]
    copies = block_copies(places, 0, weight_refs(weights), held, sems)
    for s in range(slots):
        rows = slice(s * ROWS, (s + 1) * ROWS)
        lane = 0
        for group in range(groups):
            lanes = slice(lane, lane + grad_qs[group].shape[2])
            lane = lanes.stop
            grads[0, rows, lanes] = grad_qs[group][s]
            for k in range(2):
                total = changes[group * parts][k, s].astype(F32)
                for change in changes[group * parts + 1 : (group + 1) * parts]:
                    total = total + change[k, s].astype(F32)
                grads[1 + k, rows, lanes] = total.astype(BF16)
    wait(copies)

    def partial(s):
        rows = slice(s * ROWS, (s + 1) * ROWS)
        total = dot(grads[0, rows], held[0], ((1,), (1,)))
        for k in range(1, 3):
            total = total + dot(grads[k, rows], held[k], ((1,), (1,)))
        return total

    for s in range(1, slots):
        outs[s - 1][...] = partial(s).astype(BF16)
    own[...] = grad_first[...] + partial(0)


def last_part(places, weights, grad_qs, changes, grad_first):
    slots, lanes = grad_qs[0].shape[0], sum(grad.shape[2] for grad in grad_qs)
    groups, parts = len(grad_qs), len(changes) // len(grad_qs)
    sides, shape = len(weights), jax.ShapeDtypeStruct
    outs = (shape((ROWS, D), F32),) + (shape((ROWS, D), BF16),) * (slots - 1)
    blocks = sides * weights[0].shape[0]
    made = call(
        functools.partial(last_kernel, sides, groups, parts),
        "input_gradients",
        5,
        out_shape=outs,
        in_specs=[SMEM] + [ANY] * sides + [VMEM] * (1 + groups + len(changes)),
        out_specs=(VMEM,) * len(outs),
        scratch_shapes=[
            pltpu.VMEM((3, D, lanes), BF16),
            pltpu.VMEM((3, slots * ROWS, lanes), BF16),
            pltpu.SemaphoreType.DMA((blocks,)),
        ],
    )(places, *weights, *grad_qs, *changes, grad_first)
    return made[0], made[1:]


def whole_scatter(part, pieces):
    seq = lax.axis_size("seq")
    rows = part.shape[1] // pieces // seq
    part = part.reshape(pieces, seq, rows, D).transpose(1, 0, 2, 3)
    part = part.reshape(seq, pieces * rows, D)
    return lax.psum_scatter(part, "seq", scatter_dimension=0, tiled=True)[0].astype(F32)


def by_chip(pieces):
    me = lax.axis_index("seq")
    for bit in (1, 2):
        odd = (me & (2 * bit)) != 0
        pieces = [jnp.where(odd, pieces[s ^ bit], pieces[s]) for s in range(len(pieces))]
    return pieces


def features(positions, starts):
    docs = starts.shape[0]
    segment = jnp.sum((positions[..., None] >= starts).astype(jnp.int32), axis=-1) - 1
    lane = jnp.arange(PAIR, dtype=jnp.int32) % HEAD_DIM
    own = segment[..., None] == lane
    return own, lane, docs


def on_device(
    inputs,
    cotangent,
    doc_lengths,
    doc_labels,
    query_weight,
    query_bias,
    key_weight,
    value_weight,
    value_bias,
    proj_weight,
    proj_bias,
    norm_gain,
    norm_shift,
    up_weight,
    up_bias,
    down_weight,
    down_bias,
    final_gain,
    final_shift,
    pool_weight,
    pool_bias,
    class_weight,
    class_bias,
):
    me = lax.axis_index("seq")
    tokens = inputs[0]
    share = query_bias.shape[0]
    lengths = doc_lengths[0]
    docs = lengths.shape[0]
    order = jnp.arange(docs, dtype=jnp.int32)
    starts = jnp.sum(jnp.where(order[None, :] < order[:, None], lengths[None, :], 0), axis=1)

    numbers = jnp.concatenate(
        [
            (starts - me * ROWS)[:, None].astype(F32),
            doc_labels[0][:, None].astype(F32),
            jnp.broadcast_to(class_bias.astype(F32), (docs, CLASSES)),
            jnp.zeros((docs, PAIR - 2 - CLASSES), F32),
        ],
        axis=1,
    )

    small_mesh = is_small()
    slot_list = slot_owners()
    chip, core = me // 2, me % 2
    width = D // 4
    slots = 4 if small_mesh else 1
    line = jnp.arange(ROWS, dtype=jnp.int32)
    mine = slot_list[:slots] if small_mesh else me[None]
    own, lane, _ = features(mine[:, None] * ROWS + line, starts)
    feature_q = jnp.where(own, FAR, 0.0).astype(BF16)
    own, lane, _ = features(slot_list[:, None] * ROWS + line, starts)
    feature_k = jnp.where(
        lane < docs, jnp.where(own, 0.0, 1.0), jnp.where(lane < docs + 3, 1.0, 0.0)
    ).astype(BF16)

    matrices = jnp.stack([query_weight, key_weight, value_weight])
    bias = jnp.stack([query_bias, value_bias])
    small = jnp.stack(
        [
            query_bias, value_bias, proj_bias, norm_gain, norm_shift, down_bias,
            final_gain, final_shift, pool_bias, *class_weight.T,
        ]
    )
    wide = me * up_bias.shape[0]
    up_pieces = up_weight.reshape(share, 4, D).transpose(1, 0, 2)
    proj_up = jnp.concatenate([proj_weight[None], up_pieces])
    down_pool = jnp.concatenate([down_weight, pool_weight])
    if small_mesh:
        pieces = [
            lax.dynamic_slice_in_dim(matrices, (chip ^ s) * width, width, 2) for s in range(4)
        ]
        token_blocks = gather_tokens(tokens)
        own = jnp.stack(exchange(pieces))
        own = jnp.pad(own, ((0, 0), (0, 0), (0, 0), (0, PAIR * 2 - width)))
        small = jnp.pad(small, ((0, TABLE - small.shape[0]), (0, D - share)))
        small = lax.dynamic_update_slice(small, up_bias[None], (UP_B, 0))
        early = Shared(jnp.concatenate([proj_up.reshape(5 * share, D), small]), 0)
        late = Shared(down_pool, 1)
        places = jnp.stack([slot_list, early.owners(), late.owners()])
        come = swap(bias, along(1))
        bias = jnp.where(
            core == 0, jnp.concatenate([bias, come], axis=1), jnp.concatenate([come, bias], axis=1)
        )
        bias = jnp.pad(bias, ((0, 0), (0, PAIR * 2 - width))).astype(F32)
        own = after(own, feature_q, feature_k, places, bias, numbers, token_blocks[1:3])
        weights = [own, swap(own, along(1))]
        early.near()
        late.near()
        table = None
    else:
        token_blocks = [tokens]
        weights = [lax.all_gather(matrices, "seq", axis=1, tiled=True)[None]]
        table = jnp.zeros((TABLE, D), BF16)
        table = lax.dynamic_update_slice(table, small, (0, me * share))
        table = lax.dynamic_update_slice(table, up_bias[None], (UP_B + wide // D, wide % D))
        table = sum_seq(table).astype(F32)
        bias = table[:2]
        blocks = [lax.all_gather(proj_up, "seq", axis=1, tiled=True)]
        whole = lax.all_gather(down_pool, "seq", axis=0)
        whole = [whole[:, : 4 * share].reshape(FF, D), whole[:, 4 * share :].reshape(D, D)]
        late_blocks = [jnp.concatenate(whole)]
        places = jnp.zeros((3, 1), jnp.int32)

    query, keyval = qkv_project(places, token_blocks, weights, bias)
    tokens_t = turn_tokens(after(token_blocks, query))
    if small_mesh:
        early.one, late.one = after((early.one, late.one), tokens_t)
        keyval = after(keyval, early.one, late.one)
        keyvals = [keyval, swap(keyval, along(1))]
        early.far()
        early.rest()
        early.cross()
        late.far()
    else:
        keyvals = [lax.all_gather(keyval, "seq", axis=1, tiled=True)]
    attended, total, lows = attend(query, keyvals, feature_q, feature_k, docs)
    if small_mesh:
        lows, tokens_t, early.both, early.other, early.crossed = after(
            (lows, tokens_t, early.both, early.other, early.crossed), lows
        )
        early.cross_both()
        blocks = early.finish()
    else:
        tokens_t = [tokens_t]
    lows = exchange(lows)
    if small_mesh:
        late.shard, late.one, late.both = after((late.shard, late.one, late.both), lows)
        late.rest_direct()
        late.cross()
        late.cross_both()

    made, turned = first_part(places, blocks, lows, tokens, table)
    table, unit, inverse, active, slope = made
    if small_mesh:
        late.other, late.crossed, late.middle, tokens_t, turned = after(
            (late.other, late.crossed, late.middle, tokens_t, turned), active
        )
        late_blocks = late.finish()
        tokens_t = [tokens_t, swap(tokens_t, along(1))]
    output, lines_one, docs_out, grad_second, grad_down = head_part(
        places, late_blocks, unit, active, cotangent[0], table, numbers
    )

    def both(keep, *away):
        return [keep] + [swap(a, along(1)) for a in away]

    def own_and_other(value):
        return both(value, *([value] if small_mesh else []))

    turned = both(*turned)
    down_parts = down_gradient(turned, own_and_other(grad_down), slots)
    if small_mesh:
        down_sum = Scatter(down_parts)
    grad_down = after(grad_down, down_parts, tokens_t)
    lines_two, grad_up = second_part(places, late_blocks, grad_down, slope)
    grad_second = after(grad_second, grad_up)
    made, grads = third_part(
        places, blocks, table, grad_second, grad_up, unit, inverse, slots, query.shape[-1]
    )
    lines_three, grad_first, grad_proj = made
    lines_two = lines_two + lines_three
    pack = jnp.concatenate([docs_out, lines_one, lines_two], axis=1)
    ups = own_and_other(grad_up)
    if small_mesh:
        grad_proj, grads = after((grad_proj, grads), down_sum.comes)
        down_sum.combine()
        down_sum.turn()
        grads = exchange(grads)
    up_parts = up_gradient(turned, ups, own_and_other(grad_proj), slots)

    back = functools.partial(
        attend_back, keyvals=keyvals,
        feature_q=feature_q, feature_k=feature_k, docs=docs,
    )
    if small_mesh:
        up_parts, pack, grads, down_sum.lasts = after(
            (up_parts, pack, grads, down_sum.lasts), up_parts
        )
        down_dp = SumDp(down_sum.total())
        up_sum = Scatter(up_parts)
        come = swap(pack, along(1))
        grad_q, changes = back(
            query, grads=grads, wide=attended, total=total, base=0, tiles=1, single=False
        )
        changes, pack, come, up_sum.seconds, down_dp.come = after(
            (changes, pack, come, up_sum.seconds, down_dp.come), grad_q, up_sum.comes
        )
        grad_qs, partial, changes = [grad_q], list(changes), both(*changes)
        up_sum.combine()
        up_sum.turn()
        down_dp.across()
        pack = pack + come
        come = swap(pack, along(2))
        rows = after(query, grad_q, up_sum.sends, down_dp.pair, pack)
        grad_q, more = back(
            rows, grads=grads, wide=attended, total=total, base=1, tiles=1, single=True
        )
        more, pack, come, up_sum.lasts, down_dp.cross = after(
            (more, pack, come, up_sum.lasts, down_dp.cross), grad_q
        )
        grad_qs, partial = grad_qs + [grad_q], partial + list(more)
        changes = changes + both(*more)
        up_dp = SumDp(up_sum.total())
        pack = pack + come
        come = swap(pack, along(4))
    else:
        grad_q, changes = back(
            query, grads=grads, wide=attended, total=total,
            base=0, tiles=HEADS // 2, single=False,
        )
        grad_qs, partial = [grad_q], changes
        change = changes[0].transpose(1, 0, 2, 3)
        change = lax.psum_scatter(change, "seq", scatter_dimension=0, tiled=True)
        changes = [change.transpose(1, 0, 2, 3)]
        partial = changes
        pack = sum_seq(pack)
    def own_shares(pack):
        at = me * share
        lines = pack[:, 3 * D + PAIR :].reshape(docs, 2, D).transpose(1, 0, 2).reshape(2 * docs, D)
        own = jnp.concatenate(
            [
                lax.dynamic_slice_in_dim(lines, at, share, 1),
                lax.dynamic_slice_in_dim(lines[8:12].reshape(-1), wide, 4 * share, 0).reshape(4, share),
                jnp.zeros((4, share), F32),
            ]
        )
        parts = [
            pack[:, 2 * D : 3 * D],
            lax.dynamic_slice_in_dim(pack, at, share, 1),
            lax.dynamic_slice_in_dim(pack, D + at, share, 1),
            pack[:, 3 * D : 3 * D + PAIR],
            own.reshape(docs, 3 * share),
        ]
        logits = pack[:, 3 * D + CLASSES : 3 * D + 2 * CLASSES]
        return jnp.concatenate(parts, axis=1), logits

    qkv_parts = input_gradient(places, tokens_t, grad_qs, partial, slots)
    if small_mesh:
        qkv_parts, changes, pack, come, up_dp.come, down_dp.cross = after(
            (qkv_parts, changes, pack, come, up_dp.come, down_dp.cross), qkv_parts
        )
        keep, away = both(*qkv_parts)
        up_dp.across()
        away = after(away, up_dp.pair)
        rows = 3 * share
        pieces = [
            add(keep[s * rows : (s + 1) * rows, :width], away[s * rows : (s + 1) * rows, :width])
            for s in range(4)
        ]
        ends = add(keep[4 * rows : 4 * rows + 2], away[4 * rows : 4 * rows + 2])
        pieces = [piece.astype(BF16) for piece in pieces]
        pack, come = after((pack, come), pieces)
        pieces = exchange(pieces)
        pack, logits = own_shares(pack + come)
        come = swap(pack, lambda z, i: (z ^ 1, i))
        changes = after(changes, pieces[0], pack, ends)
    input_grad, sums = last_part(places, weights, grad_qs, changes, grad_first)

    if small_mesh:
        pieces, down_dp.cross, pack, come = after(
            (pieces, down_dp.cross, pack, come), input_grad
        )
        qkv_wgrad = jnp.concatenate(by_chip(pieces), axis=1)
        ends = jnp.pad(
            lax.dynamic_slice_in_dim(ends, core * share, share, 1), ((0, 30), (0, D - share))
        )
        qkv_dp = SumDp(jnp.concatenate([qkv_wgrad.astype(F32), ends]))
        pack = jnp.concatenate([pack, come], axis=0)
        come = swap(pack, lambda z, i: (z ^ 2, i))
        down_dp.finish()
        sums = exchange([input_grad, *sums])
        qkv_dp.come, up_dp.cross = after((qkv_dp.come, up_dp.cross), qkv_dp.come)
        qkv_dp.across()
        up_dp.finish()
        every_doc = jnp.concatenate([pack, come], axis=0)
        qkv_dp.cross, sums, every_doc, down_dp.last = after(
            (qkv_dp.cross, sums, every_doc, down_dp.last), qkv_dp.cross
        )
        qkv_dp.finish()
        down_wgrad, up_wgrad = down_dp.back(), up_dp.back()
        input_grad = add(*sums)
        qkv_wgrad = qkv_dp.back()
    else:
        qkv_wgrad = whole_scatter(qkv_parts[0][None, : 3 * D], 3)
        ends = sum_seq(qkv_parts[0][3 * D : 3 * D + 2].astype(F32))
        ends = lax.dynamic_slice_in_dim(ends, me * share, share, 1)
        qkv_wgrad = sum_dp(jnp.concatenate([qkv_wgrad, jnp.pad(ends, ((0, 30), (0, D - share)))]))
        down_wgrad = sum_dp(whole_scatter(down_parts[0], 1))
        up_wgrad = sum_dp(whole_scatter(up_parts[0], 5))
    proj_wgrad = up_wgrad[4 * share :]
    up_wgrad = up_wgrad[: 4 * share].reshape(4, share, D).transpose(1, 0, 2).reshape(share, FF)
    ends = qkv_wgrad[3 * share : 3 * share + 2, :share]
    qkv_wgrad = qkv_wgrad[: 3 * share].reshape(3, share, D)
    if not small_mesh:
        pack, logits = own_shares(pack)
        every_doc = stack_dp(pack)
    pre_all, first_all, pooled_all = (
        every_doc[:, at : at + size] for at, size in ((0, D), (D, share), (D + share, share))
    )
    logit_all = every_doc[:, D + 2 * share : D + 2 * share + CLASSES]
    lines = jnp.sum(every_doc[:, D + 2 * share + PAIR :].reshape(-1, docs, 3 * share), axis=0)
    lines = lines.reshape(3 * docs, share)

    def my_share(vector):
        return lax.dynamic_slice_in_dim(vector, me * share, share, 0)

    exact = functools.partial(jnp.dot, precision=lax.Precision.HIGHEST)
    return (
        output[None],
        logits[None],
        input_grad[None],
        qkv_wgrad[0],
        ends[0],
        qkv_wgrad[1],
        qkv_wgrad[2],
        ends[1],
        proj_wgrad,
        lines[14],
        lines[12],
        lines[13],
        up_wgrad,
        lines[16:20].reshape(-1),
        down_wgrad,
        lines[0],
        lines[1],
        lines[2],
        exact(first_all.T, pre_all),
        my_share(jnp.sum(pre_all, axis=0)),
        exact(pooled_all.T, logit_all),
        jnp.sum(logit_all, axis=0),
    )


def solution(mesh):
    rows, row, part = P("dp", "seq", None), P("seq", None), P("seq")
    per_sequence = P("dp", None)
    in_specs = (
        rows, rows, per_sequence, per_sequence, row, part, row, row, part, row, part, part,
        part, row, part, row, part, part, part, row, part, row, P(),
    )
    out_specs = (
        rows, P("dp", None, None), rows, row, part, row, row, part, row, part, part, part,
        row, part, row, part, part, part, row, part, row, P(),
    )
    return jax.shard_map(
        on_device, mesh=mesh, in_specs=in_specs, out_specs=out_specs, check_vma=False
    )
```

```python
import functools

import jax
import jax.numpy as jnp
from jax import lax
from jax.experimental import pallas as pl
from jax.experimental.pallas import tpu as pltpu
from jax.sharding import PartitionSpec as P

D = 768
HEADS = 12
HEAD_DIM = 64
FF = 3072
CLASSES = 3
PAIR = 2 * HEAD_DIM
ROWS = 256
EPSILON = 1e-06
FAR = -1e30
LIMIT = 56 * 1024 * 1024
F32, BF16 = jnp.float32, jnp.bfloat16

QUERY_B, VALUE_B, PROJ_B, NORM_G, NORM_S, DOWN_B, FINAL_G, FINAL_S, POOL_B, CLASS_W, UP_B = (
    0, 1, 2, 3, 4, 5, 6, 7, 8, 9, 12,
)
TABLE = 16


def swap(value, partner):
    dp, seq = lax.axis_size("dp"), lax.axis_size("seq")
    pairs = []
    for z in range(dp):
        for i in range(seq):
            to_z, to_i = partner(z, i)
            pairs.append((z * seq + i, to_z * seq + to_i))
    return lax.ppermute(value, ("dp", "seq"), pairs)


def along(bit):
    return lambda z, i: (z, i ^ bit)


def is_small():
    return lax.axis_size("seq") == 8 and lax.axis_size("dp") == 4


class Shared:
    def __init__(self, shard, role):
        self.shard, self.role = shard, role

    def near(self):
        role = self.role
        self.one = swap(self.shard, lambda z, i: (z, i ^ (2 if (z + role) % 2 == 0 else 4)))

    def far(self):
        role = self.role
        self.both = swap(self.one, lambda z, i: (z, i ^ (4 if (z + role) % 2 == 0 else 2)))

    def cross(self):
        self.crossed = [swap(block, along(1)) for block in (self.shard, self.one)]

    def cross_both(self):
        self.middle = swap(self.both, along(1))

    def rest(self):
        self.other = swap(self.one, lambda z, i: (z ^ 1, i))

    def rest_direct(self):
        role = self.role
        self.other = swap(self.shard, lambda z, i: (z, i ^ (4 if (z + role) % 2 == 0 else 2)))

    def finish(self):
        last = swap(self.other, along(1))
        return [self.shard, self.one, self.both, self.other, *self.crossed, self.middle, last]

    def owners(self):
        me, z = lax.axis_index("seq"), lax.axis_index("dp")
        near = jnp.where((z + self.role) % 2 == 0, 2, 4)
        owners = [me, me ^ near, me ^ 6, me ^ (6 - near)]
        owners = [owners[k] for k in (0, 1, 2, 3)] + [owners[k] ^ 1 for k in (0, 1, 2, 3)]
        return jnp.stack(owners)


def gather_tokens(tokens):
    if not is_small():
        return [tokens]
    far = swap(tokens, along(6))
    return [tokens, swap(tokens, along(2)), swap(tokens, along(4)), far]


def exchange(pieces):
    return [pieces[0]] + [swap(pieces[s], along(2 * s)) for s in range(1, len(pieces))]


def slot_owners():
    if not is_small():
        return jnp.arange(lax.axis_size("seq"), dtype=jnp.int32)
    return lax.axis_index("seq") ^ jnp.array([0, 2, 4, 6, 1, 3, 5, 7], jnp.int32)


def add(*terms):
    return functools.reduce(jnp.add, [term.astype(F32) for term in terms])


class Scatter:
    def __init__(self, parts):
        self.firsts, self.seconds, self.own = parts[0:2], parts[2:4], parts[4]
        self.comes = [swap(a, along(bit)) for a, bit in zip(self.firsts, (2, 4))]

    def combine(self, *earlier):
        seconds = after(self.seconds, *earlier)
        self.sends = [add(a, come[1]).astype(BF16) for a, come in zip(seconds, self.comes)]

    def turn(self):
        self.lasts = [swap(a, along(bit)) for a, bit in zip(self.sends, (4, 2))]

    def total(self):
        half = self.own.shape[0] // 2
        owns = (self.own[:half], self.own[half:])
        return jnp.concatenate(
            [add(own, come[0], last) for own, come, last in zip(owns, self.comes, self.lasts)]
        )


def after(values, *others):
    return lax.optimization_barrier((values, others))[0]


class SumDp:
    def __init__(self, shard):
        z = lax.axis_index("dp")
        half = shard.shape[0] // 2
        self.low = jnp.logical_or(z == 0, z == 3)
        first, second = shard[:half], shard[half:]
        self.keep = jnp.where(self.low, first, second)
        self.come = swap(
            jnp.where(self.low, second, first).astype(BF16), lambda z, i: (z ^ 1, i)
        )

    def across(self):
        self.pair = add(self.keep, self.come).astype(BF16)
        self.cross = swap(self.pair, lambda z, i: (z ^ 3, i))

    def finish(self):
        self.whole = add(self.pair, self.cross).astype(BF16)
        self.last = swap(self.whole, lambda z, i: (z ^ 1, i))

    def back(self):
        total, come = self.whole, self.last
        low = self.low
        return jnp.concatenate(
            [jnp.where(low, total, come), jnp.where(low, come, total)], axis=0
        ).astype(F32)


def sum_dp(shard):
    if not is_small():
        return lax.psum(shard.astype(BF16), "dp").astype(F32)
    total = SumDp(shard)
    total.across()
    total.finish()
    return total.back()


def sum_seq(value):
    if not is_small():
        return lax.psum(value, "seq")
    for bit in (1, 2, 4):
        value = value + swap(value, along(bit))
    return value


def sum_all(value):
    value = sum_seq(value)
    if not is_small():
        return lax.psum(value, "dp")
    for bit in (1, 2):
        value = value + swap(value, lambda z, i: (z ^ bit, i))
    return value


def stack_dp(value):
    if not is_small():
        return lax.all_gather(value, "dp", axis=0, tiled=True)
    for bit in (1, 2):
        value = jnp.concatenate([value, swap(value, lambda z, i: (z ^ bit, i))], axis=0)
    return value


def dot(left, right, contract=((1,), (0,))):
    return lax.dot_general(left, right, (contract, ((), ())), preferred_element_type=F32)


def call(body, name, micros, **kwargs):
    return pl.pallas_call(
        body,
        name=name,
        cost_estimate=pl.CostEstimate(
            flops=int(micros * 1.1e9), transcendentals=0, bytes_accessed=int(micros * 1e6)
        ),
        compiler_params=pltpu.CompilerParams(vmem_limit_bytes=LIMIT),
        **kwargs,
    )


VMEM = pl.BlockSpec(memory_space=pltpu.VMEM)
ANY = pl.BlockSpec(memory_space=pl.ANY)
SMEM = pl.BlockSpec(memory_space=pltpu.SMEM)


def start(copies):
    for copy in copies:
        copy.start()
    return copies


def wait(copies):
    for copy in copies:
        copy.wait()


def like(arrays):
    return [pltpu.VMEM(a.shape, a.dtype) for a in arrays]


def block_copies(places, line, refs, target, sems, part=None):
    copies = []
    for slot, ref in enumerate(refs):
        source = ref if part is None else ref.at[part]
        rows = source.shape[-2]
        first = pl.multiple_of(places[line, slot] * rows, rows)
        if len(source.shape) == 3:
            place = target.at[:, pl.ds(first, rows), :]
        else:
            place = target.at[pl.ds(first, rows), :]
        copies.append(pltpu.make_async_copy(source, place, sems.at[slot]))
    return start(copies)


def weight_refs(weights):
    return [ref.at[s] for ref in weights for s in range(ref.shape[0])]


def qkv_kernel(blocks, sides, places, *refs):
    tokens, refs = refs[:blocks], refs[blocks:]
    weights, (bias, query, keyval, held, sems) = refs[:sides], refs[sides:]
    wait(block_copies(places, 0, weight_refs(weights), held, sems))
    for s in range(query.shape[0]):
        rows = tokens[s][...]
        keyval[0, s] = dot(rows, held[1]).astype(BF16)
        keyval[1, s] = (dot(rows, held[2]) + bias[1:2]).astype(BF16)
        query[s] = (dot(rows, held[0]) + bias[0:1]).astype(BF16)


def qkv_project(places, tokens, weights, bias):
    slots = len(tokens)
    lanes = weights[0].shape[-1]
    out = jax.ShapeDtypeStruct((slots, ROWS, lanes), BF16)
    pair = jax.ShapeDtypeStruct((2, slots, ROWS, lanes), BF16)
    return call(
        functools.partial(qkv_kernel, len(tokens), len(weights)),
        "qkv",
        5,
        out_shape=(out, pair),
        in_specs=[SMEM] + [VMEM] * len(tokens) + [ANY] * len(weights) + [VMEM],
        out_specs=(VMEM,) * 2,
        scratch_shapes=[
            pltpu.VMEM((3, D, lanes), BF16),
            pltpu.SemaphoreType.DMA((len(weights) * weights[0].shape[0],)),
        ],
    )(places, *tokens, *weights, bias)


def turn_kernel(*refs):
    for s, ref in enumerate(refs[:-1]):
        turn_wide(ref, refs[-1].at[:, s * ROWS : (s + 1) * ROWS])


def turn_tokens(tokens):
    return call(
        turn_kernel,
        "turn_tokens",
        2,
        out_shape=jax.ShapeDtypeStruct((D, len(tokens) * ROWS), BF16),
        in_specs=[VMEM] * len(tokens),
        out_specs=VMEM,
    )(*tokens)


def left_half(shape):
    return lax.broadcasted_iota(jnp.int32, shape, len(shape) - 1) < HEAD_DIM


def split3(value):
    high = value.astype(BF16).astype(F32)
    middle = (value - high).astype(BF16).astype(F32)
    low = (value - high - middle).astype(BF16).astype(F32)
    return high, middle, low


def spread3(value, docs, shape):
    lane = lax.broadcasted_iota(jnp.int32, shape, 1) % HEAD_DIM
    high, middle, low = split3(value)
    return jnp.where(
        lane == docs, high, jnp.where(lane == docs + 1, middle, jnp.where(lane == docs + 2, low, 0.0))
    )


STEP = 512


def eye(size):
    shape = (size, size)
    same = lax.broadcasted_iota(jnp.int32, shape, 0) == lax.broadcasted_iota(jnp.int32, shape, 1)
    return jnp.where(same, 1.0, 0.0).astype(BF16)


def turn(value):
    return dot(eye(value.shape[1]), value, ((1,), (1,))).astype(BF16)


def turn_wide(value, target, first=0):
    for at in range(0, value.shape[1], PAIR * 2):
        block = value[:, at : at + PAIR * 2]
        target[first + at : first + at + block.shape[1]] = turn(block)


def fill_keys(keyvals, feature_k, keys, values, mine):
    at = 0
    for ref in keyvals:
        for index in range(ref.shape[1]):
            rows = slice(at, at + ROWS)
            keys[rows] = jnp.where(mine, ref[0, index], feature_k[at // ROWS])
            values[rows] = jnp.where(mine, ref[1, index], feature_k[at // ROWS])
            at += ROWS


def for_heads(odd, body):
    if not odd:
        body(2)
        return
    tile = pl.program_id(0)
    pl.when(tile < pl.num_programs(0) - 1)(lambda: body(2))
    pl.when(tile == pl.num_programs(0) - 1)(lambda: body(1))


def attend_kernel(sides, docs, odd, *refs):
    query, feature_q, feature_k = refs[:3]
    keyvals = refs[3 : 3 + sides]
    slots, length = feature_q.shape[0], feature_k.shape[0] * ROWS
    rest = refs[3 + sides :]
    wide, total, lows, (keys, values, scores) = rest[0], rest[1], rest[2:-3], rest[-3:]
    left = left_half((ROWS, PAIR))
    sides_of = (left, jnp.logical_not(left))

    def body(heads):
        for head in range(heads):
            fill_keys(keyvals, feature_k, keys.at[head], values.at[head], sides_of[head])
        units = [(slot, head) for slot in range(slots) for head in range(heads)]

        def queries(unit):
            slot, head = unit
            return jnp.where(sides_of[head], query[slot] * 0.125, feature_q[slot])

        def score(unit, number, rows, at, most):
            made = dot(rows, keys[unit[1], at : at + STEP], ((1,), (1,)))
            scores[number % 2, :, at : at + STEP] = made
            for lane in range(0, STEP, PAIR):
                part = made[:, lane : lane + PAIR]
                most = part if most is None else jnp.maximum(most, part)
            return most

        most, rows = None, queries(units[0])
        for at in range(0, length, STEP):
            most = score(units[0], 0, rows, at, most)
        done = {}
        for number, (slot, head) in enumerate(units):
            top = jnp.max(most, axis=1, keepdims=True)
            following = units[number + 1] if number + 1 < len(units) else None
            most, acc = None, 0.0
            if following:
                rows = queries(following)
            for at in range(0, length, STEP):
                if following:
                    most = score(following, number + 1, rows, at, most)
                weights = jnp.exp(scores[number % 2, :, at : at + STEP] - top).astype(BF16)
                acc = acc + dot(weights, values[head, at : at + STEP])
            lane = docs + (HEAD_DIM if head == 0 else 0)
            weight = acc[:, lane : lane + 1]
            done[head] = (acc / weight, top + jnp.log(weight))
            if head == heads - 1:
                result, sums = done[0]
                sums = jnp.broadcast_to(sums, (ROWS, PAIR))
                if heads > 1:
                    result = jnp.where(left, result, done[1][0])
                    sums = jnp.where(left, sums, done[1][1])
                wide[slot] = result
                total[slot] = sums
                lows[slot][...] = result.astype(BF16)

    for_heads(odd, body)


def tile_spec(array, base=0):
    lead = array.shape[:-1]
    return pl.BlockSpec(lead + (PAIR,), lambda tile: (0,) * len(lead) + (tile + base,))


def fixed_spec(array):
    return pl.BlockSpec(array.shape, lambda tile: (0,) * array.ndim)


def attend(query, keyvals, feature_q, feature_k, docs):
    slots, tiles = query.shape[0], query.shape[-1] // PAIR
    wide = jax.ShapeDtypeStruct(query.shape, F32)
    low = jax.ShapeDtypeStruct(wide.shape[1:], BF16)
    length = feature_k.shape[0] * ROWS
    made = call(
        functools.partial(attend_kernel, len(keyvals), docs, slots > 1),
        "attend",
        12,
        grid=(tiles,),
        out_shape=(wide, wide) + (low,) * slots,
        in_specs=[tile_spec(query), fixed_spec(feature_q), fixed_spec(feature_k)]
        + [tile_spec(a) for a in keyvals],
        out_specs=(tile_spec(wide),) * 2 + (tile_spec(low),) * slots,
        scratch_shapes=[
            pltpu.VMEM((2, length, PAIR), BF16),
            pltpu.VMEM((2, length, PAIR), BF16),
            pltpu.VMEM((2, ROWS, length), F32),
        ],
    )(query, feature_q, feature_k, *keyvals)
    return made[0], made[1], list(made[2:])


def attend_back_kernel(sides, docs, heads, *refs):
    query, wide, total, feature_q, feature_k = refs[:5]
    slots, length = feature_q.shape[0], feature_k.shape[0] * ROWS
    grads_in, keyvals = refs[5 : 5 + slots], refs[5 + slots : 5 + slots + sides]
    rest = refs[5 + slots + sides :]
    grad_q, outs = rest[0], rest[1 : 1 + sides]
    keys, values, queries_t, grads_t, query_own, grad_own, softs, slopes, acc = rest[1 + sides :]
    left = left_half((ROWS, PAIR))
    sides_of = (left, jnp.logical_not(left))
    zero = jnp.zeros((ROWS, PAIR), BF16)
    for head in range(heads):
        fill_keys(keyvals, feature_k, keys.at[head], values.at[head], sides_of[head])
    units = [(slot, head) for head in range(heads) for slot in range(slots)]
    for unit, (slot, head) in enumerate(units):
        mine, at = sides_of[head], head * HEAD_DIM
        rows, grads = query[slot] * 0.125, grads_in[slot][...]
        product = jnp.where(mine, grads.astype(F32) * wide[slot], 0.0)
        delta = jnp.sum(product, axis=1, keepdims=True)
        sums = total[slot, :, at : at + 1]
        spare = feature_q[slot].astype(F32) + spread3(-sums, docs, (ROWS, PAIR))
        queries_t[unit] = turn(jnp.where(mine, rows, spare.astype(BF16)))
        spare = spread3(-delta, docs, (ROWS, PAIR)).astype(BF16)
        grads_t[unit] = turn(jnp.where(mine, grads, spare))
        line = slice(unit * ROWS, (unit + 1) * ROWS)
        query_own[line] = jnp.where(mine, rows, zero)
        grad_own[line] = jnp.where(mine, grads, zero)
    per = slots * ROWS
    pieces = [(ref, index) for ref in keyvals for index in range(ref.shape[1])]
    places = [(ref, index) for ref in outs for index in range(ref.shape[1])]
    for step, at in enumerate(range(0, length, STEP)):
        which = step % 2
        for unit, (slot, head) in enumerate(units):
            line = slice(unit * ROWS, (unit + 1) * ROWS)
            soft = jnp.exp(dot(keys[head, at : at + STEP], queries_t[unit]))
            change = dot(values[head, at : at + STEP], grads_t[unit])
            softs[which, :, line] = soft.astype(BF16)
            slopes[which, :, line] = (soft * change).astype(BF16)
        out_v = dot(softs[which], grad_own[...])
        out_k = dot(slopes[which], query_own[...])
        first = at // ROWS
        for k in range(STEP // ROWS):
            ref, index = places[first + k]
            ref[0, index] = out_k[k * ROWS : (k + 1) * ROWS].astype(BF16)
            ref[1, index] = out_v[k * ROWS : (k + 1) * ROWS].astype(BF16)
        key = jnp.concatenate(
            [pieces[first + k][0][0, pieces[first + k][1]] for k in range(STEP // ROWS)], axis=0
        )
        key_t = turn(key)
        for head in range(heads):
            part = slice(head * HEAD_DIM, (head + 1) * HEAD_DIM)
            made = dot(key_t[part], slopes[which, :, head * per : (head + 1) * per])
            if step == 0:
                acc[part] = made
            else:
                acc[part] += made
    if heads == 1:
        acc[HEAD_DIM:] = jnp.zeros((PAIR - HEAD_DIM, per), F32)
    for slot in range(slots):
        made = (acc[:, slot * ROWS : (slot + 1) * ROWS] * 0.125).astype(BF16)
        grad_q[slot] = turn(made)


def attend_back(query, keyvals, grads, wide, total, feature_q, feature_k, docs, base, tiles, single):
    slots, heads = query.shape[0], 1 if single else 2
    length = feature_k.shape[0] * ROWS
    outs = tuple(
        jax.ShapeDtypeStruct(a.shape[:-1] + (tiles * PAIR,), BF16) for a in (query, *keyvals)
    )
    units = slots * heads
    made = call(
        functools.partial(attend_back_kernel, len(keyvals), docs, heads),
        "attend_back",
        8 if single else 15,
        grid=(tiles,),
        out_shape=outs,
        in_specs=[tile_spec(a, base) for a in (query, wide, total)]
        + [fixed_spec(feature_q), fixed_spec(feature_k)]
        + [tile_spec(a, base) for a in (*grads, *keyvals)],
        out_specs=tuple(tile_spec(a) for a in outs),
        scratch_shapes=[
            pltpu.VMEM((heads, length, PAIR), BF16),
            pltpu.VMEM((heads, length, PAIR), BF16),
            pltpu.VMEM((units, PAIR, ROWS), BF16),
            pltpu.VMEM((units, PAIR, ROWS), BF16),
            pltpu.VMEM((units * ROWS, PAIR), BF16),
            pltpu.VMEM((units * ROWS, PAIR), BF16),
            pltpu.VMEM((2, STEP, units * ROWS), BF16),
            pltpu.VMEM((2, STEP, units * ROWS), BF16),
            pltpu.VMEM((PAIR, slots * ROWS), F32),
        ],
    )(query, wide, total, feature_q, feature_k, *grads, *keyvals)
    return made[0], list(made[1:])


def normalise(value):
    centred = value - jnp.mean(value, axis=-1, keepdims=True)
    inverse = lax.rsqrt(jnp.mean(centred * centred, axis=-1, keepdims=True) + EPSILON)
    return centred * inverse, inverse


def norm_back(grad, gain, unit, inverse):
    scaled = grad * gain
    return inverse * (
        scaled
        - jnp.mean(scaled, axis=-1, keepdims=True)
        - unit * jnp.mean(scaled * unit, axis=-1, keepdims=True)
    )


def erf(value):
    value = jnp.clip(value, -3.7439211627767994, 3.7439211627767994)
    square = value * value
    top = 0.00022905065861350646
    for factor in (0.0034082910107109506, 0.050955695062380861, 0.18520832239976145, 1.128379143519084):
        top = top * square + factor
    bottom = -1.1791602954361697e-7
    for factor in (
        0.000023547966471313185, 0.0010179625278914885, 0.014070470171167667,
        0.11098505178285362, 0.49746925110067538, 1.0,
    ):
        bottom = bottom * square + factor
    return value * top / bottom


def column_sum(value):
    return jnp.sum(value, axis=0, keepdims=True)


def early_copies(places, blocks, weights, sems):
    if len(blocks) == 1:
        return [block_copies(places, 1, blocks, weights, sems)] + [[]] * 4
    rows = D // len(blocks)
    copies = []
    for piece in range(5):
        copies.append([])
        for slot, ref in enumerate(blocks):
            first = pl.multiple_of(places[1, slot] * rows, rows)
            copies[piece].append(
                pltpu.make_async_copy(
                    ref.at[piece * rows : (piece + 1) * rows],
                    weights.at[piece, pl.ds(first, rows), :],
                    sems.at[5 * slot + piece],
                )
            )
    return copies


def start_all(groups):
    for copies in groups:
        start(copies)


def late_rows(places, blocks, down, sems):
    rows = FF // len(blocks)
    found = []
    for slot, ref in enumerate(blocks):
        part = slice(slot * rows, (slot + 1) * rows)
        copy = pltpu.make_async_copy(ref.at[:rows], down.at[part], sems.at[slot])
        copy.start()
        found.append((pl.multiple_of(places[2, slot] * rows, rows), part, copy))
    return found


def fill_table(places, smalls, table):
    count, share = smalls.shape[0], D // smalls.shape[0]
    line = lax.broadcasted_iota(jnp.int32, (PAIR, D), 0)
    lane = lax.broadcasted_iota(jnp.int32, (PAIR, D), 1)
    made = 0.0
    for slot in range(count):
        spread = jnp.where(jnp.logical_and(lane == line + places[1, slot] * share, line < share), 1.0, 0.0)
        made = made + dot(smalls[slot, :, :PAIR], spread.astype(BF16))
    table[0:UP_B] = made[0:UP_B]
    for slot in range(count):
        at = places[1, slot]
        table[pl.ds(UP_B + at // 2, 1), pl.ds(pl.multiple_of(at % 2 * 4 * share, 4 * share), 4 * share)] = (
            smalls[slot, UP_B : UP_B + 1, : 4 * share].astype(F32)
        )


def first_kernel(count, slots, groups, places, *refs):
    blocks, refs = refs[:count], refs[count:]
    attended, refs = refs[: slots * groups], refs[slots * groups :]
    tokens, given, refs = refs[0], refs[1] if count == 1 else None, refs[1 if count > 1 else 2 :]
    many = 2 if slots > 1 else 1
    table, unit, inverse, active, slope_out, sides_out = *refs[:5], refs[5 : 5 + many]
    slope, sides = refs[5 + many], refs[6 + many : 6 + 2 * many]
    weights, turned, smalls, sems, small_sems, out_sems = refs[-6:]
    sent = []

    def leave_part(source, target):
        copy = pltpu.make_async_copy(source, target, out_sems.at[len(sent)])
        copy.start()
        sent.append(copy)

    copies = early_copies(places, blocks, weights, sems)
    if count > 1:
        start_all(copies)
        more = start(
            [
                pltpu.make_async_copy(ref.at[5 * D // count :], smalls.at[slot], small_sems.at[slot])
                for slot, ref in enumerate(blocks)
            ]
        )
    width = D // slots

    def row(at):
        return table[at : at + 1]

    core = places[0, 0] % 2 if slots > 1 else 0
    per = width // 2 if slots > 1 else width
    rows_of = [
        jnp.concatenate([a[...] for a in attended[s * groups : (s + 1) * groups]], axis=1)
        for s in range(slots)
    ]
    far = 4 * FF // 8

    for s in range(slots):
        turn_wide(rows_of[s].astype(BF16), turned)
        if slots > 1:
            first = far + (slots + s) * per
            sides[0][first : first + per] = turned[pl.ds(pl.multiple_of(core * per, per), per)]
            sides[1][first : first + per] = turned[pl.ds(pl.multiple_of((1 - core) * per, per), per)]
        else:
            sides[0][FF + D :] = turned[...]
    if count > 1:
        wait(more)
        fill_table(places, smalls, table)
    else:
        table[...] = given[...]
    wait(copies[0])
    residual = tokens[...].astype(F32) + row(PROJ_B)
    for s in range(slots):
        first = pl.multiple_of((places[0, s] // 2) * width, width)
        residual = residual + dot(rows_of[s][:, :width], weights[0, pl.ds(first, width), :])
    first_unit, first_inverse = normalise(residual)
    unit[...] = first_unit
    inverse[...] = first_inverse
    normed = first_unit * row(NORM_G) + row(NORM_S)
    normed_low = normed.astype(BF16)
    turn_wide(normed_low, turned)
    for side, target in enumerate(sides):
        if slots == 1:
            target[FF : FF + D] = turned[...]
            continue
        for s in range(slots):
            first = pl.multiple_of(places[0, side * slots + s] * per, per)
            target[far + s * per : far + (s + 1) * per] = turned[pl.ds(first, per)]
    for side, target in enumerate(sides):
        rows = slice(FF // len(sides), None)
        leave_part(target.at[rows], sides_out[side].at[rows])
    step = 384
    for at in range(0, FF, step):
        line, col = at // D, at % D
        if col == 0:
            wait(copies[1 + line])
        upward = (
            dot(normed_low, weights[1 + line, :, col : col + step])
            + table[UP_B + line : UP_B + line + 1, col : col + step]
        )
        share = 0.5 + 0.5 * erf(upward * 0.7071067811865476)
        bell = jnp.exp(upward * upward * -0.5) * 0.3989422804014327
        active[:, at : at + step] = (upward * share).astype(BF16)
        slope[:, at : at + step] = (share + upward * bell).astype(BF16)
        if (at + step) % D == 0:
            lanes = slice(at + step - D, at + step)
            leave_part(slope.at[:, lanes], slope_out.at[:, lanes])
    for side, target in enumerate(sides):
        if slots == 1:
            turn_wide(active, target)
            leave_part(target.at[:FF], sides_out[side].at[:FF])
            continue
        rows = FF // 8
        for s in range(slots):
            first = pl.multiple_of(places[0, side * slots + s] * rows, rows)
            for at in range(0, rows, PAIR):
                block = active[:, pl.ds(pl.multiple_of(first + at, PAIR), PAIR)]
                target[s * rows + at : s * rows + at + PAIR] = turn(block)
            part = slice(s * rows, (s + 1) * rows)
            leave_part(target.at[part], sides_out[side].at[part])
    wait(sent)


def first_part(places, blocks, attended, tokens, table):
    count = len(blocks)
    slots = 4 if count > 1 else 1
    groups = len(attended) // slots
    given = [table] if count == 1 else []
    shape = jax.ShapeDtypeStruct
    sides = 2 if slots > 1 else 1
    outs = (
        shape((TABLE, D), F32), shape((ROWS, D), F32), shape((ROWS, 1), F32),
        shape((ROWS, FF), BF16), shape((ROWS, FF), BF16),
    )
    outs += (shape(((FF + 2 * D) // sides, ROWS), BF16),) * sides
    made = call(
        functools.partial(first_kernel, count, slots, groups),
        "forward_up",
        11,
        out_shape=outs,
        in_specs=[SMEM] + [ANY] * count + [VMEM] * (slots * groups + 1 + len(given)),
        out_specs=(VMEM,) * 4 + (ANY,) * (1 + sides),
        scratch_shapes=like(outs[4:])
        + [
            pltpu.VMEM((5, D, D), BF16),
            pltpu.VMEM((D, ROWS), BF16),
            pltpu.VMEM((count, TABLE, D), BF16),
            pltpu.SemaphoreType.DMA((5 * count,)),
            pltpu.SemaphoreType.DMA((count,)),
            pltpu.SemaphoreType.DMA((16,)),
        ],
    )(places, *blocks, *attended, tokens, *given)
    return made[:5], made[5:]


def head_kernel(count, docs, places, *refs):
    blocks, refs = refs[:count], refs[count:]
    unit, active, cotangent, table, numbers = refs[:5]
    output, lines, docs_out, grad_second, grad_out = refs[5:10]
    pool, down, sems = refs[10:]
    down_parts = late_rows(places, blocks, down, sems.at[1])
    pool_copies = block_copies(places, 2, blocks, pool, sems.at[0], slice(FF // count, (FF + D) // count))

    def row(at):
        return table[at : at + 1]

    normed = unit[...] * row(NORM_G) + row(NORM_S)
    residual = normed + row(DOWN_B)
    for first, part, copy in down_parts:
        copy.wait()
        residual = residual + dot(active[:, pl.ds(first, FF // count)], down[part])
    last_unit, last_inverse = normalise(residual)
    outcome = last_unit * row(FINAL_G) + row(FINAL_S)
    out_low = outcome.astype(BF16)
    output[...] = out_low

    at_row, label = numbers[:, 0:1], numbers[:, 1:2]
    here = jnp.logical_and(at_row >= 0.0, at_row < float(ROWS))
    line = lax.broadcasted_iota(jnp.int32, (docs, ROWS), 1).astype(F32)
    pick = jnp.where(line == at_row, 1.0, 0.0)
    first_low = dot(pick.astype(BF16), out_low).astype(BF16)
    wait(pool_copies)
    pooled = jnp.tanh(dot(first_low, pool[...]) + row(POOL_B))
    pooled_low = pooled.astype(BF16).astype(F32)
    logits = [
        jnp.sum(pooled_low * row(CLASS_W + c), axis=1, keepdims=True)
        + numbers[:, 2 + c : 3 + c]
        for c in range(CLASSES)
    ]
    top = functools.reduce(jnp.maximum, logits)
    powers = [jnp.exp(logit - top) for logit in logits]
    whole = functools.reduce(jnp.add, powers)
    grads = [powers[c] / whole - jnp.where(label == float(c), 1.0, 0.0) for c in range(CLASSES)]
    grad_pre = functools.reduce(jnp.add, [grads[c] * row(CLASS_W + c) for c in range(CLASSES)])
    grad_pre = grad_pre * (1.0 - pooled * pooled)
    parts = jnp.concatenate(split3(grad_pre), axis=0).astype(BF16)
    made = dot(parts, pool[...], ((1,), (1,)))
    grad_first = made[:docs] + made[docs : 2 * docs] + made[2 * docs :]
    parts = jnp.concatenate(split3(grad_first), axis=0).astype(BF16)
    picks = jnp.concatenate([pick] * 3, axis=0).astype(BF16)
    grad_outcome = cotangent[...] + dot(picks, parts, ((0,), (0,)))
    lane = lax.broadcasted_iota(jnp.int32, (docs, 128), 1)
    small = jnp.zeros((docs, 128), F32)
    for c in range(CLASSES):
        small = jnp.where(lane == c, grads[c], jnp.where(lane == CLASSES + c, logits[c], small))
    docs_out[...] = jnp.where(
        here,
        jnp.concatenate([first_low.astype(F32), pooled_low, grad_pre, small], axis=1),
        0.0,
    )

    grad = norm_back(grad_outcome, row(FINAL_G), last_unit, last_inverse)
    grad_second[...] = grad
    grad_out[...] = grad.astype(BF16)
    lines[0:1] = column_sum(grad)
    lines[1:2] = column_sum(grad_outcome * last_unit)
    lines[2:3] = column_sum(grad_outcome)
    lines[3:8] = jnp.zeros((5, D), F32)


def head_part(places, late, unit, active, cotangent, table, numbers):
    count, docs = len(late), numbers.shape[0]
    shape = jax.ShapeDtypeStruct
    outs = (
        shape((ROWS, D), BF16),
        shape((8, D), F32),
        shape((docs, 3 * D + 128), F32),
        shape((ROWS, D), F32),
        shape((ROWS, D), BF16),
    )
    return call(
        functools.partial(head_kernel, count, docs),
        "head",
        7,
        out_shape=outs,
        in_specs=[SMEM] + [ANY] * count + [VMEM] * 5,
        out_specs=(VMEM,) * len(outs),
        scratch_shapes=[
            pltpu.VMEM((D, D), BF16),
            pltpu.VMEM((FF, D), BF16),
            pltpu.SemaphoreType.DMA((2, count)),
        ],
    )(places, *late, unit, active, cotangent, table, numbers)


def second_kernel(count, places, *refs):
    downs, (grad_down, slope, lines, grad_up, down, sems) = refs[:count], refs[count:]
    grad_low = grad_down[...]
    whole = FF // count
    step = min(whole, 384)
    for first, part, copy in late_rows(places, downs, down, sems):
        copy.wait()
        for at in range(0, whole, step):
            rows = down[part.start + at : part.start + at + step]
            grad = dot(grad_low, rows, ((1,), (1,))).astype(BF16).astype(F32)
            here = pl.multiple_of(first + at, step)
            grad = grad * slope[:, pl.ds(here, step)].astype(F32)
            line, col = here // D, pl.multiple_of(here % D, step)
            lines[pl.ds(line, 1), pl.ds(col, step)] = column_sum(grad)
            grad_up[line, :, pl.ds(col, step)] = grad.astype(BF16)
    lines[4:8] = jnp.zeros((4, D), F32)


def second_part(places, late, grad_down, slope):
    count, shape = len(late), jax.ShapeDtypeStruct
    outs = (shape((8, D), F32), shape((4, ROWS, D), BF16))
    return call(
        functools.partial(second_kernel, count),
        "backward_down",
        5,
        out_shape=outs,
        in_specs=[SMEM] + [ANY] * count + [VMEM] * 2,
        out_specs=(VMEM,) * 2,
        scratch_shapes=[pltpu.VMEM((FF, D), BF16), pltpu.SemaphoreType.DMA((count,))],
    )(places, *late, grad_down, slope)


def third_kernel(count, slots, places, *refs):
    blocks, refs = refs[:count], refs[count:]
    table, grad_second, grad_up, unit, inverse = refs[:5]
    lines, grad_first, grad_out = refs[5:8]
    grad_attended = refs[8 : 8 + slots]
    weights, sems = refs[8 + slots :]
    copies = early_copies(places, blocks, weights, sems)
    if count > 1:
        start_all(copies[1:] + copies[:1])
    else:
        wait(copies[0])
    width = D // slots

    def row(at):
        return table[at : at + 1]

    back = 0.0
    for line in range(4):
        wait(copies[1 + line])
        back = back + dot(grad_up[line], weights[1 + line], ((1,), (1,)))
    grad_normed = grad_second[...] + back.astype(BF16).astype(F32)
    lines[0:4] = jnp.zeros((4, D), F32)
    lines[4:5] = column_sum(grad_normed * unit[...])
    lines[5:6] = column_sum(grad_normed)
    grad = norm_back(grad_normed, row(NORM_G), unit[...], inverse[...])
    grad_first[...] = grad
    lines[6:7] = column_sum(grad)
    lines[7:8] = jnp.zeros((1, D), F32)
    grad_low = grad.astype(BF16)
    grad_out[...] = grad_low
    if count > 1:
        wait(copies[0])
    for s in range(slots):
        first = pl.multiple_of((places[0, s] // 2) * width, width)
        made = dot(grad_low, weights[0, pl.ds(first, width), :], ((1,), (1,))).astype(BF16)
        if width < grad_attended[s].shape[1]:
            grad_attended[s][:, PAIR:] = jnp.zeros((ROWS, PAIR), BF16)
        grad_attended[s][:, :width] = made


def third_part(places, blocks, table, grad_second, grad_up, unit, inverse, slots, lanes):
    count = len(blocks)
    shape = jax.ShapeDtypeStruct
    outs = (shape((8, D), F32), shape((ROWS, D), F32), shape((ROWS, D), BF16))
    outs += (shape((ROWS, lanes), BF16),) * slots
    made = call(
        functools.partial(third_kernel, count, slots),
        "backward_up",
        7,
        out_shape=outs,
        in_specs=[SMEM] + [ANY] * count + [VMEM] * 5,
        out_specs=(VMEM,) * len(outs),
        scratch_shapes=[pltpu.VMEM((5, D, D), BF16), pltpu.SemaphoreType.DMA((5 * count,))],
    )(places, *blocks, table, grad_second, grad_up, unit, inverse)
    return made[:3], list(made[3:])


def wgrad_outs(slots, rows):
    shape = jax.ShapeDtypeStruct
    if slots == 1:
        return (shape((1, rows, D), BF16),)
    half = rows // 2
    return (shape((2, half, D), BF16),) * 2 + (shape((half, D), BF16),) * 2 + (shape((rows, D), F32),)


def put_slot(outs, s, first, value):
    if len(outs) == 1:
        outs[0][0, first : first + value.shape[0]] = value.astype(BF16)
        return
    if s == 0:
        outs[4][first : first + value.shape[0]] = value
        return
    half = outs[2].shape[0]
    for k, order in enumerate(((1, 3, 2), (2, 3, 1))):
        low, high = max(first, k * half), min(first + value.shape[0], (k + 1) * half)
        if low >= high:
            continue
        rows, part = slice(low - k * half, high - k * half), value[low - first : high - first]
        if s == order[2]:
            outs[2 + k][rows] = part.astype(BF16)
        else:
            outs[k][order.index(s), rows] = part.astype(BF16)


def gradient_call(body, name, micros, ins, outs, scratch, waits):
    return call(
        body,
        name,
        micros,
        out_shape=outs,
        in_specs=[ANY] * len(ins),
        out_specs=(ANY,) * len(outs),
        scratch_shapes=[pltpu.VMEM(a.shape, a.dtype) for a in outs]
        + scratch
        + [pltpu.SemaphoreType.DMA((waits,)), pltpu.SemaphoreType.DMA((len(outs),))],
    )(*ins)


def leave(kept, outs, sems, which):
    return start([pltpu.make_async_copy(kept[k], outs[k], sems.at[k]) for k in which])


def down_kernel(slots, sides, *refs):
    lefts, rights, refs = refs[:sides], refs[sides : 2 * sides], refs[2 * sides :]
    count = 5 if slots > 1 else 1
    outs, kept, (left, right, sems, out_sems) = refs[:count], refs[count : 2 * count], refs[-4:]
    rows = FF // sides // slots
    step = min(rows, 384)
    copies = {}
    for side in range(sides):
        copies[side] = pltpu.make_async_copy(rights[side], right.at[side], sems.at[side])
    order = (3, 1, 2, 0) if slots > 1 else (0,)
    for s in order:
        for side in range(sides):
            part = slice(s * rows, (s + 1) * rows)
            copies[s, side] = pltpu.make_async_copy(
                lefts[side].at[part], left.at[side, part], sems.at[sides + s * sides + side]
            )
    start(copies.values())
    wait([copies[side] for side in range(sides)])
    sent = []
    for s in order:
        wait([copies[s, side] for side in range(sides)])
        for at in range(0, rows, step):
            first = s * rows + at
            made = dot(left[0, first : first + step], right[0])
            for side in range(1, sides):
                made = made + dot(left[side, first : first + step], right[side])
            put_slot(kept, s, at, made)
        if slots > 1:
            sent += leave(kept, outs, out_sems, {3: (), 1: (0, 3), 2: (1, 2), 0: (4,)}[s])
        else:
            sent += leave(kept, outs, out_sems, (0,))
    wait(sent)


def down_gradient(lefts, rights, slots):
    sides = len(lefts)
    outs = wgrad_outs(slots, FF // sides // slots)
    scratch = [pltpu.VMEM((sides, FF // sides, ROWS), BF16), pltpu.VMEM((sides, ROWS, D), BF16)]
    body = functools.partial(down_kernel, slots, sides)
    return gradient_call(
        body, "down_gradient", 3, (*lefts, *rights), outs, scratch, sides * (slots + 1)
    )


def up_kernel(slots, sides, *refs):
    lefts, ups, projs, refs = *(refs[k * sides : (k + 1) * sides] for k in range(3)), refs[3 * sides :]
    count = 5 if slots > 1 else 1
    outs, kept, (left, right, sems, out_sems) = refs[:count], refs[count : 2 * count], refs[-4:]
    whole = D // sides
    rows = whole // slots
    copies = {}
    for side in range(sides):
        copies[side] = pltpu.make_async_copy(
            lefts[side].at[FF // sides :], left.at[side], sems.at[side]
        )
    for line in range(5):
        for side in range(sides):
            copies[line, side] = pltpu.make_async_copy(
                ups[side].at[line] if line < 4 else projs[side],
                right.at[side, line],
                sems.at[sides + line * sides + side],
            )
    start(copies.values())
    wait([copies[side] for side in range(sides)])
    sent = []
    for line in range(5):
        wait([copies[line, side] for side in range(sides)])
        at = 0 if line < 4 else whole
        made = dot(left[0, at : at + whole], right[0, line])
        for side in range(1, sides):
            made = made + dot(left[side, at : at + whole], right[side, line])
        for s in range(slots):
            put_slot(kept, s, line * rows, made[s * rows : (s + 1) * rows])
        if slots > 1:
            sent += leave(kept, outs, out_sems, {2: (0, 2), 4: (1, 3, 4)}.get(line, ()))
        elif line == 4:
            sent += leave(kept, outs, out_sems, (0,))
    wait(sent)


def up_gradient(lefts, ups, projs, slots):
    sides = len(lefts)
    outs = wgrad_outs(slots, 5 * D // sides // slots)
    scratch = [pltpu.VMEM((sides, 2 * D // sides, ROWS), BF16), pltpu.VMEM((sides, 5, ROWS, D), BF16)]
    body = functools.partial(up_kernel, slots, sides)
    return gradient_call(body, "up_gradient", 4, (*lefts, *ups, *projs), outs, scratch, 6 * sides)


def input_kernel(groups, sides, places, *refs):
    turned, refs = refs[:sides], refs[sides:]
    grad_qs, refs = refs[:groups], refs[groups:]
    changes, refs = refs[: groups * sides], refs[groups * sides :]
    outs, (made, lines, grads, sems) = refs[:-4], refs[-4:]
    rows = turned[0].shape[1]
    count = outs[0].shape[0] // 3 // (D // (8 if sides > 1 else 1))
    share = D // (8 if sides > 1 else 1)
    sums, sends = [], []
    for k in range(3):
        total, line = None, None
        for side in range(sides if k else 1):
            lane = 0
            for group in range(groups):
                source = changes[group * sides + side].at[k - 1] if k else grad_qs[group]
                lanes = slice(lane, lane + source.shape[2])
                lane = lanes.stop
                grads[:, lanes] = source[...].reshape(rows, source.shape[2])
            part = dot(turned[side][...], grads[...])
            total = part if total is None else total + part
            if k != 1:
                part = dot(jnp.ones((8, rows), BF16), grads[...])
                line = part if line is None else line + part
        made[k] = total.astype(BF16)
        if k != 1:
            sums.append(line[:1])
        for side, out in enumerate(outs):
            for s in range(count):
                first = pl.multiple_of(places[0, side * count + s] * share, share)
                target = out.at[(3 * s + k) * share : (3 * s + k + 1) * share]
                sends.append((made.at[k, pl.ds(first, share), :], target))
                pltpu.make_async_copy(*sends[-1], sems.at[len(sends) - 1]).start()
    lines[...] = jnp.concatenate([*sums, jnp.zeros((14, lines.shape[1]), F32)], axis=0).astype(BF16)
    for out in outs:
        sends.append((lines, out.at[3 * count * share :]))
        pltpu.make_async_copy(*sends[-1], sems.at[len(sends) - 1]).start()
    wait([pltpu.make_async_copy(a, b, sems.at[k]) for k, (a, b) in enumerate(sends)])


def input_gradient(places, turned, grad_qs, changes, slots):
    lanes = sum(grad.shape[2] for grad in grad_qs)
    sides, groups = len(turned), len(grad_qs)
    out = jax.ShapeDtypeStruct((3 * D // sides + 16, lanes), BF16)
    made = call(
        functools.partial(input_kernel, groups, sides),
        "input_weights",
        5,
        out_shape=(out,) * sides,
        in_specs=[SMEM] + [VMEM] * (sides + groups + groups * sides),
        out_specs=(ANY,) * sides,
        scratch_shapes=[
            pltpu.VMEM((3, D, lanes), BF16),
            pltpu.VMEM((16, lanes), BF16),
            pltpu.VMEM((turned[0].shape[1], lanes), BF16),
            pltpu.SemaphoreType.DMA((sides * (3 * slots + 1),)),
        ],
    )(places, *turned, *grad_qs, *changes)
    return list(made)


def last_kernel(sides, groups, parts, places, *refs):
    weights, refs = refs[:sides], refs[sides:]
    grad_qs, refs = refs[:groups], refs[groups:]
    changes, refs = refs[: groups * parts], refs[groups * parts :]
    grad_first, own, outs = *refs[:2], refs[2:-3]
    held, grads, sems = refs[-3:]
    slots = grad_qs[0].shape[0]
    copies = block_copies(places, 0, weight_refs(weights), held, sems)
    for s in range(slots):
        rows = slice(s * ROWS, (s + 1) * ROWS)
        lane = 0
        for group in range(groups):
            lanes = slice(lane, lane + grad_qs[group].shape[2])
            lane = lanes.stop
            grads[0, rows, lanes] = grad_qs[group][s]
            for k in range(2):
                total = changes[group * parts][k, s].astype(F32)
                for change in changes[group * parts + 1 : (group + 1) * parts]:
                    total = total + change[k, s].astype(F32)
                grads[1 + k, rows, lanes] = total.astype(BF16)
    wait(copies)

    def partial(s):
        rows = slice(s * ROWS, (s + 1) * ROWS)
        total = dot(grads[0, rows], held[0], ((1,), (1,)))
        for k in range(1, 3):
            total = total + dot(grads[k, rows], held[k], ((1,), (1,)))
        return total

    for s in range(1, slots):
        outs[s - 1][...] = partial(s).astype(BF16)
    own[...] = grad_first[...] + partial(0)


def last_part(places, weights, grad_qs, changes, grad_first):
    slots, lanes = grad_qs[0].shape[0], sum(grad.shape[2] for grad in grad_qs)
    groups, parts = len(grad_qs), len(changes) // len(grad_qs)
    sides, shape = len(weights), jax.ShapeDtypeStruct
    outs = (shape((ROWS, D), F32),) + (shape((ROWS, D), BF16),) * (slots - 1)
    blocks = sides * weights[0].shape[0]
    made = call(
        functools.partial(last_kernel, sides, groups, parts),
        "input_gradients",
        5,
        out_shape=outs,
        in_specs=[SMEM] + [ANY] * sides + [VMEM] * (1 + groups + len(changes)),
        out_specs=(VMEM,) * len(outs),
        scratch_shapes=[
            pltpu.VMEM((3, D, lanes), BF16),
            pltpu.VMEM((3, slots * ROWS, lanes), BF16),
            pltpu.SemaphoreType.DMA((blocks,)),
        ],
    )(places, *weights, *grad_qs, *changes, grad_first)
    return made[0], made[1:]


def whole_scatter(part, pieces):
    seq = lax.axis_size("seq")
    rows = part.shape[1] // pieces // seq
    part = part.reshape(pieces, seq, rows, D).transpose(1, 0, 2, 3)
    part = part.reshape(seq, pieces * rows, D)
    return lax.psum_scatter(part, "seq", scatter_dimension=0, tiled=True)[0].astype(F32)


def by_chip(pieces):
    me = lax.axis_index("seq")
    for bit in (1, 2):
        odd = (me & (2 * bit)) != 0
        pieces = [jnp.where(odd, pieces[s ^ bit], pieces[s]) for s in range(len(pieces))]
    return pieces


def features(positions, starts):
    docs = starts.shape[0]
    segment = jnp.sum((positions[..., None] >= starts).astype(jnp.int32), axis=-1) - 1
    lane = jnp.arange(PAIR, dtype=jnp.int32) % HEAD_DIM
    own = segment[..., None] == lane
    return own, lane, docs


def on_device(
    inputs,
    cotangent,
    doc_lengths,
    doc_labels,
    query_weight,
    query_bias,
    key_weight,
    value_weight,
    value_bias,
    proj_weight,
    proj_bias,
    norm_gain,
    norm_shift,
    up_weight,
    up_bias,
    down_weight,
    down_bias,
    final_gain,
    final_shift,
    pool_weight,
    pool_bias,
    class_weight,
    class_bias,
):
    me = lax.axis_index("seq")
    tokens = inputs[0]
    share = query_bias.shape[0]
    lengths = doc_lengths[0]
    docs = lengths.shape[0]
    order = jnp.arange(docs, dtype=jnp.int32)
    starts = jnp.sum(jnp.where(order[None, :] < order[:, None], lengths[None, :], 0), axis=1)

    numbers = jnp.concatenate(
        [
            (starts - me * ROWS)[:, None].astype(F32),
            doc_labels[0][:, None].astype(F32),
            jnp.broadcast_to(class_bias.astype(F32), (docs, CLASSES)),
            jnp.zeros((docs, PAIR - 2 - CLASSES), F32),
        ],
        axis=1,
    )

    small_mesh = is_small()
    slot_list = slot_owners()
    chip, core = me // 2, me % 2
    width = D // 4
    slots = 4 if small_mesh else 1
    line = jnp.arange(ROWS, dtype=jnp.int32)
    mine = slot_list[:slots] if small_mesh else me[None]
    own, lane, _ = features(mine[:, None] * ROWS + line, starts)
    feature_q = jnp.where(own, FAR, 0.0).astype(BF16)
    own, lane, _ = features(slot_list[:, None] * ROWS + line, starts)
    feature_k = jnp.where(
        lane < docs, jnp.where(own, 0.0, 1.0), jnp.where(lane < docs + 3, 1.0, 0.0)
    ).astype(BF16)

    matrices = jnp.stack([query_weight, key_weight, value_weight])
    bias = jnp.stack([query_bias, value_bias])
    small = jnp.stack(
        [
            query_bias, value_bias, proj_bias, norm_gain, norm_shift, down_bias,
            final_gain, final_shift, pool_bias, *class_weight.T,
        ]
    )
    wide = me * up_bias.shape[0]
    up_pieces = up_weight.reshape(share, 4, D).transpose(1, 0, 2)
    proj_up = jnp.concatenate([proj_weight[None], up_pieces])
    down_pool = jnp.concatenate([down_weight, pool_weight])
    if small_mesh:
        pieces = [
            lax.dynamic_slice_in_dim(matrices, (chip ^ s) * width, width, 2) for s in range(4)
        ]
        token_blocks = gather_tokens(tokens)
        own = jnp.stack(exchange(pieces))
        own = jnp.pad(own, ((0, 0), (0, 0), (0, 0), (0, PAIR * 2 - width)))
        small = jnp.pad(small, ((0, TABLE - small.shape[0]), (0, D - share)))
        small = lax.dynamic_update_slice(small, up_bias[None], (UP_B, 0))
        early = Shared(jnp.concatenate([proj_up.reshape(5 * share, D), small]), 0)
        late = Shared(down_pool, 1)
        places = jnp.stack([slot_list, early.owners(), late.owners()])
        come = swap(bias, along(1))
        bias = jnp.where(
            core == 0, jnp.concatenate([bias, come], axis=1), jnp.concatenate([come, bias], axis=1)
        )
        bias = jnp.pad(bias, ((0, 0), (0, PAIR * 2 - width))).astype(F32)
        own = after(own, feature_q, feature_k, places, bias, numbers, token_blocks[1:3])
        weights = [own, swap(own, along(1))]
        early.near()
        late.near()
        table = None
    else:
        token_blocks = [tokens]
        weights = [lax.all_gather(matrices, "seq", axis=1, tiled=True)[None]]
        table = jnp.zeros((TABLE, D), BF16)
        table = lax.dynamic_update_slice(table, small, (0, me * share))
        table = lax.dynamic_update_slice(table, up_bias[None], (UP_B + wide // D, wide % D))
        table = sum_seq(table).astype(F32)
        bias = table[:2]
        blocks = [lax.all_gather(proj_up, "seq", axis=1, tiled=True)]
        whole = lax.all_gather(down_pool, "seq", axis=0)
        whole = [whole[:, : 4 * share].reshape(FF, D), whole[:, 4 * share :].reshape(D, D)]
        late_blocks = [jnp.concatenate(whole)]
        places = jnp.zeros((3, 1), jnp.int32)

    query, keyval = qkv_project(places, token_blocks, weights, bias)
    tokens_t = turn_tokens(after(token_blocks, query))
    if small_mesh:
        early.one, late.one = after((early.one, late.one), tokens_t)
        keyval = after(keyval, early.one, late.one)
        keyvals = [keyval, swap(keyval, along(1))]
        early.far()
        early.rest()
        early.cross()
        late.far()
    else:
        keyvals = [lax.all_gather(keyval, "seq", axis=1, tiled=True)]
    attended, total, lows = attend(query, keyvals, feature_q, feature_k, docs)
    if small_mesh:
        lows, tokens_t, early.both, early.other, early.crossed = after(
            (lows, tokens_t, early.both, early.other, early.crossed), lows
        )
        early.cross_both()
        blocks = early.finish()
    else:
        tokens_t = [tokens_t]
    lows = exchange(lows)
    if small_mesh:
        late.shard, late.one, late.both = after((late.shard, late.one, late.both), lows)
        late.rest_direct()
        late.cross()
        late.cross_both()

    made, turned = first_part(places, blocks, lows, tokens, table)
    table, unit, inverse, active, slope = made
    if small_mesh:
        late.other, late.crossed, late.middle, tokens_t, turned = after(
            (late.other, late.crossed, late.middle, tokens_t, turned), active
        )
        late_blocks = late.finish()
        tokens_t = [tokens_t, swap(tokens_t, along(1))]
    output, lines_one, docs_out, grad_second, grad_down = head_part(
        places, late_blocks, unit, active, cotangent[0], table, numbers
    )

    def both(keep, *away):
        return [keep] + [swap(a, along(1)) for a in away]

    def own_and_other(value):
        return both(value, *([value] if small_mesh else []))

    turned = both(*turned)
    down_parts = down_gradient(turned, own_and_other(grad_down), slots)
    if small_mesh:
        down_sum = Scatter(down_parts)
    grad_down = after(grad_down, down_parts, tokens_t)
    lines_two, grad_up = second_part(places, late_blocks, grad_down, slope)
    grad_second = after(grad_second, grad_up)
    made, grads = third_part(
        places, blocks, table, grad_second, grad_up, unit, inverse, slots, query.shape[-1]
    )
    lines_three, grad_first, grad_proj = made
    lines_two = lines_two + lines_three
    pack = jnp.concatenate([docs_out, lines_one, lines_two], axis=1)
    ups = own_and_other(grad_up)
    if small_mesh:
        grad_proj, grads = after((grad_proj, grads), down_sum.comes)
        down_sum.combine()
        down_sum.turn()
        grads = exchange(grads)
    up_parts = up_gradient(turned, ups, own_and_other(grad_proj), slots)

    back = functools.partial(
        attend_back, keyvals=keyvals,
        feature_q=feature_q, feature_k=feature_k, docs=docs,
    )
    if small_mesh:
        up_parts, pack, grads, down_sum.lasts = after(
            (up_parts, pack, grads, down_sum.lasts), up_parts
        )
        down_dp = SumDp(down_sum.total())
        up_sum = Scatter(up_parts)
        come = swap(pack, along(1))
        grad_q, changes = back(
            query, grads=grads, wide=attended, total=total, base=0, tiles=1, single=False
        )
        changes, pack, come, up_sum.seconds, down_dp.come = after(
            (changes, pack, come, up_sum.seconds, down_dp.come), grad_q, up_sum.comes
        )
        grad_qs, partial, changes = [grad_q], list(changes), both(*changes)
        up_sum.combine()
        up_sum.turn()
        down_dp.across()
        pack = pack + come
        come = swap(pack, along(2))
        rows = after(query, grad_q, up_sum.sends, down_dp.pair, pack)
        grad_q, more = back(
            rows, grads=grads, wide=attended, total=total, base=1, tiles=1, single=True
        )
        more, pack, come, up_sum.lasts, down_dp.cross = after(
            (more, pack, come, up_sum.lasts, down_dp.cross), grad_q
        )
        grad_qs, partial = grad_qs + [grad_q], partial + list(more)
        changes = changes + both(*more)
        up_dp = SumDp(up_sum.total())
        pack = pack + come
        come = swap(pack, along(4))
    else:
        grad_q, changes = back(
            query, grads=grads, wide=attended, total=total,
            base=0, tiles=HEADS // 2, single=False,
        )
        grad_qs, partial = [grad_q], changes
        change = changes[0].transpose(1, 0, 2, 3)
        change = lax.psum_scatter(change, "seq", scatter_dimension=0, tiled=True)
        changes = [change.transpose(1, 0, 2, 3)]
        partial = changes
        pack = sum_seq(pack)
    def own_shares(pack):
        at = me * share
        lines = pack[:, 3 * D + PAIR :].reshape(docs, 2, D).transpose(1, 0, 2).reshape(2 * docs, D)
        own = jnp.concatenate(
            [
                lax.dynamic_slice_in_dim(lines, at, share, 1),
                lax.dynamic_slice_in_dim(lines[8:12].reshape(-1), wide, 4 * share, 0).reshape(4, share),
                jnp.zeros((4, share), F32),
            ]
        )
        parts = [
            pack[:, 2 * D : 3 * D],
            lax.dynamic_slice_in_dim(pack, at, share, 1),
            lax.dynamic_slice_in_dim(pack, D + at, share, 1),
            pack[:, 3 * D : 3 * D + PAIR],
            own.reshape(docs, 3 * share),
        ]
        logits = pack[:, 3 * D + CLASSES : 3 * D + 2 * CLASSES]
        return jnp.concatenate(parts, axis=1), logits

    def from_docs(every_doc):
        pre_all, first_all, pooled_all = (
            every_doc[:, at : at + size] for at, size in ((0, D), (D, share), (D + share, share))
        )
        logit_all = every_doc[:, D + 2 * share : D + 2 * share + CLASSES]
        lines = jnp.sum(every_doc[:, D + 2 * share + PAIR :].reshape(-1, docs, 3 * share), axis=0)
        exact = functools.partial(jnp.dot, precision=lax.Precision.HIGHEST)
        pool_bgrad = lax.dynamic_slice_in_dim(jnp.sum(pre_all, axis=0), me * share, share, 0)
        return (
            lines.reshape(3 * docs, share),
            (exact(first_all.T, pre_all), pool_bgrad),
            (exact(pooled_all.T, logit_all), jnp.sum(logit_all, axis=0)),
        )

    qkv_parts = input_gradient(places, tokens_t, grad_qs, partial, slots)
    if small_mesh:
        qkv_parts, changes, pack, come, up_dp.come, down_dp.cross = after(
            (qkv_parts, changes, pack, come, up_dp.come, down_dp.cross), qkv_parts
        )
        keep, away = both(*qkv_parts)
        up_dp.across()
        away = after(away, up_dp.pair)
        rows = 3 * share
        pieces = [
            add(keep[s * rows : (s + 1) * rows, :width], away[s * rows : (s + 1) * rows, :width])
            for s in range(4)
        ]
        ends = add(keep[4 * rows : 4 * rows + 2], away[4 * rows : 4 * rows + 2])
        pieces = [piece.astype(BF16) for piece in pieces]
        pack, come = after((pack, come), pieces)
        pieces = exchange(pieces)
        pack, logits = own_shares(pack + come)
        come = swap(pack, lambda z, i: (z ^ 1, i))
        changes = after(changes, pieces[0], pack, ends)
    input_grad, sums = last_part(places, weights, grad_qs, changes, grad_first)

    if small_mesh:
        pieces, down_dp.cross, pack, come = after(
            (pieces, down_dp.cross, pack, come), input_grad
        )
        qkv_wgrad = jnp.concatenate(by_chip(pieces), axis=1)
        ends = jnp.pad(
            lax.dynamic_slice_in_dim(ends, core * share, share, 1), ((0, 30), (0, D - share))
        )
        qkv_dp = SumDp(jnp.concatenate([qkv_wgrad.astype(F32), ends]))
        pack = jnp.concatenate([pack, come], axis=0)
        come = swap(pack, lambda z, i: (z ^ 2, i))
        down_dp.finish()
        qkv_dp.come, up_dp.cross, sums, input_grad = after(
            (qkv_dp.come, up_dp.cross, sums, input_grad), qkv_dp.come
        )
        qkv_dp.across()
        sums, input_grad = after((sums, input_grad), qkv_dp.pair)
        sums = exchange([input_grad, *sums])
        up_dp.finish()
        of_docs = from_docs(jnp.concatenate([pack, come], axis=0))
        down_wgrad = down_dp.back()
        qkv_dp.cross, of_docs, down_wgrad = after((qkv_dp.cross, of_docs, down_wgrad), qkv_dp.cross)
        qkv_dp.finish()
        up_wgrad = up_dp.back()
        input_grad = add(*sums)
        qkv_wgrad = qkv_dp.back()
    else:
        qkv_wgrad = whole_scatter(qkv_parts[0][None, : 3 * D], 3)
        ends = sum_seq(qkv_parts[0][3 * D : 3 * D + 2].astype(F32))
        ends = lax.dynamic_slice_in_dim(ends, me * share, share, 1)
        qkv_wgrad = sum_dp(jnp.concatenate([qkv_wgrad, jnp.pad(ends, ((0, 30), (0, D - share)))]))
        down_wgrad = sum_dp(whole_scatter(down_parts[0], 1))
        up_wgrad = sum_dp(whole_scatter(up_parts[0], 5))
    proj_wgrad = up_wgrad[4 * share :]
    up_wgrad = up_wgrad[: 4 * share].reshape(4, share, D).transpose(1, 0, 2).reshape(share, FF)
    ends = qkv_wgrad[3 * share : 3 * share + 2, :share]
    qkv_wgrad = qkv_wgrad[: 3 * share].reshape(3, share, D)
    if not small_mesh:
        pack, logits = own_shares(pack)
        of_docs = from_docs(stack_dp(pack))
    lines, of_pool, of_class = of_docs
    return (
        output[None],
        logits[None],
        input_grad[None],
        qkv_wgrad[0],
        ends[0],
        qkv_wgrad[1],
        qkv_wgrad[2],
        ends[1],
        proj_wgrad,
        lines[14],
        lines[12],
        lines[13],
        up_wgrad,
        lines[16:20].reshape(-1),
        down_wgrad,
        lines[0],
        lines[1],
        lines[2],
        *of_pool,
        *of_class,
    )


def solution(mesh):
    rows, row, part = P("dp", "seq", None), P("seq", None), P("seq")
    per_sequence = P("dp", None)
    in_specs = (
        rows, rows, per_sequence, per_sequence, row, part, row, row, part, row, part, part,
        part, row, part, row, part, part, part, row, part, row, P(),
    )
    out_specs = (
        rows, P("dp", None, None), rows, row, part, row, row, part, row, part, part, part,
        row, part, row, part, part, part, row, part, row, P(),
    )
    return jax.shard_map(
        on_device, mesh=mesh, in_specs=in_specs, out_specs=out_specs, check_vma=False
    )
```

```python
import functools

import jax
import jax.numpy as jnp
from jax import lax
from jax.experimental import pallas as pl
from jax.experimental.pallas import tpu as pltpu
from jax.sharding import PartitionSpec as P

D = 768
HEADS = 12
HEAD_DIM = 64
FF = 3072
CLASSES = 3
PAIR = 2 * HEAD_DIM
ROWS = 256
EPSILON = 1e-06
FAR = -1e30
LIMIT = 56 * 1024 * 1024
F32, BF16 = jnp.float32, jnp.bfloat16

QUERY_B, VALUE_B, PROJ_B, NORM_G, NORM_S, DOWN_B, FINAL_G, FINAL_S, POOL_B, CLASS_W, UP_B = (
    0, 1, 2, 3, 4, 5, 6, 7, 8, 9, 12,
)
TABLE = 16


def swap(value, partner):
    dp, seq = lax.axis_size("dp"), lax.axis_size("seq")
    pairs = []
    for z in range(dp):
        for i in range(seq):
            to_z, to_i = partner(z, i)
            pairs.append((z * seq + i, to_z * seq + to_i))
    return lax.ppermute(value, ("dp", "seq"), pairs)


def along(bit):
    return lambda z, i: (z, i ^ bit)


def is_small():
    return lax.axis_size("seq") == 8 and lax.axis_size("dp") == 4


class Shared:
    def __init__(self, shard, role):
        self.shard, self.role = shard, role

    def near(self):
        role = self.role
        self.one = swap(self.shard, lambda z, i: (z, i ^ (2 if (z + role) % 2 == 0 else 4)))

    def far(self):
        role = self.role
        self.both = swap(self.one, lambda z, i: (z, i ^ (4 if (z + role) % 2 == 0 else 2)))

    def cross(self):
        self.crossed = [swap(block, along(1)) for block in (self.shard, self.one)]

    def cross_both(self):
        self.middle = swap(self.both, along(1))

    def rest(self):
        self.other = swap(self.one, lambda z, i: (z ^ 1, i))

    def rest_direct(self):
        role = self.role
        self.other = swap(self.shard, lambda z, i: (z, i ^ (4 if (z + role) % 2 == 0 else 2)))

    def finish(self):
        last = swap(self.other, along(1))
        return [self.shard, self.one, self.both, self.other, *self.crossed, self.middle, last]

    def owners(self):
        me, z = lax.axis_index("seq"), lax.axis_index("dp")
        near = jnp.where((z + self.role) % 2 == 0, 2, 4)
        owners = [me, me ^ near, me ^ 6, me ^ (6 - near)]
        owners = [owners[k] for k in (0, 1, 2, 3)] + [owners[k] ^ 1 for k in (0, 1, 2, 3)]
        return jnp.stack(owners)


def gather_tokens(tokens):
    if not is_small():
        return [tokens]
    far = swap(tokens, along(6))
    return [tokens, swap(tokens, along(2)), swap(tokens, along(4)), far]


def exchange(pieces):
    return [pieces[0]] + [swap(pieces[s], along(2 * s)) for s in range(1, len(pieces))]


def slot_owners():
    if not is_small():
        return jnp.arange(lax.axis_size("seq"), dtype=jnp.int32)
    return lax.axis_index("seq") ^ jnp.array([0, 2, 4, 6, 1, 3, 5, 7], jnp.int32)


def add(*terms):
    return functools.reduce(jnp.add, [term.astype(F32) for term in terms])


class Scatter:
    def __init__(self, parts):
        self.firsts, self.seconds, self.own = parts[0:2], parts[2:4], parts[4]
        self.comes = [swap(a, along(bit)) for a, bit in zip(self.firsts, (2, 4))]

    def combine(self, *earlier):
        seconds = after(self.seconds, *earlier)
        self.sends = [add(a, come[1]).astype(BF16) for a, come in zip(seconds, self.comes)]

    def turn(self):
        self.lasts = [swap(a, along(bit)) for a, bit in zip(self.sends, (4, 2))]

    def total(self):
        half = self.own.shape[0] // 2
        owns = (self.own[:half], self.own[half:])
        return jnp.concatenate(
            [add(own, come[0], last) for own, come, last in zip(owns, self.comes, self.lasts)]
        )


def after(values, *others):
    return lax.optimization_barrier((values, others))[0]


class SumDp:
    def __init__(self, shard):
        z = lax.axis_index("dp")
        half = shard.shape[0] // 2
        self.low = jnp.logical_or(z == 0, z == 3)
        first, second = shard[:half], shard[half:]
        self.keep = jnp.where(self.low, first, second)
        self.come = swap(
            jnp.where(self.low, second, first).astype(BF16), lambda z, i: (z ^ 1, i)
        )

    def across(self):
        self.pair = add(self.keep, self.come).astype(BF16)
        self.cross = swap(self.pair, lambda z, i: (z ^ 3, i))

    def finish(self):
        self.whole = add(self.pair, self.cross).astype(BF16)
        self.last = swap(self.whole, lambda z, i: (z ^ 1, i))

    def back(self):
        total, come = self.whole, self.last
        low = self.low
        return jnp.concatenate(
            [jnp.where(low, total, come), jnp.where(low, come, total)], axis=0
        ).astype(F32)


def sum_dp(shard):
    if not is_small():
        return lax.psum(shard.astype(BF16), "dp").astype(F32)
    total = SumDp(shard)
    total.across()
    total.finish()
    return total.back()


def sum_seq(value):
    if not is_small():
        return lax.psum(value, "seq")
    for bit in (1, 2, 4):
        value = value + swap(value, along(bit))
    return value


def sum_all(value):
    value = sum_seq(value)
    if not is_small():
        return lax.psum(value, "dp")
    for bit in (1, 2):
        value = value + swap(value, lambda z, i: (z ^ bit, i))
    return value


def stack_dp(value):
    if not is_small():
        return lax.all_gather(value, "dp", axis=0, tiled=True)
    for bit in (1, 2):
        value = jnp.concatenate([value, swap(value, lambda z, i: (z ^ bit, i))], axis=0)
    return value


def dot(left, right, contract=((1,), (0,))):
    return lax.dot_general(left, right, (contract, ((), ())), preferred_element_type=F32)


def call(body, name, micros, **kwargs):
    return pl.pallas_call(
        body,
        name=name,
        cost_estimate=pl.CostEstimate(
            flops=int(micros * 1.1e9), transcendentals=0, bytes_accessed=int(micros * 1e6)
        ),
        compiler_params=pltpu.CompilerParams(vmem_limit_bytes=LIMIT),
        **kwargs,
    )


VMEM = pl.BlockSpec(memory_space=pltpu.VMEM)
ANY = pl.BlockSpec(memory_space=pl.ANY)
SMEM = pl.BlockSpec(memory_space=pltpu.SMEM)


def start(copies):
    for copy in copies:
        copy.start()
    return copies


def wait(copies):
    for copy in copies:
        copy.wait()


def like(arrays):
    return [pltpu.VMEM(a.shape, a.dtype) for a in arrays]


def block_copies(places, line, refs, target, sems, part=None):
    copies = []
    for slot, ref in enumerate(refs):
        source = ref if part is None else ref.at[part]
        rows = source.shape[-2]
        first = pl.multiple_of(places[line, slot] * rows, rows)
        if len(source.shape) == 3:
            place = target.at[:, pl.ds(first, rows), :]
        else:
            place = target.at[pl.ds(first, rows), :]
        copies.append(pltpu.make_async_copy(source, place, sems.at[slot]))
    return start(copies)


def weight_refs(weights):
    return [ref.at[s] for ref in weights for s in range(ref.shape[0])]


def qkv_kernel(blocks, sides, places, *refs):
    tokens, refs = refs[:blocks], refs[blocks:]
    weights, (bias, query, keyval, held, sems) = refs[:sides], refs[sides:]
    wait(block_copies(places, 0, weight_refs(weights), held, sems))
    for s in range(query.shape[0]):
        rows = tokens[s][...]
        keyval[0, s] = dot(rows, held[1]).astype(BF16)
        keyval[1, s] = (dot(rows, held[2]) + bias[1:2]).astype(BF16)
        query[s] = (dot(rows, held[0]) + bias[0:1]).astype(BF16)


def qkv_project(places, tokens, weights, bias):
    slots = len(tokens)
    lanes = weights[0].shape[-1]
    out = jax.ShapeDtypeStruct((slots, ROWS, lanes), BF16)
    pair = jax.ShapeDtypeStruct((2, slots, ROWS, lanes), BF16)
    return call(
        functools.partial(qkv_kernel, len(tokens), len(weights)),
        "qkv",
        5,
        out_shape=(out, pair),
        in_specs=[SMEM] + [VMEM] * len(tokens) + [ANY] * len(weights) + [VMEM],
        out_specs=(VMEM,) * 2,
        scratch_shapes=[
            pltpu.VMEM((3, D, lanes), BF16),
            pltpu.SemaphoreType.DMA((len(weights) * weights[0].shape[0],)),
        ],
    )(places, *tokens, *weights, bias)


def turn_kernel(*refs):
    for s, ref in enumerate(refs[:-1]):
        turn_wide(ref, refs[-1].at[:, s * ROWS : (s + 1) * ROWS])


def turn_tokens(tokens):
    return call(
        turn_kernel,
        "turn_tokens",
        2,
        out_shape=jax.ShapeDtypeStruct((D, len(tokens) * ROWS), BF16),
        in_specs=[VMEM] * len(tokens),
        out_specs=VMEM,
    )(*tokens)


def left_half(shape):
    return lax.broadcasted_iota(jnp.int32, shape, len(shape) - 1) < HEAD_DIM


def split3(value):
    high = value.astype(BF16).astype(F32)
    middle = (value - high).astype(BF16).astype(F32)
    low = (value - high - middle).astype(BF16).astype(F32)
    return high, middle, low


def spread3(value, docs, shape):
    lane = lax.broadcasted_iota(jnp.int32, shape, 1) % HEAD_DIM
    high, middle, low = split3(value)
    return jnp.where(
        lane == docs, high, jnp.where(lane == docs + 1, middle, jnp.where(lane == docs + 2, low, 0.0))
    )


STEP = 512


def eye(size):
    shape = (size, size)
    same = lax.broadcasted_iota(jnp.int32, shape, 0) == lax.broadcasted_iota(jnp.int32, shape, 1)
    return jnp.where(same, 1.0, 0.0).astype(BF16)


def turn(value):
    return dot(eye(value.shape[1]), value, ((1,), (1,))).astype(BF16)


def turn_wide(value, target, first=0):
    for at in range(0, value.shape[1], PAIR * 2):
        block = value[:, at : at + PAIR * 2]
        target[first + at : first + at + block.shape[1]] = turn(block)


def fill_keys(keyvals, feature_k, keys, values, mine):
    at = 0
    for ref in keyvals:
        for index in range(ref.shape[1]):
            rows = slice(at, at + ROWS)
            keys[rows] = jnp.where(mine, ref[0, index], feature_k[at // ROWS])
            values[rows] = jnp.where(mine, ref[1, index], feature_k[at // ROWS])
            at += ROWS


def for_heads(odd, body):
    if not odd:
        body(2)
        return
    tile = pl.program_id(0)
    pl.when(tile < pl.num_programs(0) - 1)(lambda: body(2))
    pl.when(tile == pl.num_programs(0) - 1)(lambda: body(1))


def attend_kernel(sides, docs, odd, *refs):
    query, feature_q, feature_k = refs[:3]
    keyvals = refs[3 : 3 + sides]
    slots, length = feature_q.shape[0], feature_k.shape[0] * ROWS
    rest = refs[3 + sides :]
    wide, total, lows, (keys, values, scores) = rest[0], rest[1], rest[2:-3], rest[-3:]
    left = left_half((ROWS, PAIR))
    sides_of = (left, jnp.logical_not(left))

    def body(heads):
        for head in range(heads):
            fill_keys(keyvals, feature_k, keys.at[head], values.at[head], sides_of[head])
        units = [(slot, head) for slot in range(slots) for head in range(heads)]

        def queries(unit):
            slot, head = unit
            return jnp.where(sides_of[head], query[slot] * 0.125, feature_q[slot])

        def score(unit, number, rows, at, most):
            made = dot(rows, keys[unit[1], at : at + STEP], ((1,), (1,)))
            scores[number % 2, :, at : at + STEP] = made
            for lane in range(0, STEP, PAIR):
                part = made[:, lane : lane + PAIR]
                most = part if most is None else jnp.maximum(most, part)
            return most

        most, rows = None, queries(units[0])
        for at in range(0, length, STEP):
            most = score(units[0], 0, rows, at, most)
        done = {}
        for number, (slot, head) in enumerate(units):
            top = jnp.max(most, axis=1, keepdims=True)
            following = units[number + 1] if number + 1 < len(units) else None
            most, acc = None, 0.0
            if following:
                rows = queries(following)
            for at in range(0, length, STEP):
                if following:
                    most = score(following, number + 1, rows, at, most)
                weights = jnp.exp(scores[number % 2, :, at : at + STEP] - top).astype(BF16)
                acc = acc + dot(weights, values[head, at : at + STEP])
            lane = docs + (HEAD_DIM if head == 0 else 0)
            weight = acc[:, lane : lane + 1]
            done[head] = (acc / weight, top + jnp.log(weight))
            if head == heads - 1:
                result, sums = done[0]
                sums = jnp.broadcast_to(sums, (ROWS, PAIR))
                if heads > 1:
                    result = jnp.where(left, result, done[1][0])
                    sums = jnp.where(left, sums, done[1][1])
                wide[slot] = result
                total[slot] = sums
                lows[slot][...] = result.astype(BF16)

    for_heads(odd, body)


def tile_spec(array, base=0):
    lead = array.shape[:-1]
    return pl.BlockSpec(lead + (PAIR,), lambda tile: (0,) * len(lead) + (tile + base,))


def fixed_spec(array):
    return pl.BlockSpec(array.shape, lambda tile: (0,) * array.ndim)


def attend(query, keyvals, feature_q, feature_k, docs):
    slots, tiles = query.shape[0], query.shape[-1] // PAIR
    wide = jax.ShapeDtypeStruct(query.shape, F32)
    low = jax.ShapeDtypeStruct(wide.shape[1:], BF16)
    length = feature_k.shape[0] * ROWS
    made = call(
        functools.partial(attend_kernel, len(keyvals), docs, slots > 1),
        "attend",
        12,
        grid=(tiles,),
        out_shape=(wide, wide) + (low,) * slots,
        in_specs=[tile_spec(query), fixed_spec(feature_q), fixed_spec(feature_k)]
        + [tile_spec(a) for a in keyvals],
        out_specs=(tile_spec(wide),) * 2 + (tile_spec(low),) * slots,
        scratch_shapes=[
            pltpu.VMEM((2, length, PAIR), BF16),
            pltpu.VMEM((2, length, PAIR), BF16),
            pltpu.VMEM((2, ROWS, length), F32),
        ],
    )(query, feature_q, feature_k, *keyvals)
    return made[0], made[1], list(made[2:])


def head_lanes(ref, first, heads):
    if first is None:
        return ref[...]
    found = ref[:, first : first + heads * HEAD_DIM]
    if heads > 1:
        return found
    return jnp.concatenate([found, jnp.zeros_like(found)], axis=1)


def attend_back_kernel(sides, docs, heads, first, *refs):
    query, wide, total, feature_q, feature_k = refs[:5]
    slots, length = feature_q.shape[0], feature_k.shape[0] * ROWS
    grads_in, keyvals = refs[5 : 5 + slots], refs[5 + slots : 5 + slots + sides]
    rest = refs[5 + slots + sides :]
    grad_q, outs = rest[0], rest[1 : 1 + sides]
    keys, values, queries_t, grads_t, query_own, grad_own, softs, slopes, acc = rest[1 + sides :]
    left = left_half((ROWS, PAIR))
    sides_of = (left, jnp.logical_not(left))
    zero = jnp.zeros((ROWS, PAIR), BF16)
    for head in range(heads):
        fill_keys(keyvals, feature_k, keys.at[head], values.at[head], sides_of[head])
    units = [(slot, head) for head in range(heads) for slot in range(slots)]
    for unit, (slot, head) in enumerate(units):
        mine, at = sides_of[head], head * HEAD_DIM
        rows, grads = query[slot] * 0.125, head_lanes(grads_in[slot], first, heads)
        product = jnp.where(mine, grads.astype(F32) * wide[slot], 0.0)
        delta = jnp.sum(product, axis=1, keepdims=True)
        sums = total[slot, :, at : at + 1]
        spare = feature_q[slot].astype(F32) + spread3(-sums, docs, (ROWS, PAIR))
        queries_t[unit] = turn(jnp.where(mine, rows, spare.astype(BF16)))
        spare = spread3(-delta, docs, (ROWS, PAIR)).astype(BF16)
        grads_t[unit] = turn(jnp.where(mine, grads, spare))
        line = slice(unit * ROWS, (unit + 1) * ROWS)
        query_own[line] = jnp.where(mine, rows, zero)
        grad_own[line] = jnp.where(mine, grads, zero)
    per = slots * ROWS
    pieces = [(ref, index) for ref in keyvals for index in range(ref.shape[1])]
    places = [(ref, index) for ref in outs for index in range(ref.shape[1])]
    for step, at in enumerate(range(0, length, STEP)):
        which = step % 2
        for unit, (slot, head) in enumerate(units):
            line = slice(unit * ROWS, (unit + 1) * ROWS)
            soft = jnp.exp(dot(keys[head, at : at + STEP], queries_t[unit]))
            change = dot(values[head, at : at + STEP], grads_t[unit])
            softs[which, :, line] = soft.astype(BF16)
            slopes[which, :, line] = (soft * change).astype(BF16)
        out_v = dot(softs[which], grad_own[...])
        out_k = dot(slopes[which], query_own[...])
        first = at // ROWS
        for k in range(STEP // ROWS):
            ref, index = places[first + k]
            ref[0, index] = out_k[k * ROWS : (k + 1) * ROWS].astype(BF16)
            ref[1, index] = out_v[k * ROWS : (k + 1) * ROWS].astype(BF16)
        key = jnp.concatenate(
            [pieces[first + k][0][0, pieces[first + k][1]] for k in range(STEP // ROWS)], axis=0
        )
        key_t = turn(key)
        for head in range(heads):
            part = slice(head * HEAD_DIM, (head + 1) * HEAD_DIM)
            made = dot(key_t[part], slopes[which, :, head * per : (head + 1) * per])
            if step == 0:
                acc[part] = made
            else:
                acc[part] += made
    if heads == 1:
        acc[HEAD_DIM:] = jnp.zeros((PAIR - HEAD_DIM, per), F32)
    for slot in range(slots):
        made = (acc[:, slot * ROWS : (slot + 1) * ROWS] * 0.125).astype(BF16)
        grad_q[slot] = turn(made)


def attend_back(query, keyvals, grads, wide, total, feature_q, feature_k, docs, base, tiles, single):
    slots, heads = query.shape[0], 1 if single else 2
    length = feature_k.shape[0] * ROWS
    outs = tuple(
        jax.ShapeDtypeStruct(a.shape[:-1] + (tiles * PAIR,), BF16) for a in (query, *keyvals)
    )
    units = slots * heads
    whole = tiles > 1
    made = call(
        functools.partial(
            attend_back_kernel, len(keyvals), docs, heads, None if whole else base * PAIR
        ),
        "attend_back",
        8 if single else 15,
        grid=(tiles,),
        out_shape=outs,
        in_specs=[tile_spec(a, base) for a in (query, wide, total)]
        + [fixed_spec(feature_q), fixed_spec(feature_k)]
        + [tile_spec(a, base) if whole else fixed_spec(a) for a in grads]
        + [tile_spec(a, base) for a in keyvals],
        out_specs=tuple(tile_spec(a) for a in outs),
        scratch_shapes=[
            pltpu.VMEM((heads, length, PAIR), BF16),
            pltpu.VMEM((heads, length, PAIR), BF16),
            pltpu.VMEM((units, PAIR, ROWS), BF16),
            pltpu.VMEM((units, PAIR, ROWS), BF16),
            pltpu.VMEM((units * ROWS, PAIR), BF16),
            pltpu.VMEM((units * ROWS, PAIR), BF16),
            pltpu.VMEM((2, STEP, units * ROWS), BF16),
            pltpu.VMEM((2, STEP, units * ROWS), BF16),
            pltpu.VMEM((PAIR, slots * ROWS), F32),
        ],
    )(query, wide, total, feature_q, feature_k, *grads, *keyvals)
    return made[0], list(made[1:])


def normalise(value):
    centred = value - jnp.mean(value, axis=-1, keepdims=True)
    inverse = lax.rsqrt(jnp.mean(centred * centred, axis=-1, keepdims=True) + EPSILON)
    return centred * inverse, inverse


def norm_back(grad, gain, unit, inverse):
    scaled = grad * gain
    return inverse * (
        scaled
        - jnp.mean(scaled, axis=-1, keepdims=True)
        - unit * jnp.mean(scaled * unit, axis=-1, keepdims=True)
    )


def erf(value):
    value = jnp.clip(value, -3.7439211627767994, 3.7439211627767994)
    square = value * value
    top = 0.00022905065861350646
    for factor in (0.0034082910107109506, 0.050955695062380861, 0.18520832239976145, 1.128379143519084):
        top = top * square + factor
    bottom = -1.1791602954361697e-7
    for factor in (
        0.000023547966471313185, 0.0010179625278914885, 0.014070470171167667,
        0.11098505178285362, 0.49746925110067538, 1.0,
    ):
        bottom = bottom * square + factor
    return value * top / bottom


def column_sum(value):
    return jnp.sum(value, axis=0, keepdims=True)


def early_copies(places, blocks, weights, sems):
    if len(blocks) == 1:
        return [block_copies(places, 1, blocks, weights, sems)] + [[]] * 4
    rows = D // len(blocks)
    copies = []
    for piece in range(5):
        copies.append([])
        for slot, ref in enumerate(blocks):
            first = pl.multiple_of(places[1, slot] * rows, rows)
            copies[piece].append(
                pltpu.make_async_copy(
                    ref.at[piece * rows : (piece + 1) * rows],
                    weights.at[piece, pl.ds(first, rows), :],
                    sems.at[5 * slot + piece],
                )
            )
    return copies


def start_all(groups):
    for copies in groups:
        start(copies)


def late_rows(places, blocks, down, sems):
    rows = FF // len(blocks)
    found = []
    for slot, ref in enumerate(blocks):
        part = slice(slot * rows, (slot + 1) * rows)
        copy = pltpu.make_async_copy(ref.at[:rows], down.at[part], sems.at[slot])
        copy.start()
        found.append((pl.multiple_of(places[2, slot] * rows, rows), part, copy))
    return found


def fill_table(places, smalls, table):
    count, share = smalls.shape[0], D // smalls.shape[0]
    line = lax.broadcasted_iota(jnp.int32, (PAIR, D), 0)
    lane = lax.broadcasted_iota(jnp.int32, (PAIR, D), 1)
    made = 0.0
    for slot in range(count):
        spread = jnp.where(jnp.logical_and(lane == line + places[1, slot] * share, line < share), 1.0, 0.0)
        made = made + dot(smalls[slot, :, :PAIR], spread.astype(BF16))
    table[0:UP_B] = made[0:UP_B]
    for slot in range(count):
        at = places[1, slot]
        table[pl.ds(UP_B + at // 2, 1), pl.ds(pl.multiple_of(at % 2 * 4 * share, 4 * share), 4 * share)] = (
            smalls[slot, UP_B : UP_B + 1, : 4 * share].astype(F32)
        )


def first_kernel(count, slots, groups, places, *refs):
    blocks, refs = refs[:count], refs[count:]
    attended, refs = refs[: slots * groups], refs[slots * groups :]
    tokens, given, refs = refs[0], refs[1] if count == 1 else None, refs[1 if count > 1 else 2 :]
    many = 2 if slots > 1 else 1
    table, unit, inverse, active, slope_out, sides_out = *refs[:5], refs[5 : 5 + many]
    slope, sides = refs[5 + many], refs[6 + many : 6 + 2 * many]
    weights, turned, smalls, sems, small_sems, out_sems = refs[-6:]
    sent = []

    def leave_part(source, target):
        copy = pltpu.make_async_copy(source, target, out_sems.at[len(sent)])
        copy.start()
        sent.append(copy)

    copies = early_copies(places, blocks, weights, sems)
    if count > 1:
        start_all(copies)
        more = start(
            [
                pltpu.make_async_copy(ref.at[5 * D // count :], smalls.at[slot], small_sems.at[slot])
                for slot, ref in enumerate(blocks)
            ]
        )
    width = D // slots

    def row(at):
        return table[at : at + 1]

    core = places[0, 0] % 2 if slots > 1 else 0
    per = width // 2 if slots > 1 else width
    rows_of = [
        jnp.concatenate([a[...] for a in attended[s * groups : (s + 1) * groups]], axis=1)
        for s in range(slots)
    ]
    far = 4 * FF // 8

    for s in range(slots):
        turn_wide(rows_of[s].astype(BF16), turned)
        if slots > 1:
            first = far + (slots + s) * per
            sides[0][first : first + per] = turned[pl.ds(pl.multiple_of(core * per, per), per)]
            sides[1][first : first + per] = turned[pl.ds(pl.multiple_of((1 - core) * per, per), per)]
        else:
            sides[0][FF + D :] = turned[...]
    if count > 1:
        wait(more)
        fill_table(places, smalls, table)
    else:
        table[...] = given[...]
    wait(copies[0])
    residual = tokens[...].astype(F32) + row(PROJ_B)
    for s in range(slots):
        first = pl.multiple_of((places[0, s] // 2) * width, width)
        residual = residual + dot(rows_of[s][:, :width], weights[0, pl.ds(first, width), :])
    first_unit, first_inverse = normalise(residual)
    unit[...] = first_unit
    inverse[...] = first_inverse
    normed = first_unit * row(NORM_G) + row(NORM_S)
    normed_low = normed.astype(BF16)
    turn_wide(normed_low, turned)
    for side, target in enumerate(sides):
        if slots == 1:
            target[FF : FF + D] = turned[...]
            continue
        for s in range(slots):
            first = pl.multiple_of(places[0, side * slots + s] * per, per)
            target[far + s * per : far + (s + 1) * per] = turned[pl.ds(first, per)]
    for side, target in enumerate(sides):
        rows = slice(FF // len(sides), None)
        leave_part(target.at[rows], sides_out[side].at[rows])
    step = 384
    for at in range(0, FF, step):
        line, col = at // D, at % D
        if col == 0:
            wait(copies[1 + line])
        upward = (
            dot(normed_low, weights[1 + line, :, col : col + step])
            + table[UP_B + line : UP_B + line + 1, col : col + step]
        )
        share = 0.5 + 0.5 * erf(upward * 0.7071067811865476)
        bell = jnp.exp(upward * upward * -0.5) * 0.3989422804014327
        active[:, at : at + step] = (upward * share).astype(BF16)
        slope[:, at : at + step] = (share + upward * bell).astype(BF16)
        if (at + step) % D == 0:
            lanes = slice(at + step - D, at + step)
            leave_part(slope.at[:, lanes], slope_out.at[:, lanes])
    for side, target in enumerate(sides):
        if slots == 1:
            turn_wide(active, target)
            leave_part(target.at[:FF], sides_out[side].at[:FF])
            continue
        rows = FF // 8
        for s in range(slots):
            first = pl.multiple_of(places[0, side * slots + s] * rows, rows)
            for at in range(0, rows, PAIR):
                block = active[:, pl.ds(pl.multiple_of(first + at, PAIR), PAIR)]
                target[s * rows + at : s * rows + at + PAIR] = turn(block)
            part = slice(s * rows, (s + 1) * rows)
            leave_part(target.at[part], sides_out[side].at[part])
    wait(sent)


def first_part(places, blocks, attended, tokens, table):
    count = len(blocks)
    slots = 4 if count > 1 else 1
    groups = len(attended) // slots
    given = [table] if count == 1 else []
    shape = jax.ShapeDtypeStruct
    sides = 2 if slots > 1 else 1
    outs = (
        shape((TABLE, D), F32), shape((ROWS, D), F32), shape((ROWS, 1), F32),
        shape((ROWS, FF), BF16), shape((ROWS, FF), BF16),
    )
    outs += (shape(((FF + 2 * D) // sides, ROWS), BF16),) * sides
    made = call(
        functools.partial(first_kernel, count, slots, groups),
        "forward_up",
        11,
        out_shape=outs,
        in_specs=[SMEM] + [ANY] * count + [VMEM] * (slots * groups + 1 + len(given)),
        out_specs=(VMEM,) * 4 + (ANY,) * (1 + sides),
        scratch_shapes=like(outs[4:])
        + [
            pltpu.VMEM((5, D, D), BF16),
            pltpu.VMEM((D, ROWS), BF16),
            pltpu.VMEM((count, TABLE, D), BF16),
            pltpu.SemaphoreType.DMA((5 * count,)),
            pltpu.SemaphoreType.DMA((count,)),
            pltpu.SemaphoreType.DMA((16,)),
        ],
    )(places, *blocks, *attended, tokens, *given)
    return made[:5], made[5:]


def head_kernel(count, docs, places, *refs):
    blocks, refs = refs[:count], refs[count:]
    unit, active, cotangent, table, numbers = refs[:5]
    output, lines, docs_out, grad_second, grad_out = refs[5:10]
    pool, down, sems = refs[10:]
    down_parts = late_rows(places, blocks, down, sems.at[1])
    pool_copies = block_copies(places, 2, blocks, pool, sems.at[0], slice(FF // count, (FF + D) // count))

    def row(at):
        return table[at : at + 1]

    normed = unit[...] * row(NORM_G) + row(NORM_S)
    residual = normed + row(DOWN_B)
    for first, part, copy in down_parts:
        copy.wait()
        residual = residual + dot(active[:, pl.ds(first, FF // count)], down[part])
    last_unit, last_inverse = normalise(residual)
    outcome = last_unit * row(FINAL_G) + row(FINAL_S)
    out_low = outcome.astype(BF16)
    output[...] = out_low

    at_row, label = numbers[:, 0:1], numbers[:, 1:2]
    here = jnp.logical_and(at_row >= 0.0, at_row < float(ROWS))
    line = lax.broadcasted_iota(jnp.int32, (docs, ROWS), 1).astype(F32)
    pick = jnp.where(line == at_row, 1.0, 0.0)
    first_low = dot(pick.astype(BF16), out_low).astype(BF16)
    wait(pool_copies)
    pooled = jnp.tanh(dot(first_low, pool[...]) + row(POOL_B))
    pooled_low = pooled.astype(BF16).astype(F32)
    logits = [
        jnp.sum(pooled_low * row(CLASS_W + c), axis=1, keepdims=True)
        + numbers[:, 2 + c : 3 + c]
        for c in range(CLASSES)
    ]
    top = functools.reduce(jnp.maximum, logits)
    powers = [jnp.exp(logit - top) for logit in logits]
    whole = functools.reduce(jnp.add, powers)
    grads = [powers[c] / whole - jnp.where(label == float(c), 1.0, 0.0) for c in range(CLASSES)]
    grad_pre = functools.reduce(jnp.add, [grads[c] * row(CLASS_W + c) for c in range(CLASSES)])
    grad_pre = grad_pre * (1.0 - pooled * pooled)
    parts = jnp.concatenate(split3(grad_pre), axis=0).astype(BF16)
    made = dot(parts, pool[...], ((1,), (1,)))
    grad_first = made[:docs] + made[docs : 2 * docs] + made[2 * docs :]
    parts = jnp.concatenate(split3(grad_first), axis=0).astype(BF16)
    picks = jnp.concatenate([pick] * 3, axis=0).astype(BF16)
    grad_outcome = cotangent[...] + dot(picks, parts, ((0,), (0,)))
    lane = lax.broadcasted_iota(jnp.int32, (docs, 128), 1)
    small = jnp.zeros((docs, 128), F32)
    for c in range(CLASSES):
        small = jnp.where(lane == c, grads[c], jnp.where(lane == CLASSES + c, logits[c], small))
    docs_out[...] = jnp.where(
        here,
        jnp.concatenate([first_low.astype(F32), pooled_low, grad_pre, small], axis=1),
        0.0,
    )

    grad = norm_back(grad_outcome, row(FINAL_G), last_unit, last_inverse)
    grad_second[...] = grad
    grad_out[...] = grad.astype(BF16)
    lines[0:1] = column_sum(grad)
    lines[1:2] = column_sum(grad_outcome * last_unit)
    lines[2:3] = column_sum(grad_outcome)
    lines[3:8] = jnp.zeros((5, D), F32)


def head_part(places, late, unit, active, cotangent, table, numbers):
    count, docs = len(late), numbers.shape[0]
    shape = jax.ShapeDtypeStruct
    outs = (
        shape((ROWS, D), BF16),
        shape((8, D), F32),
        shape((docs, 3 * D + 128), F32),
        shape((ROWS, D), F32),
        shape((ROWS, D), BF16),
    )
    return call(
        functools.partial(head_kernel, count, docs),
        "head",
        7,
        out_shape=outs,
        in_specs=[SMEM] + [ANY] * count + [VMEM] * 5,
        out_specs=(VMEM,) * len(outs),
        scratch_shapes=[
            pltpu.VMEM((D, D), BF16),
            pltpu.VMEM((FF, D), BF16),
            pltpu.SemaphoreType.DMA((2, count)),
        ],
    )(places, *late, unit, active, cotangent, table, numbers)


def second_kernel(count, places, *refs):
    downs, (grad_down, slope, lines, grad_up, down, sems) = refs[:count], refs[count:]
    grad_low = grad_down[...]
    whole = FF // count
    step = min(whole, 384)
    for first, part, copy in late_rows(places, downs, down, sems):
        copy.wait()
        for at in range(0, whole, step):
            rows = down[part.start + at : part.start + at + step]
            grad = dot(grad_low, rows, ((1,), (1,))).astype(BF16).astype(F32)
            here = pl.multiple_of(first + at, step)
            grad = grad * slope[:, pl.ds(here, step)].astype(F32)
            line, col = here // D, pl.multiple_of(here % D, step)
            lines[pl.ds(line, 1), pl.ds(col, step)] = column_sum(grad)
            grad_up[line, :, pl.ds(col, step)] = grad.astype(BF16)
    lines[4:8] = jnp.zeros((4, D), F32)


def second_part(places, late, grad_down, slope):
    count, shape = len(late), jax.ShapeDtypeStruct
    outs = (shape((8, D), F32), shape((4, ROWS, D), BF16))
    return call(
        functools.partial(second_kernel, count),
        "backward_down",
        5,
        out_shape=outs,
        in_specs=[SMEM] + [ANY] * count + [VMEM] * 2,
        out_specs=(VMEM,) * 2,
        scratch_shapes=[pltpu.VMEM((FF, D), BF16), pltpu.SemaphoreType.DMA((count,))],
    )(places, *late, grad_down, slope)


def third_kernel(count, slots, places, *refs):
    blocks, refs = refs[:count], refs[count:]
    table, grad_second, grad_up, unit, inverse = refs[:5]
    lines, grad_first, grad_out = refs[5:8]
    grad_attended = refs[8 : 8 + slots]
    weights, sems = refs[8 + slots :]
    copies = early_copies(places, blocks, weights, sems)
    if count > 1:
        start_all(copies[1:] + copies[:1])
    else:
        wait(copies[0])
    width = D // slots

    def row(at):
        return table[at : at + 1]

    back = 0.0
    for line in range(4):
        wait(copies[1 + line])
        back = back + dot(grad_up[line], weights[1 + line], ((1,), (1,)))
    grad_normed = grad_second[...] + back.astype(BF16).astype(F32)
    lines[0:4] = jnp.zeros((4, D), F32)
    lines[4:5] = column_sum(grad_normed * unit[...])
    lines[5:6] = column_sum(grad_normed)
    grad = norm_back(grad_normed, row(NORM_G), unit[...], inverse[...])
    grad_first[...] = grad
    lines[6:7] = column_sum(grad)
    lines[7:8] = jnp.zeros((1, D), F32)
    grad_low = grad.astype(BF16)
    grad_out[...] = grad_low
    if count > 1:
        wait(copies[0])
    for s in range(slots):
        first = pl.multiple_of((places[0, s] // 2) * width, width)
        made = dot(grad_low, weights[0, pl.ds(first, width), :], ((1,), (1,))).astype(BF16)
        grad_attended[s][...] = made


def third_part(places, blocks, table, grad_second, grad_up, unit, inverse, slots, lanes):
    count = len(blocks)
    shape = jax.ShapeDtypeStruct
    outs = (shape((8, D), F32), shape((ROWS, D), F32), shape((ROWS, D), BF16))
    outs += (shape((ROWS, lanes), BF16),) * slots
    made = call(
        functools.partial(third_kernel, count, slots),
        "backward_up",
        7,
        out_shape=outs,
        in_specs=[SMEM] + [ANY] * count + [VMEM] * 5,
        out_specs=(VMEM,) * len(outs),
        scratch_shapes=[pltpu.VMEM((5, D, D), BF16), pltpu.SemaphoreType.DMA((5 * count,))],
    )(places, *blocks, table, grad_second, grad_up, unit, inverse)
    return made[:3], list(made[3:])


def wgrad_outs(slots, rows):
    shape = jax.ShapeDtypeStruct
    if slots == 1:
        return (shape((1, rows, D), BF16),)
    half = rows // 2
    return (shape((2, half, D), BF16),) * 2 + (shape((half, D), BF16),) * 2 + (shape((rows, D), F32),)


def put_slot(outs, s, first, value):
    if len(outs) == 1:
        outs[0][0, first : first + value.shape[0]] = value.astype(BF16)
        return
    if s == 0:
        outs[4][first : first + value.shape[0]] = value
        return
    half = outs[2].shape[0]
    for k, order in enumerate(((1, 3, 2), (2, 3, 1))):
        low, high = max(first, k * half), min(first + value.shape[0], (k + 1) * half)
        if low >= high:
            continue
        rows, part = slice(low - k * half, high - k * half), value[low - first : high - first]
        if s == order[2]:
            outs[2 + k][rows] = part.astype(BF16)
        else:
            outs[k][order.index(s), rows] = part.astype(BF16)


def gradient_call(body, name, micros, ins, outs, scratch, waits):
    return call(
        body,
        name,
        micros,
        out_shape=outs,
        in_specs=[ANY] * len(ins),
        out_specs=(ANY,) * len(outs),
        scratch_shapes=[pltpu.VMEM(a.shape, a.dtype) for a in outs]
        + scratch
        + [pltpu.SemaphoreType.DMA((waits,)), pltpu.SemaphoreType.DMA((len(outs),))],
    )(*ins)


def leave(kept, outs, sems, which):
    return start([pltpu.make_async_copy(kept[k], outs[k], sems.at[k]) for k in which])


def down_kernel(slots, sides, *refs):
    lefts, rights, refs = refs[:sides], refs[sides : 2 * sides], refs[2 * sides :]
    count = 5 if slots > 1 else 1
    outs, kept, (left, right, sems, out_sems) = refs[:count], refs[count : 2 * count], refs[-4:]
    rows = FF // sides // slots
    step = min(rows, 384)
    copies = {}
    for side in range(sides):
        copies[side] = pltpu.make_async_copy(rights[side], right.at[side], sems.at[side])
    order = (3, 1, 2, 0) if slots > 1 else (0,)
    for s in order:
        for side in range(sides):
            part = slice(s * rows, (s + 1) * rows)
            copies[s, side] = pltpu.make_async_copy(
                lefts[side].at[part], left.at[side, part], sems.at[sides + s * sides + side]
            )
    start(copies.values())
    wait([copies[side] for side in range(sides)])
    sent = []
    for s in order:
        wait([copies[s, side] for side in range(sides)])
        for at in range(0, rows, step):
            first = s * rows + at
            made = dot(left[0, first : first + step], right[0])
            for side in range(1, sides):
                made = made + dot(left[side, first : first + step], right[side])
            put_slot(kept, s, at, made)
        if slots > 1:
            sent += leave(kept, outs, out_sems, {3: (), 1: (0, 3), 2: (1, 2), 0: (4,)}[s])
        else:
            sent += leave(kept, outs, out_sems, (0,))
    wait(sent)


def down_gradient(lefts, rights, slots):
    sides = len(lefts)
    outs = wgrad_outs(slots, FF // sides // slots)
    scratch = [pltpu.VMEM((sides, FF // sides, ROWS), BF16), pltpu.VMEM((sides, ROWS, D), BF16)]
    body = functools.partial(down_kernel, slots, sides)
    return gradient_call(
        body, "down_gradient", 3, (*lefts, *rights), outs, scratch, sides * (slots + 1)
    )


def up_kernel(slots, sides, *refs):
    lefts, ups, projs, refs = *(refs[k * sides : (k + 1) * sides] for k in range(3)), refs[3 * sides :]
    count = 5 if slots > 1 else 1
    outs, kept, (left, right, sems, out_sems) = refs[:count], refs[count : 2 * count], refs[-4:]
    whole = D // sides
    rows = whole // slots
    copies = {}
    for side in range(sides):
        copies[side] = pltpu.make_async_copy(
            lefts[side].at[FF // sides :], left.at[side], sems.at[side]
        )
    for line in range(5):
        for side in range(sides):
            copies[line, side] = pltpu.make_async_copy(
                ups[side].at[line] if line < 4 else projs[side],
                right.at[side, line],
                sems.at[sides + line * sides + side],
            )
    start(copies.values())
    wait([copies[side] for side in range(sides)])
    sent = []
    for line in range(5):
        wait([copies[line, side] for side in range(sides)])
        at = 0 if line < 4 else whole
        made = dot(left[0, at : at + whole], right[0, line])
        for side in range(1, sides):
            made = made + dot(left[side, at : at + whole], right[side, line])
        for s in range(slots):
            put_slot(kept, s, line * rows, made[s * rows : (s + 1) * rows])
        if slots > 1:
            sent += leave(kept, outs, out_sems, {2: (0, 2), 4: (1, 3, 4)}.get(line, ()))
        elif line == 4:
            sent += leave(kept, outs, out_sems, (0,))
    wait(sent)


def up_gradient(lefts, ups, projs, slots):
    sides = len(lefts)
    outs = wgrad_outs(slots, 5 * D // sides // slots)
    scratch = [pltpu.VMEM((sides, 2 * D // sides, ROWS), BF16), pltpu.VMEM((sides, 5, ROWS, D), BF16)]
    body = functools.partial(up_kernel, slots, sides)
    return gradient_call(body, "up_gradient", 4, (*lefts, *ups, *projs), outs, scratch, 6 * sides)


def input_kernel(groups, sides, places, *refs):
    turned, refs = refs[:sides], refs[sides:]
    grad_qs, refs = refs[:groups], refs[groups:]
    changes, refs = refs[: groups * sides], refs[groups * sides :]
    outs, (made, lines, grads, sems) = refs[:-4], refs[-4:]
    rows = turned[0].shape[1]
    count = outs[0].shape[0] // 3 // (D // (8 if sides > 1 else 1))
    share = D // (8 if sides > 1 else 1)
    sums, sends = [], []
    for k in range(3):
        total, line = None, None
        for side in range(sides if k else 1):
            lane = 0
            for group in range(groups):
                source = changes[group * sides + side].at[k - 1] if k else grad_qs[group]
                lanes = slice(lane, lane + source.shape[2])
                lane = lanes.stop
                grads[:, lanes] = source[...].reshape(rows, source.shape[2])
            part = dot(turned[side][...], grads[...])
            total = part if total is None else total + part
            if k != 1:
                part = dot(jnp.ones((8, rows), BF16), grads[...])
                line = part if line is None else line + part
        made[k] = total.astype(BF16)
        if k != 1:
            sums.append(line[:1])
        for side, out in enumerate(outs):
            for s in range(count):
                first = pl.multiple_of(places[0, side * count + s] * share, share)
                target = out.at[(3 * s + k) * share : (3 * s + k + 1) * share]
                sends.append((made.at[k, pl.ds(first, share), :], target))
                pltpu.make_async_copy(*sends[-1], sems.at[len(sends) - 1]).start()
    lines[...] = jnp.concatenate([*sums, jnp.zeros((14, lines.shape[1]), F32)], axis=0).astype(BF16)
    for out in outs:
        sends.append((lines, out.at[3 * count * share :]))
        pltpu.make_async_copy(*sends[-1], sems.at[len(sends) - 1]).start()
    wait([pltpu.make_async_copy(a, b, sems.at[k]) for k, (a, b) in enumerate(sends)])


def input_gradient(places, turned, grad_qs, changes, slots):
    lanes = sum(grad.shape[2] for grad in grad_qs)
    sides, groups = len(turned), len(grad_qs)
    out = jax.ShapeDtypeStruct((3 * D // sides + 16, lanes), BF16)
    made = call(
        functools.partial(input_kernel, groups, sides),
        "input_weights",
        5,
        out_shape=(out,) * sides,
        in_specs=[SMEM] + [VMEM] * (sides + groups + groups * sides),
        out_specs=(ANY,) * sides,
        scratch_shapes=[
            pltpu.VMEM((3, D, lanes), BF16),
            pltpu.VMEM((16, lanes), BF16),
            pltpu.VMEM((turned[0].shape[1], lanes), BF16),
            pltpu.SemaphoreType.DMA((sides * (3 * slots + 1),)),
        ],
    )(places, *turned, *grad_qs, *changes)
    return list(made)


def last_kernel(sides, groups, parts, places, *refs):
    weights, refs = refs[:sides], refs[sides:]
    grad_qs, refs = refs[:groups], refs[groups:]
    changes, refs = refs[: groups * parts], refs[groups * parts :]
    grad_first, own, outs = *refs[:2], refs[2:-3]
    held, grads, sems = refs[-3:]
    slots = grad_qs[0].shape[0]
    copies = block_copies(places, 0, weight_refs(weights), held, sems)
    for s in range(slots):
        rows = slice(s * ROWS, (s + 1) * ROWS)
        lane = 0
        for group in range(groups):
            lanes = slice(lane, lane + grad_qs[group].shape[2])
            lane = lanes.stop
            grads[0, rows, lanes] = grad_qs[group][s]
            for k in range(2):
                total = changes[group * parts][k, s].astype(F32)
                for change in changes[group * parts + 1 : (group + 1) * parts]:
                    total = total + change[k, s].astype(F32)
                grads[1 + k, rows, lanes] = total.astype(BF16)
    wait(copies)

    def partial(s):
        rows = slice(s * ROWS, (s + 1) * ROWS)
        total = dot(grads[0, rows], held[0], ((1,), (1,)))
        for k in range(1, 3):
            total = total + dot(grads[k, rows], held[k], ((1,), (1,)))
        return total

    for s in range(1, slots):
        outs[s - 1][...] = partial(s).astype(BF16)
    own[...] = grad_first[...] + partial(0)


def last_part(places, weights, grad_qs, changes, grad_first):
    slots, lanes = grad_qs[0].shape[0], sum(grad.shape[2] for grad in grad_qs)
    groups, parts = len(grad_qs), len(changes) // len(grad_qs)
    sides, shape = len(weights), jax.ShapeDtypeStruct
    outs = (shape((ROWS, D), F32),) + (shape((ROWS, D), BF16),) * (slots - 1)
    blocks = sides * weights[0].shape[0]
    made = call(
        functools.partial(last_kernel, sides, groups, parts),
        "input_gradients",
        5,
        out_shape=outs,
        in_specs=[SMEM] + [ANY] * sides + [VMEM] * (1 + groups + len(changes)),
        out_specs=(VMEM,) * len(outs),
        scratch_shapes=[
            pltpu.VMEM((3, D, lanes), BF16),
            pltpu.VMEM((3, slots * ROWS, lanes), BF16),
            pltpu.SemaphoreType.DMA((blocks,)),
        ],
    )(places, *weights, *grad_qs, *changes, grad_first)
    return made[0], made[1:]


def whole_scatter(part, pieces):
    seq = lax.axis_size("seq")
    rows = part.shape[1] // pieces // seq
    part = part.reshape(pieces, seq, rows, D).transpose(1, 0, 2, 3)
    part = part.reshape(seq, pieces * rows, D)
    return lax.psum_scatter(part, "seq", scatter_dimension=0, tiled=True)[0].astype(F32)


def by_chip(pieces):
    me = lax.axis_index("seq")
    for bit in (1, 2):
        odd = (me & (2 * bit)) != 0
        pieces = [jnp.where(odd, pieces[s ^ bit], pieces[s]) for s in range(len(pieces))]
    return pieces


def features(positions, starts):
    docs = starts.shape[0]
    segment = jnp.sum((positions[..., None] >= starts).astype(jnp.int32), axis=-1) - 1
    lane = jnp.arange(PAIR, dtype=jnp.int32) % HEAD_DIM
    own = segment[..., None] == lane
    return own, lane, docs


def on_device(
    inputs,
    cotangent,
    doc_lengths,
    doc_labels,
    query_weight,
    query_bias,
    key_weight,
    value_weight,
    value_bias,
    proj_weight,
    proj_bias,
    norm_gain,
    norm_shift,
    up_weight,
    up_bias,
    down_weight,
    down_bias,
    final_gain,
    final_shift,
    pool_weight,
    pool_bias,
    class_weight,
    class_bias,
):
    me = lax.axis_index("seq")
    tokens = inputs[0]
    share = query_bias.shape[0]
    lengths = doc_lengths[0]
    docs = lengths.shape[0]
    order = jnp.arange(docs, dtype=jnp.int32)
    starts = jnp.sum(jnp.where(order[None, :] < order[:, None], lengths[None, :], 0), axis=1)

    numbers = jnp.concatenate(
        [
            (starts - me * ROWS)[:, None].astype(F32),
            doc_labels[0][:, None].astype(F32),
            jnp.broadcast_to(class_bias.astype(F32), (docs, CLASSES)),
            jnp.zeros((docs, PAIR - 2 - CLASSES), F32),
        ],
        axis=1,
    )

    small_mesh = is_small()
    slot_list = slot_owners()
    chip, core = me // 2, me % 2
    width = D // 4
    slots = 4 if small_mesh else 1
    line = jnp.arange(ROWS, dtype=jnp.int32)
    mine = slot_list[:slots] if small_mesh else me[None]
    own, lane, _ = features(mine[:, None] * ROWS + line, starts)
    feature_q = jnp.where(own, FAR, 0.0).astype(BF16)
    own, lane, _ = features(slot_list[:, None] * ROWS + line, starts)
    feature_k = jnp.where(
        lane < docs, jnp.where(own, 0.0, 1.0), jnp.where(lane < docs + 3, 1.0, 0.0)
    ).astype(BF16)

    matrices = jnp.stack([query_weight, key_weight, value_weight])
    bias = jnp.stack([query_bias, value_bias])
    small = jnp.stack(
        [
            query_bias, value_bias, proj_bias, norm_gain, norm_shift, down_bias,
            final_gain, final_shift, pool_bias, *class_weight.T,
        ]
    )
    wide = me * up_bias.shape[0]
    up_pieces = up_weight.reshape(share, 4, D).transpose(1, 0, 2)
    proj_up = jnp.concatenate([proj_weight[None], up_pieces])
    down_pool = jnp.concatenate([down_weight, pool_weight])
    if small_mesh:
        pieces = [
            lax.dynamic_slice_in_dim(matrices, (chip ^ s) * width, width, 2) for s in range(4)
        ]
        token_blocks = gather_tokens(tokens)
        own = jnp.stack(exchange(pieces))
        own = jnp.pad(own, ((0, 0), (0, 0), (0, 0), (0, PAIR * 2 - width)))
        small = jnp.pad(small, ((0, TABLE - small.shape[0]), (0, D - share)))
        small = lax.dynamic_update_slice(small, up_bias[None], (UP_B, 0))
        early = Shared(jnp.concatenate([proj_up.reshape(5 * share, D), small]), 0)
        late = Shared(down_pool, 1)
        places = jnp.stack([slot_list, early.owners(), late.owners()])
        come = swap(bias, along(1))
        bias = jnp.where(
            core == 0, jnp.concatenate([bias, come], axis=1), jnp.concatenate([come, bias], axis=1)
        )
        bias = jnp.pad(bias, ((0, 0), (0, PAIR * 2 - width))).astype(F32)
        own = after(own, feature_q, feature_k, places, bias, numbers, token_blocks[1:3])
        weights = [own, swap(own, along(1))]
        early.near()
        late.near()
        table = None
    else:
        token_blocks = [tokens]
        weights = [lax.all_gather(matrices, "seq", axis=1, tiled=True)[None]]
        table = jnp.zeros((TABLE, D), BF16)
        table = lax.dynamic_update_slice(table, small, (0, me * share))
        table = lax.dynamic_update_slice(table, up_bias[None], (UP_B + wide // D, wide % D))
        table = sum_seq(table).astype(F32)
        bias = table[:2]
        blocks = [lax.all_gather(proj_up, "seq", axis=1, tiled=True)]
        whole = lax.all_gather(down_pool, "seq", axis=0)
        whole = [whole[:, : 4 * share].reshape(FF, D), whole[:, 4 * share :].reshape(D, D)]
        late_blocks = [jnp.concatenate(whole)]
        places = jnp.zeros((3, 1), jnp.int32)

    query, keyval = qkv_project(places, token_blocks, weights, bias)
    tokens_t = turn_tokens(after(token_blocks, query))
    if small_mesh:
        early.one, late.one = after((early.one, late.one), tokens_t)
        keyval = after(keyval, early.one, late.one)
        keyvals = [keyval, swap(keyval, along(1))]
        early.far()
        early.rest()
        early.cross()
        late.far()
    else:
        keyvals = [lax.all_gather(keyval, "seq", axis=1, tiled=True)]
    attended, total, lows = attend(query, keyvals, feature_q, feature_k, docs)
    if small_mesh:
        lows, tokens_t, early.both, early.other, early.crossed = after(
            (lows, tokens_t, early.both, early.other, early.crossed), lows
        )
        early.cross_both()
        blocks = early.finish()
    else:
        tokens_t = [tokens_t]
    lows = exchange(lows)
    if small_mesh:
        late.shard, late.one, late.both = after((late.shard, late.one, late.both), lows)
        late.rest_direct()
        late.cross()
        late.cross_both()

    made, turned = first_part(places, blocks, lows, tokens, table)
    table, unit, inverse, active, slope = made
    if small_mesh:
        late.other, late.crossed, late.middle, tokens_t, turned = after(
            (late.other, late.crossed, late.middle, tokens_t, turned), active
        )
        late_blocks = late.finish()
        tokens_t = [tokens_t, swap(tokens_t, along(1))]
    output, lines_one, docs_out, grad_second, grad_down = head_part(
        places, late_blocks, unit, active, cotangent[0], table, numbers
    )

    def both(keep, *away):
        return [keep] + [swap(a, along(1)) for a in away]

    def own_and_other(value):
        return both(value, *([value] if small_mesh else []))

    turned = both(*turned)
    down_parts = down_gradient(turned, own_and_other(grad_down), slots)
    if small_mesh:
        down_sum = Scatter(down_parts)
    grad_down = after(grad_down, down_parts, tokens_t)
    lines_two, grad_up = second_part(places, late_blocks, grad_down, slope)
    grad_second = after(grad_second, grad_up)
    made, grads = third_part(
        places, blocks, table, grad_second, grad_up, unit, inverse, slots, D // slots
    )
    lines_three, grad_first, grad_proj = made
    lines_two = lines_two + lines_three
    pack = jnp.concatenate([docs_out, lines_one, lines_two], axis=1)
    ups = own_and_other(grad_up)
    if small_mesh:
        grad_proj, grads = after((grad_proj, grads), down_sum.comes)
        down_sum.combine()
        down_sum.turn()
        grads = exchange(grads)
    up_parts = up_gradient(turned, ups, own_and_other(grad_proj), slots)

    back = functools.partial(
        attend_back, keyvals=keyvals,
        feature_q=feature_q, feature_k=feature_k, docs=docs,
    )
    if small_mesh:
        up_parts, pack, grads, down_sum.lasts = after(
            (up_parts, pack, grads, down_sum.lasts), up_parts
        )
        down_dp = SumDp(down_sum.total())
        up_sum = Scatter(up_parts)
        come = swap(pack, along(1))
        grad_q, changes = back(
            query, grads=grads, wide=attended, total=total, base=0, tiles=1, single=False
        )
        changes, pack, come, up_sum.seconds, down_dp.come = after(
            (changes, pack, come, up_sum.seconds, down_dp.come), grad_q, up_sum.comes
        )
        grad_qs, partial, changes = [grad_q], list(changes), both(*changes)
        up_sum.combine()
        up_sum.turn()
        down_dp.across()
        pack = pack + come
        come = swap(pack, along(2))
        rows = after(query, grad_q, up_sum.sends, down_dp.pair, pack)
        grad_q, more = back(
            rows, grads=grads, wide=attended, total=total, base=1, tiles=1, single=True
        )
        more, pack, come, up_sum.lasts, down_dp.cross = after(
            (more, pack, come, up_sum.lasts, down_dp.cross), grad_q
        )
        grad_qs, partial = grad_qs + [grad_q], partial + list(more)
        changes = changes + both(*more)
        up_dp = SumDp(up_sum.total())
        pack = pack + come
        come = swap(pack, along(4))
    else:
        grad_q, changes = back(
            query, grads=grads, wide=attended, total=total,
            base=0, tiles=HEADS // 2, single=False,
        )
        grad_qs, partial = [grad_q], changes
        change = changes[0].transpose(1, 0, 2, 3)
        change = lax.psum_scatter(change, "seq", scatter_dimension=0, tiled=True)
        changes = [change.transpose(1, 0, 2, 3)]
        partial = changes
        pack = sum_seq(pack)
    def own_shares(pack):
        at = me * share
        lines = pack[:, 3 * D + PAIR :].reshape(docs, 2, D).transpose(1, 0, 2).reshape(2 * docs, D)
        own = jnp.concatenate(
            [
                lax.dynamic_slice_in_dim(lines, at, share, 1),
                lax.dynamic_slice_in_dim(lines[8:12].reshape(-1), wide, 4 * share, 0).reshape(4, share),
                jnp.zeros((4, share), F32),
            ]
        )
        parts = [
            pack[:, 2 * D : 3 * D],
            lax.dynamic_slice_in_dim(pack, at, share, 1),
            lax.dynamic_slice_in_dim(pack, D + at, share, 1),
            pack[:, 3 * D : 3 * D + PAIR],
            own.reshape(docs, 3 * share),
        ]
        logits = pack[:, 3 * D + CLASSES : 3 * D + 2 * CLASSES]
        return jnp.concatenate(parts, axis=1), logits

    def from_docs(every_doc):
        pre_all, first_all, pooled_all = (
            every_doc[:, at : at + size] for at, size in ((0, D), (D, share), (D + share, share))
        )
        logit_all = every_doc[:, D + 2 * share : D + 2 * share + CLASSES]
        lines = jnp.sum(every_doc[:, D + 2 * share + PAIR :].reshape(-1, docs, 3 * share), axis=0)
        exact = functools.partial(jnp.dot, precision=lax.Precision.HIGHEST)
        pool_bgrad = lax.dynamic_slice_in_dim(jnp.sum(pre_all, axis=0), me * share, share, 0)
        return (
            lines.reshape(3 * docs, share),
            (exact(first_all.T, pre_all), pool_bgrad),
            (exact(pooled_all.T, logit_all), jnp.sum(logit_all, axis=0)),
        )

    qkv_parts = input_gradient(places, tokens_t, grad_qs, partial, slots)
    if small_mesh:
        qkv_parts, changes, pack, come, up_dp.come, down_dp.cross = after(
            (qkv_parts, changes, pack, come, up_dp.come, down_dp.cross), qkv_parts
        )
        keep, away = both(*qkv_parts)
        up_dp.across()
        away = after(away, up_dp.pair)
        rows = 3 * share
        pieces = [
            add(keep[s * rows : (s + 1) * rows, :width], away[s * rows : (s + 1) * rows, :width])
            for s in range(4)
        ]
        ends = add(keep[4 * rows : 4 * rows + 2], away[4 * rows : 4 * rows + 2])
        pieces = [piece.astype(BF16) for piece in pieces]
        pack, come = after((pack, come), pieces)
        pieces = exchange(pieces)
        pack, logits = own_shares(pack + come)
        come = swap(pack, lambda z, i: (z ^ 1, i))
        changes = after(changes, pieces[0], pack, ends)
    input_grad, sums = last_part(places, weights, grad_qs, changes, grad_first)

    if small_mesh:
        pieces, down_dp.cross, pack, come = after(
            (pieces, down_dp.cross, pack, come), input_grad
        )
        qkv_wgrad = jnp.concatenate(by_chip(pieces), axis=1)
        ends = jnp.pad(
            lax.dynamic_slice_in_dim(ends, core * share, share, 1), ((0, 14), (0, D - share))
        )
        qkv_dp = SumDp(jnp.concatenate([qkv_wgrad.astype(F32), ends]))
        pack = jnp.concatenate([pack, come], axis=0)
        come = swap(pack, lambda z, i: (z ^ 2, i))
        down_dp.finish()
        qkv_dp.come, up_dp.cross, sums, input_grad = after(
            (qkv_dp.come, up_dp.cross, sums, input_grad), qkv_dp.come
        )
        qkv_dp.across()
        sums, input_grad = after((sums, input_grad), qkv_dp.pair)
        sums = exchange([input_grad, *sums])
        up_dp.finish()
        of_docs = from_docs(jnp.concatenate([pack, come], axis=0))
        down_wgrad = down_dp.back()
        qkv_dp.cross, of_docs, down_wgrad = after((qkv_dp.cross, of_docs, down_wgrad), qkv_dp.cross)
        qkv_dp.finish()
        up_wgrad = up_dp.back()
        input_grad = add(*sums)
        qkv_wgrad = qkv_dp.back()
    else:
        qkv_wgrad = whole_scatter(qkv_parts[0][None, : 3 * D], 3)
        ends = sum_seq(qkv_parts[0][3 * D : 3 * D + 2].astype(F32))
        ends = lax.dynamic_slice_in_dim(ends, me * share, share, 1)
        qkv_wgrad = sum_dp(jnp.concatenate([qkv_wgrad, jnp.pad(ends, ((0, 14), (0, D - share)))]))
        down_wgrad = sum_dp(whole_scatter(down_parts[0], 1))
        up_wgrad = sum_dp(whole_scatter(up_parts[0], 5))
    proj_wgrad = up_wgrad[4 * share :]
    up_wgrad = up_wgrad[: 4 * share].reshape(4, share, D).transpose(1, 0, 2).reshape(share, FF)
    ends = qkv_wgrad[3 * share : 3 * share + 2, :share]
    qkv_wgrad = qkv_wgrad[: 3 * share].reshape(3, share, D)
    if not small_mesh:
        pack, logits = own_shares(pack)
        of_docs = from_docs(stack_dp(pack))
    lines, of_pool, of_class = of_docs
    return (
        output[None],
        logits[None],
        input_grad[None],
        qkv_wgrad[0],
        ends[0],
        qkv_wgrad[1],
        qkv_wgrad[2],
        ends[1],
        proj_wgrad,
        lines[14],
        lines[12],
        lines[13],
        up_wgrad,
        lines[16:20].reshape(-1),
        down_wgrad,
        lines[0],
        lines[1],
        lines[2],
        *of_pool,
        *of_class,
    )


def solution(mesh):
    rows, row, part = P("dp", "seq", None), P("seq", None), P("seq")
    per_sequence = P("dp", None)
    in_specs = (
        rows, rows, per_sequence, per_sequence, row, part, row, row, part, row, part, part,
        part, row, part, row, part, part, part, row, part, row, P(),
    )
    out_specs = (
        rows, P("dp", None, None), rows, row, part, row, row, part, row, part, part, part,
        row, part, row, part, part, part, row, part, row, P(),
    )
    return jax.shard_map(
        on_device, mesh=mesh, in_specs=in_specs, out_specs=out_specs, check_vma=False
    )
```
